128 devices in a mesh: gx: 8 (over x, y_hi), gy: 16 (over z, y_lo, core).
Axes of the slice: x: 4, y: 4 (y_hi: 2, y_lo: 2; y = y_hi * 2 + y_lo), z: 4, core: 2. Of those that a mesh axis runs over, the one named last changes fastest.
Arguments:
- features: bfloat16 [16, 256, 256, 128], P(None, 'gx', 'gy'), may hold values from -24 to 24
- w_first: bfloat16 [27, 16, 16], replicated, may hold values from -0.3125 to 0.3125
- w_second: bfloat16 [27, 16, 16], replicated, may hold values from -0.3125 to 0.3125
- w_lift: bfloat16 [512, 16], replicated, may hold values from -1.5 to 1.5
- w_coarse: bfloat16 [512, 27, 512], P('gy'), may hold values from -0.0546875 to 0.0546875
- w_decode: bfloat16 [16, 512], replicated, may hold values from -0.25 to 0.25
- w_joining: bfloat16 [16, 32], replicated, may hold values from -1 to 1
Outputs:
- joined: bfloat16 [16, 256, 256, 128], P(None, 'gx', 'gy')
The draws below stay inside these ranges and needn't reach their ends.
All inputs are finite; a program needn't handle non-finite values.
Results may differ from the reference program's by a relative error of at most 0.0065.
Values may be sent and summed in bfloat16 or wider, within the bound.
No kernel may reach another device: no remote copies, remote signals or barrier semaphores. Data moves between devices by JAX's collectives and lax.ppermute only.
A program may use at most 192 MiB of HBM per device.

```python
import math
import jax
import jax.numpy as jnp

C = 16
CC = 512
POOL = 16
NZ = 128
NX = 256
NY = 256


def draw_features(key, part):
    key_scale, key_offset, key_noise = jax.random.split(jax.random.fold_in(key, 11), 3)
    blocks = (C, NX // POOL, NY // POOL, NZ // POOL)
    scale = jnp.exp(jax.random.uniform(key_scale, blocks, jnp.float32, math.log(0.3), math.log(3.0)))
    offset = 0.7 * jax.random.normal(key_offset, blocks, jnp.float32)
    noise = jax.random.normal(key_noise, (C, NX, NY, NZ), jnp.float32)

    def spread(small):
        return jnp.repeat(jnp.repeat(jnp.repeat(small, POOL, 1), POOL, 2), POOL, 3)
    return jnp.clip((noise + spread(offset)) * spread(scale), -24.0, 24.0).astype(jnp.bfloat16)


def block_levels(key, dims, pieces, smallest, top_value):
    def one(axis_at, blocks):
        draws = jax.random.uniform(jax.random.fold_in(jax.random.fold_in(key, 6), axis_at), (blocks,), jnp.float32, smallest / len(pieces), top_value / len(pieces))
        return jnp.repeat(jnp.exp(draws), dims[axis_at] // blocks).reshape((-1,) + (1,) * (len(dims) - axis_at - 1))

    factor_of = one(*pieces[0])
    for cut in pieces[1:]:
        factor_of = factor_of * one(*cut)
    return factor_of


def normal_values(rng, extent, deviation, most, shards=(), kind=jnp.bfloat16):
    drawn = deviation * jax.random.normal(rng, extent, jnp.float32)
    if shards:
        drawn = drawn * block_levels(rng, extent, shards, -0.22, 0.18)
    return jnp.clip(drawn, -most, most).astype(kind)


def setup_inputs(seed: int = 0) -> dict:
    key_list = jax.random.split(jax.random.key(seed), 8)
    features = draw_features(jax.random.fold_in(key_list[7], 71), 0)
    w_first = normal_values(key_list[1], (27, C, C), (27 * C) ** -0.5, 0.3125)
    w_second = normal_values(key_list[2], (27, C, C), (27 * C) ** -0.5, 0.3125)
    w_lift = normal_values(key_list[3], (CC, C), C ** -0.5, 1.5)
    w_coarse = normal_values(key_list[4], (CC, 27, CC), (27 * CC) ** -0.5, 0.0546875, ((0, 16),))
    w_decode = normal_values(key_list[5], (C, CC), CC ** -0.5, 0.25)
    w_joining = normal_values(key_list[6], (C, 2 * C), (2 * C) ** -0.5, 1.0)
    return {"features": features, "w_first": w_first, "w_second": w_second, "w_lift": w_lift, "w_coarse": w_coarse, "w_decode": w_decode, "w_joining": w_joining}


def conv_full(field, weight):
    count = weight.shape[1]
    padded = jnp.pad(field.astype(jnp.float32), ((0, 0), (1, 1), (1, 1), (1, 1)))
    size_x, size_y, size_z = field.shape[1], field.shape[2], field.shape[3]
    total = jnp.zeros((count, size_x, size_y, size_z), jnp.float32)
    for offset in range(27):
        shift_a, shift_b, shift_c = offset // 9, (offset // 3) % 3, offset % 3
        window = padded[:, shift_a:shift_a + size_x, shift_b:shift_b + size_y, shift_c:shift_c + size_z]
        total = total + jnp.einsum("oc,cxyz->oxyz", weight[offset].astype(jnp.float32), window)
    return total


def reference(features, w_first, w_second, w_lift, w_coarse, w_decode, w_joining):
    first = jnp.maximum(conv_full(features, w_first), 0.0).astype(jnp.bfloat16)
    second = jnp.maximum(conv_full(first, w_second), 0.0).astype(jnp.bfloat16)
    blocks = second.astype(jnp.float32).reshape(C, NX // POOL, POOL, NY // POOL, POOL, NZ // POOL, POOL)
    pooled = jnp.mean(blocks, axis=(2, 4, 6))
    lifted = jnp.maximum(jnp.einsum("oc,cxyz->oxyz", w_lift.astype(jnp.float32), pooled), 0.0).astype(jnp.bfloat16)
    coarse = jnp.maximum(conv_full(lifted, jnp.transpose(w_coarse, (1, 0, 2))), 0.0).astype(jnp.bfloat16)
    decoded = jnp.einsum("oc,cxyz->oxyz", w_decode.astype(jnp.float32), coarse.astype(jnp.float32)).astype(jnp.bfloat16)
    upsampled = jnp.repeat(jnp.repeat(jnp.repeat(decoded, POOL, 1), POOL, 2), POOL, 3)
    joined = jnp.einsum("oc,cxyz->oxyz", w_joining[:, :C].astype(jnp.float32), second.astype(jnp.float32))
    joined = joined + jnp.einsum("oc,cxyz->oxyz", w_joining[:, C:].astype(jnp.float32), upsampled.astype(jnp.float32))
    return joined.astype(jnp.bfloat16)
```

```python
import jax
import jax.numpy as jnp
from jax import lax
from jax.experimental import pallas as pl
from jax.experimental.pallas import tpu as pltpu
from jax.sharding import PartitionSpec as P

POOL = 16
F32 = jnp.float32
BF16 = jnp.bfloat16


def iota(shape, dim):
    return lax.broadcasted_iota(jnp.int32, shape, dim)


def dot(a, b):
    return jnp.dot(a, b, preferred_element_type=F32)


def vmem_call(kernel, out_shape, scratch=(), flops=0, nbytes=0, smem=0):
    single = not isinstance(out_shape, (list, tuple))

    def call(*args):
        return pl.pallas_call(
            kernel,
            out_shape=out_shape,
            in_specs=[pl.BlockSpec(memory_space=pltpu.VMEM) for _ in args],
            out_specs=(
                pl.BlockSpec(memory_space=pltpu.VMEM)
                if single
                else [pl.BlockSpec(memory_space=pltpu.VMEM) for _ in out_shape]
            ),
            scratch_shapes=list(scratch),
            cost_estimate=pl.CostEstimate(flops=flops, bytes_accessed=nbytes, transcendentals=0),
        )(*args)

    return call


def pack_kernel(feat, xlo, xhi, ylo, yhi):
    size_x = feat.shape[1]
    for j in range(2):
        xlo[j] = feat[:, j].reshape(256, 128)
        xhi[j] = feat[:, size_x - 2 + j].reshape(256, 128)
    row, col = iota((64, 256), 0), iota((64, 256), 1)
    want = ((row >> 1) & 15) * 16 + (row & 1) + 14 * (row >> 5)
    select = jnp.where(col == want, 1.0, 0.0).astype(BF16)

    def step(p, carry):
        x = 2 * p
        both = jnp.concatenate(
            [feat[:, x].reshape(256, 128), feat[:, x + 1].reshape(256, 128)], axis=1
        )
        rows = dot(select, both).astype(BF16)
        for h in range(2):
            ylo[x + h] = rows[0:32, h * 128 : h * 128 + 128]
            yhi[x + h] = rows[32:64, h * 128 : h * 128 + 128]
        return carry

    lax.fori_loop(0, size_x // 2, step, 0)


def band(w_ref, wc_ref, t_ref, halo_rows, halo_cols):
    rows, cols = 256 + halo_rows, 256 + halo_cols
    crow, ccol = iota((16, cols), 0), iota((16, cols), 1)
    j = ccol - 256
    if halo_cols == 64:
        halo_in = (j >> 1) & 15
    else:
        halo_in = j & 15
    spread = jnp.where(jnp.where(ccol < 256, ccol >> 4, halo_in) == crow, 1.0, 0.0).astype(BF16)
    wc_ref[...] = dot(w_ref[...], spread).astype(BF16)
    r, o = iota((rows, 16), 0), iota((rows, 16), 1)
    expand = jnp.where(jnp.where(r < 256, r >> 4, r & 15) == o, 1.0, 0.0).astype(BF16)
    r, c = iota((rows, cols), 0), iota((rows, cols), 1)
    y_out = jnp.where(r < 256, r & 15, jnp.where(r < 272, -1, 16))
    j = c - 256
    if halo_cols == 64:
        y_halo = jnp.where(j < 32, (j & 1) - 2, (j & 1) + 16)
    else:
        y_halo = jnp.where(j < 16, -1, 16)
    y_in = jnp.where(c < 256, c & 15, y_halo)
    delta = y_in - y_out
    for off_c in range(3):
        for off_a in range(3):
            total = jnp.zeros((rows, cols), F32)
            for off_b in range(3):
                k = 9 * off_a + 3 * off_b + off_c
                value = dot(expand, wc_ref[16 * k : 16 * k + 16, :])
                total = jnp.where(delta == off_b - 1, value, total)
            total = total.astype(BF16)
            at = off_c * rows
            t_ref[at : at + rows, 256 * off_a : 256 * off_a + 256] = total[:, :256]
            left = 768 + halo_cols * off_a
            t_ref[at : at + rows, left : left + halo_cols] = total[:, 256:]


def prep_kernel(w1, w2, t1, t2, wc1, wc2):
    band(w1, wc1, t1, 32, 64)
    band(w2, wc2, t2, 0, 32)


def shifted_sum(acc, rows, half):
    lanes = slice(half * 128, half * 128 + 128)
    lane = iota((rows, 128), 1)
    before = pltpu.roll(acc[0:rows, lanes], 1, 1)
    after = pltpu.roll(acc[2 * rows : 3 * rows, lanes], 127, 1)
    total = acc[rows : 2 * rows, lanes]
    total = total + jnp.where(lane > 0, before, 0.0)
    total = total + jnp.where(lane < 127, after, 0.0)
    return jnp.maximum(total, 0.0)


def conv_kernel(
    feat, xl, xr, hl, hr, cl, cr, masks, t1, t2, second, pooled, fe, fh, f1, f1h, psum
):
    size_x = feat.shape[1]
    m_xl, m_xr = masks[0:1, :], masks[1:2, :]
    m_yl, m_yr = masks[2:3, :], masks[3:4, :]

    def scaled(v, m):
        return (v.astype(F32) * m).astype(BF16)

    def fill(x, carry):
        fe[x + 2] = feat[:, x].reshape(256, 128)
        fh[x + 2, 0:32] = scaled(hl[x], m_yl)
        fh[x + 2, 32:64] = scaled(hr[x], m_yr)
        return carry

    lax.fori_loop(0, size_x, fill, 0)
    for j in range(2):
        fe[j] = scaled(xl[j], m_xl)
        fh[j, 0:32] = scaled(cl[0, j], m_xl * m_yl)
        fh[j, 32:64] = scaled(cl[1, j], m_xl * m_yr)
        fe[size_x + 2 + j] = scaled(xr[j], m_xr)
        fh[size_x + 2 + j, 0:32] = scaled(cr[0, j], m_xr * m_yl)
        fh[size_x + 2 + j, 32:64] = scaled(cr[1, j], m_xr * m_yr)

    halo_row = iota((32, 128), 0)
    m_rim = jnp.where(halo_row < 16, m_yl, m_yr)

    def window(planes, rims, at, rim):
        return jnp.concatenate(
            [
                planes[pl.ds(at, 3)].reshape(768, 128),
                rims[pl.ds(at, 3)].reshape(3 * rim, 128),
            ],
            axis=0,
        )

    def conv_one(p, carry):
        at = 2 * p
        rhs = jnp.concatenate([window(fe, fh, at, 64), window(fe, fh, at + 1, 64)], axis=1)
        acc = dot(t1[...], rhs)
        for h in range(2):
            value = shifted_sum(acc, 288, h)
            f1[at + h] = value[:256].astype(BF16)
            f1h[at + h] = (value[256:] * m_rim).astype(BF16)
        return carry

    lax.fori_loop(0, (size_x + 2) // 2, conv_one, 0)
    f1[0] = scaled(f1[0], m_xl)
    f1h[0] = scaled(f1h[0], m_xl)
    f1[size_x + 1] = scaled(f1[size_x + 1], m_xr)
    f1h[size_x + 1] = scaled(f1h[size_x + 1], m_xr)

    z, lane = iota((128, 128), 0), iota((128, 128), 1)
    gather = jnp.where((z >> 4) == (lane & 7), 1.0, 0.0).astype(F32)
    keep = (iota((16, 128), 1) >> 3) == iota((16, 128), 0)
    results = []
    for block in range(size_x // POOL):
        psum[...] = jnp.zeros((256, 128), F32)

        def conv_two(q, carry):
            at = block * POOL + 2 * q
            rhs = jnp.concatenate([window(f1, f1h, at, 32), window(f1, f1h, at + 1, 32)], axis=1)
            acc = dot(t2[...], rhs)
            values = []
            for h in range(2):
                value = shifted_sum(acc, 256, h).astype(BF16)
                second[at + h] = value
                values.append(value.astype(F32))
            psum[...] += values[0] + values[1]
            return carry

        lax.fori_loop(0, POOL // 2, conv_two, 0)
        summed = jnp.sum(psum[...].reshape(16, 16, 128), axis=1)
        cells = jnp.dot(
            summed, gather, preferred_element_type=F32, precision=lax.Precision.HIGHEST
        )
        row = jnp.sum(jnp.where(keep, cells, 0.0), axis=0, keepdims=True) * (1.0 / POOL**3)
        results.append(row)
    both = jnp.concatenate(results, axis=0)
    for d in range(16):
        pooled[d] = both


def split3(v):
    a = v.astype(BF16)
    v = v - a.astype(F32)
    b = v.astype(BF16)
    c = (v - b.astype(F32)).astype(BF16)
    return a, b, c


def swap_groups(rows):
    lane = iota((256, 128), 1)
    major, minor = iota((256, 128), 0) >> 4, iota((256, 128), 0) & 15
    spread = jnp.broadcast_to(rows[:, None, :], (16, 16, 128)).reshape(256, 128)
    spread = jnp.where((lane >> 3) == minor, spread, 0.0)
    l0, l1 = iota((128, 128), 0), iota((128, 128), 1)
    fold = jnp.where((l0 & 7) == (l1 & 7), 1.0, 0.0).astype(BF16)
    out = []
    for piece in split3(spread):
        moved = jnp.where((lane >> 3) == major, dot(piece, fold), 0.0)
        out.append(jnp.sum(moved.reshape(16, 16, 128), axis=0))
    return out


def coarse_kernel(own, gl, gr, masks, w_lift, w_coarse, w_dec, out):
    m_xl, m_xr = masks[0:1, :], masks[1:2, :]
    slabs = [gl[...] * m_xl, own[:, 0, :], own[:, 1, :], gr[...] * m_xr]
    columns = []
    for slab in slabs:
        pieces = [v.astype(BF16) for v in swap_groups(slab)]
        columns.append(jnp.concatenate(pieces, axis=0))
    stacked = jnp.concatenate(columns, axis=1)
    lift = w_lift[...]
    lift3 = jnp.concatenate([lift, lift, lift], axis=1)
    lifted = jnp.maximum(dot(lift3, stacked), 0.0).astype(BF16)
    count = w_dec.shape[1]
    partial = dot(w_coarse[...], lifted)
    lane = iota((count, 128), 1)
    y, z = lane >> 3, lane & 7
    for x in range(2):
        total = jnp.zeros((count, 128), F32)
        for k in range(27):
            a, b, c = k // 9, k // 3 % 3 - 1, k % 3 - 1
            piece = partial[k * count : (k + 1) * count, (x + a) * 128 : (x + a) * 128 + 128]
            step = 8 * b + c
            if step:
                piece = pltpu.roll(piece, (-step) % 128, 1)
            good = None
            if b:
                good = (y < 15) if b > 0 else (y > 0)
            if c:
                inside = (z < 7) if c > 0 else (z > 0)
                good = inside if good is None else good & inside
            total = total + (piece if good is None else jnp.where(good, piece, 0.0))
        coarse = jnp.maximum(total, 0.0).astype(BF16)
        part = dot(w_dec[...], coarse)
        pieces = swap_groups(part)
        out[:, x, :] = pieces[0] + pieces[1] + pieces[2]


def join_kernel(second, parts, w_join, out):
    size_x = second.shape[0]
    r, c = iota((256, 16), 0), iota((256, 16), 1)
    rows = jnp.where((r >> 4) == c, 1.0, 0.0).astype(BF16)
    mixed = dot(rows, w_join[...]).astype(BF16)
    skip = mixed[:, 0:16]
    up = mixed[:, 16:32]
    r, c = iota((16, 256), 0), iota((16, 256), 1)
    cols = jnp.where((c >> 4) == r, 1.0, 0.0).astype(BF16)
    r, c = iota((256, 256), 0), iota((256, 256), 1)
    matrix = jnp.where((r & 15) == (c & 15), dot(skip, cols), 0.0).astype(BF16)
    keep = (iota((16, 128), 1) >> 3) == iota((16, 128), 0)
    l0, l1 = iota((128, 128), 0), iota((128, 128), 1)
    widen = jnp.where((l0 & 7) == (l1 >> 4), 1.0, 0.0).astype(BF16)
    total = parts[0]
    for d in range(1, 16):
        total = total + parts[d]
    for block in range(size_x // POOL):
        decoded = jnp.broadcast_to(total[block : block + 1, :], (16, 128))
        decoded = jnp.where(keep, decoded, 0.0).astype(BF16)
        cells = dot(decoded, widen).astype(BF16)
        term = dot(up, cells)
        term = jnp.concatenate([term, term], axis=1)

        def step(q, carry):
            x = block * POOL + 2 * q
            both = jnp.concatenate([second[x], second[x + 1]], axis=1)
            value = (dot(matrix, both) + term).astype(BF16)
            for h in range(2):
                out[:, x + h] = value[:, h * 128 : h * 128 + 128].reshape(16, 16, 128)
            return carry

        lax.fori_loop(0, POOL // 2, step, 0)


def local(features, w_first, w_second, w_lift, w_coarse, w_decode, w_joining):
    size_x = features.shape[1]
    nx, ny = lax.axis_size("gx"), lax.axis_size("gy")
    gx, gy = lax.axis_index("gx"), lax.axis_index("gy")

    def ring(count, step):
        return [(i, (i + step) % count) for i in range(count)]

    def shape(*dims, dtype=BF16):
        return jax.ShapeDtypeStruct(dims, dtype)

    row = lax.broadcasted_iota(jnp.int32, (8, 128), 0)
    masks = jnp.where(
        row == 0, gx > 0, jnp.where(row == 1, gx < nx - 1, jnp.where(row == 2, gy > 0, gy < ny - 1))
    ).astype(F32)

    xlo, xhi, ylo, yhi = vmem_call(
        pack_kernel,
        [shape(2, 256, 128), shape(2, 256, 128), shape(size_x, 32, 128), shape(size_x, 32, 128)],
        flops=2 * 64 * 256 * 128 * size_x,
        nbytes=3 << 20,
    )(features)
    hl = lax.ppermute(yhi, "gy", ring(ny, 1))
    hr = lax.ppermute(ylo, "gy", ring(ny, -1))
    xl = lax.ppermute(xhi, "gx", ring(nx, 1))
    xr = lax.ppermute(xlo, "gx", ring(nx, -1))
    cl = lax.ppermute(jnp.stack([hl[size_x - 2 :], hr[size_x - 2 :]]), "gx", ring(nx, 1))
    cr = lax.ppermute(jnp.stack([hl[:2], hr[:2]]), "gx", ring(nx, -1))

    t1, t2 = vmem_call(
        prep_kernel,
        [shape(864, 960), shape(768, 864)],
        scratch=[pltpu.VMEM((432, 320), BF16), pltpu.VMEM((432, 288), BF16)],
        flops=2 * 27 * 288 * 256 * 320,
        nbytes=4 << 20,
    )(w_first.reshape(432, 16), w_second.reshape(432, 16))
    count = w_coarse.shape[0]
    w_rows = jnp.transpose(w_coarse, (1, 0, 2)).reshape(27 * count, w_coarse.shape[2])
    w_dec = lax.dynamic_slice_in_dim(w_decode, gy * count, count, axis=1)

    second, pooled = vmem_call(
        conv_kernel,
        [shape(size_x, 256, 128), shape(16, 2, 128, dtype=F32)],
        scratch=[
            pltpu.VMEM((size_x + 4, 256, 128), BF16),
            pltpu.VMEM((size_x + 4, 64, 128), BF16),
            pltpu.VMEM((size_x + 2, 256, 128), BF16),
            pltpu.VMEM((size_x + 2, 32, 128), BF16),
            pltpu.VMEM((256, 128), F32),
        ],
        flops=2 * 2 * 864 * 960 * 128 * size_x,
        nbytes=9 << 20,
    )(features, xl, xr, hl, hr, cl, cr, masks, t1, t2)

    gathered = lax.all_to_all(pooled, "gy", 0, 0)
    gl = lax.ppermute(gathered[:, 1, :], "gx", ring(nx, 1))
    gr = lax.ppermute(gathered[:, 0, :], "gx", ring(nx, -1))
    parts = vmem_call(
        coarse_kernel,
        shape(16, 2, 128, dtype=F32),
        flops=2 * 864 * 512 * 512,
        nbytes=2 << 20,
    )(gathered, gl, gr, masks, w_lift, w_rows, w_dec)
    parts = lax.all_to_all(parts, "gy", 0, 0)
    joined = vmem_call(
        join_kernel,
        shape(16, size_x, 16, 128),
        flops=2 * 256 * 256 * 128 * size_x,
        nbytes=4 << 20,
    )(second, parts, w_joining)
    return joined


def solution(mesh):
    in_specs = (P(None, "gx", "gy", None), P(), P(), P(), P("gy", None, None), P(), P())
    out_specs = P(None, "gx", "gy", None)
    return jax.shard_map(local, mesh=mesh, in_specs=in_specs, out_specs=out_specs, check_vma=False)
```

```python
import jax
import jax.numpy as jnp
from jax import lax
from jax.experimental import pallas as pl
from jax.experimental.pallas import tpu as pltpu
from jax.sharding import PartitionSpec as P

POOL = 16
F32 = jnp.float32
BF16 = jnp.bfloat16


def iota(shape, dim):
    return lax.broadcasted_iota(jnp.int32, shape, dim)


def dot(a, b):
    return jnp.dot(a, b, preferred_element_type=F32)


def vmem_call(kernel, out_shape, scratch=(), flops=0, nbytes=0, smem=0):
    single = not isinstance(out_shape, (list, tuple))

    def call(*args):
        return pl.pallas_call(
            kernel,
            out_shape=out_shape,
            in_specs=[pl.BlockSpec(memory_space=pltpu.VMEM) for _ in args],
            out_specs=(
                pl.BlockSpec(memory_space=pltpu.VMEM)
                if single
                else [pl.BlockSpec(memory_space=pltpu.VMEM) for _ in out_shape]
            ),
            scratch_shapes=list(scratch),
            cost_estimate=pl.CostEstimate(flops=flops, bytes_accessed=nbytes, transcendentals=0),
        )(*args)

    return call


def pack_kernel(side, feat, planes, gy_a, gy_b, gx_a, gx_b, c_aa, c_ab, c_ba, c_bb):
    step = pl.program_id(0)
    count = feat.shape[1]
    row, col = iota((256, 256), 0), iota((256, 256), 1)
    match = ((row >> 4) == (col & 15)) & ((row & 15) == (col >> 4))
    swap = jnp.where(match, 1.0, 0.0).astype(BF16)
    rows_a = pl.multiple_of(side[2] * 224, 32)
    rows_b = pl.multiple_of(side[3] * 224, 32)
    for x in range(0, count, 2):
        both = jnp.concatenate(
            [feat[:, x].reshape(256, 128), feat[:, x + 1].reshape(256, 128)], axis=1
        )
        moved = dot(swap, both).astype(BF16)
        planes[x] = moved[:, :128]
        planes[x + 1] = moved[:, 128:]
    gy_a[...] = planes[:, pl.ds(rows_a, 32), :]
    gy_b[...] = planes[:, pl.ds(rows_b, 32), :]
    last = pl.num_programs(0) - 1
    for which, face, edges in ((0, gx_a, (c_aa, c_ab)), (1, gx_b, (c_ba, c_bb))):

        @pl.when(step == side[which] * last)
        def _():
            at = side[which] * (count - 2)
            face[...] = planes[pl.ds(at, 2)]
            edges[0][...] = planes[pl.ds(at, 2), pl.ds(rows_a, 32), :]
            edges[1][...] = planes[pl.ds(at, 2), pl.ds(rows_b, 32), :]


def pack(side, features):
    size_x = features.shape[1]
    step = 8

    def fixed(*dims):
        return pl.BlockSpec(dims, lambda i: (0,) * len(dims))

    def shape(*dims):
        return jax.ShapeDtypeStruct(dims, BF16)

    return pl.pallas_call(
        pack_kernel,
        grid=(size_x // step,),
        in_specs=[
            pl.BlockSpec(memory_space=pltpu.SMEM),
            pl.BlockSpec((16, step, 16, 128), lambda i: (0, i, 0, 0)),
        ],
        out_specs=[pl.BlockSpec((step, 256, 128), lambda i: (i, 0, 0))]
        + [pl.BlockSpec((step, 32, 128), lambda i: (i, 0, 0))] * 2
        + [fixed(2, 256, 128)] * 2
        + [fixed(2, 32, 128)] * 4,
        out_shape=[shape(size_x, 256, 128)]
        + [shape(size_x, 32, 128)] * 2
        + [shape(2, 256, 128)] * 2
        + [shape(2, 32, 128)] * 4,
        cost_estimate=pl.CostEstimate(
            flops=2 * 256 * 256 * 128 * size_x, bytes_accessed=5 << 20, transcendentals=0
        ),
    )(side, features)


def band(w_ref, t_ref, block):
    rows, cols = 16 * block, 16 * (block + 2)
    spread = jnp.where((iota((16, cols), 1) & 15) == iota((16, cols), 0), 1.0, 0.0).astype(BF16)
    expand = jnp.where((iota((rows, 16), 0) & 15) == iota((rows, 16), 1), 1.0, 0.0).astype(BF16)
    delta = (iota((rows, cols), 1) >> 4) - (iota((rows, cols), 0) >> 4)
    for off_c in range(3):
        for off_a in range(3):
            total = jnp.zeros((rows, cols), F32)
            for off_b in range(3):
                tall = dot(expand, w_ref[9 * off_a + 3 * off_b + off_c]).astype(BF16)
                total = jnp.where(delta == off_b, dot(tall, spread), total)
            t_ref[off_c * rows : (off_c + 1) * rows, off_a * cols : (off_a + 1) * cols] = (
                total.astype(BF16)
            )


def prep_kernel(w1, w2, t1, t2, t2_last):
    band(w1, t1, 3)
    band(w2, t2, 3)
    band(w2, t2_last, 1)


def shifted_sum(acc, rows, half):
    lanes = slice(half * 128, half * 128 + 128)
    lane = iota((rows, 128), 1)
    before = pltpu.roll(acc[0:rows, lanes], 1, 1)
    after = pltpu.roll(acc[2 * rows : 3 * rows, lanes], 127, 1)
    total = acc[rows : 2 * rows, lanes]
    total = total + jnp.where(lane > 0, before, 0.0)
    total = total + jnp.where(lane < 127, after, 0.0)
    return jnp.maximum(total, 0.0)


def window(planes, at, row, rows):
    return jnp.concatenate(
        [
            jnp.concatenate([planes[at + h + a, row : row + rows] for a in range(3)], axis=0)
            for h in range(2)
        ],
        axis=1,
    )


def conv_kernel(
    planes, gy_a, gy_b, gx_a, gx_b, c_aa, c_ab, c_ba, c_bb, masks, t1, t2, t2_last,
    second, pooled, fe, f1, f2, psum, sems,
):
    size_x = planes.shape[0]
    flags = [masks[i : i + 1, :] for i in range(8)]
    x_sides = (flags[0:2], flags[2:4])
    y_sides = (flags[4:6], flags[6:8])

    def mix(a, b, flag_a, flag_b):
        return (a.astype(F32) * flag_a + b.astype(F32) * flag_b).astype(BF16)

    def scaled(v, m):
        return (v.astype(F32) * m).astype(BF16)

    def fill(x, carry):
        fe[x + 2, 32:288] = planes[x]
        fe[x + 2, 0:32] = mix(gy_a[x], gy_b[x], *y_sides[0])
        fe[x + 2, 288:320] = mix(gy_a[x], gy_b[x], *y_sides[1])
        return carry

    lax.fori_loop(0, size_x, fill, 0, unroll=2)
    for (x_a, x_b), base in zip(x_sides, (0, size_x + 2)):
        for j in range(2):
            fe[base + j, 32:288] = mix(gx_a[j], gx_b[j], x_a, x_b)
            for (y_a, y_b), row in zip(y_sides, (0, 288)):
                total = c_aa[j].astype(F32) * (x_a * y_a) + c_ab[j].astype(F32) * (x_a * y_b)
                total = total + c_ba[j].astype(F32) * (x_b * y_a)
                total = total + c_bb[j].astype(F32) * (x_b * y_b)
                fe[base + j, row : row + 32] = total.astype(BF16)

    y_left, y_right = y_sides[0][0] + y_sides[0][1], y_sides[1][0] + y_sides[1][1]

    def conv_one(p, carry):
        at = 2 * p
        for j in range(6):
            acc = dot(t1[...], window(fe, at, 48 * j, 80))
            for h in range(2):
                value = shifted_sum(acc, 48, h)
                if j == 0:
                    value = jnp.concatenate([value[:16] * y_left, value[16:]], axis=0)
                if j == 5:
                    value = jnp.concatenate([value[:32], value[32:] * y_right], axis=0)
                f1[at + h, 48 * j : 48 * j + 48] = value.astype(BF16)
        return carry

    lax.fori_loop(0, (size_x + 2) // 2, conv_one, 0)
    f1[0] = scaled(f1[0], x_sides[0][0] + x_sides[0][1])
    f1[size_x + 1] = scaled(f1[size_x + 1], x_sides[1][0] + x_sides[1][1])

    def copy(q):
        return pltpu.make_async_copy(
            f2.at[pl.ds(2 * q, 2)], second.at[pl.ds(2 * q, 2)], sems.at[q]
        )

    psum[...] = jnp.zeros(psum.shape, F32)

    def conv_two(q, carry):
        at = 2 * q
        summed = jnp.zeros((16, 128), F32)
        for j in range(6):
            if j < 5:
                rows = 48
                acc = dot(t2[...], window(f1, at, 48 * j, 80))
            else:
                rows = 16
                acc = dot(t2_last[...], window(f1, at, 240, 48))
            for h in range(2):
                value = shifted_sum(acc, rows, h).astype(BF16)
                f2[at + h, 48 * j : 48 * j + rows] = value
                summed = summed + jnp.sum(
                    value.astype(F32).reshape(rows // 16, 16, 128), axis=0
                )
        block = q // (POOL // 2)
        psum[block] += summed
        copy(q).start()
        return carry

    lax.fori_loop(0, size_x // 2, conv_two, 0)
    z, lane = iota((128, 128), 0), iota((128, 128), 1)
    gather = jnp.where((z >> 4) == (lane & 7), 1.0, 0.0).astype(F32)
    keep = (iota((16, 128), 1) >> 3) == iota((16, 128), 0)
    results = []
    for block in range(size_x // POOL):
        cells = jnp.dot(
            psum[block], gather, preferred_element_type=F32, precision=lax.Precision.HIGHEST
        )
        row = jnp.sum(jnp.where(keep, cells, 0.0), axis=0, keepdims=True) * (1.0 / POOL**3)
        results.append(row)
    both = jnp.concatenate(results, axis=0)
    for d in range(16):
        pooled[d] = both

    def finish(q, carry):
        copy(q).wait()
        return carry

    lax.fori_loop(0, size_x // 2, finish, 0)


def convolve(args, size_x):
    vmem = pl.BlockSpec(memory_space=pltpu.VMEM)
    return pl.pallas_call(
        conv_kernel,
        in_specs=[vmem] * len(args),
        out_specs=[pl.BlockSpec(memory_space=pl.ANY), vmem],
        out_shape=[
            jax.ShapeDtypeStruct((size_x, 256, 128), BF16),
            jax.ShapeDtypeStruct((16, 2, 128), F32),
        ],
        scratch_shapes=[
            pltpu.VMEM((size_x + 4, 320, 128), BF16),
            pltpu.VMEM((size_x + 2, 288, 128), BF16),
            pltpu.VMEM((size_x, 256, 128), BF16),
            pltpu.VMEM((size_x // POOL, 16, 128), F32),
            pltpu.SemaphoreType.DMA((size_x // 2,)),
        ],
        cost_estimate=pl.CostEstimate(
            flops=2 * 2 * 864 * 256 * 128 * size_x, bytes_accessed=6 << 20, transcendentals=0
        ),
    )(*args)


def split3(v):
    a = v.astype(BF16)
    v = v - a.astype(F32)
    b = v.astype(BF16)
    c = (v - b.astype(F32)).astype(BF16)
    return a, b, c


def swap_groups(rows):
    lane = iota((256, 128), 1)
    major, minor = iota((256, 128), 0) >> 4, iota((256, 128), 0) & 15
    spread = jnp.broadcast_to(rows[:, None, :], (16, 16, 128)).reshape(256, 128)
    spread = jnp.where((lane >> 3) == minor, spread, 0.0)
    l0, l1 = iota((128, 128), 0), iota((128, 128), 1)
    fold = jnp.where((l0 & 7) == (l1 & 7), 1.0, 0.0).astype(BF16)
    out = []
    for piece in split3(spread):
        moved = jnp.where((lane >> 3) == major, dot(piece, fold), 0.0)
        out.append(jnp.sum(moved.reshape(16, 16, 128), axis=0))
    return out


def coarse_kernel(own, gl, gr, masks, w_lift, w_coarse, w_dec, out):
    m_xl, m_xr = masks[0:1, :], masks[1:2, :]
    slabs = [gl[...] * m_xl, own[:, 0, :], own[:, 1, :], gr[...] * m_xr]
    columns = []
    for slab in slabs:
        pieces = [v.astype(BF16) for v in swap_groups(slab)]
        columns.append(jnp.concatenate(pieces, axis=0))
    stacked = jnp.concatenate(columns, axis=1)
    lift = w_lift[...]
    lift3 = jnp.concatenate([lift, lift, lift], axis=1)
    lifted = jnp.maximum(dot(lift3, stacked), 0.0).astype(BF16)
    count = w_dec.shape[1]
    partial = dot(w_coarse[...], lifted)
    lane = iota((count, 128), 1)
    y, z = lane >> 3, lane & 7
    for x in range(2):
        total = jnp.zeros((count, 128), F32)
        for k in range(27):
            a, b, c = k // 9, k // 3 % 3 - 1, k % 3 - 1
            piece = partial[k * count : (k + 1) * count, (x + a) * 128 : (x + a) * 128 + 128]
            step = 8 * b + c
            if step:
                piece = pltpu.roll(piece, (-step) % 128, 1)
            good = None
            if b:
                good = (y < 15) if b > 0 else (y > 0)
            if c:
                inside = (z < 7) if c > 0 else (z > 0)
                good = inside if good is None else good & inside
            total = total + (piece if good is None else jnp.where(good, piece, 0.0))
        coarse = jnp.maximum(total, 0.0).astype(BF16)
        part = dot(w_dec[...], coarse)
        pieces = swap_groups(part)
        out[:, x, :] = pieces[0] + pieces[1] + pieces[2]


def join_kernel(second, parts, w_join, out, matrix, term):
    @pl.when(pl.program_id(0) == 0)
    def _():
        r, c = iota((256, 16), 0), iota((256, 16), 1)
        rows = jnp.where((r >> 4) == c, 1.0, 0.0).astype(BF16)
        mixed = dot(rows, w_join[...]).astype(BF16)
        r, c = iota((16, 256), 0), iota((16, 256), 1)
        cols = jnp.where((c & 15) == r, 1.0, 0.0).astype(BF16)
        r, c = iota((256, 256), 0), iota((256, 256), 1)
        matrix[...] = jnp.where((r & 15) == (c >> 4), dot(mixed[:, 0:16], cols), 0.0).astype(BF16)
        keep = (iota((16, 128), 1) >> 3) == iota((16, 128), 0)
        l0, l1 = iota((128, 128), 0), iota((128, 128), 1)
        widen = jnp.where((l0 & 7) == (l1 >> 4), 1.0, 0.0).astype(BF16)
        total = parts[0]
        for d in range(1, 16):
            total = total + parts[d]
        for block in range(2):
            decoded = jnp.broadcast_to(total[block : block + 1, :], (16, 128))
            decoded = jnp.where(keep, decoded, 0.0).astype(BF16)
            term[block] = dot(mixed[:, 16:32], dot(decoded, widen).astype(BF16))

    count = second.shape[0]
    value = term[pl.program_id(0) * count // POOL]
    value = jnp.concatenate([value, value], axis=1)
    for x in range(0, count, 2):
        both = jnp.concatenate([second[x], second[x + 1]], axis=1)
        result = (dot(matrix[...], both) + value).astype(BF16)
        for h in range(2):
            out[:, x + h] = result[:, h * 128 : h * 128 + 128].reshape(16, 16, 128)


def join(second, parts, w_join):
    size_x = second.shape[0]
    step = 8
    return pl.pallas_call(
        join_kernel,
        grid=(size_x // step,),
        in_specs=[
            pl.BlockSpec((step, 256, 128), lambda i: (i, 0, 0)),
            pl.BlockSpec((16, 2, 128), lambda i: (0, 0, 0)),
            pl.BlockSpec((16, 32), lambda i: (0, 0)),
        ],
        out_specs=pl.BlockSpec((16, step, 16, 128), lambda i: (0, i, 0, 0)),
        out_shape=jax.ShapeDtypeStruct((16, size_x, 16, 128), BF16),
        scratch_shapes=[pltpu.VMEM((256, 256), BF16), pltpu.VMEM((2, 256, 128), F32)],
        cost_estimate=pl.CostEstimate(
            flops=2 * 256 * 256 * 128 * size_x, bytes_accessed=4 << 20, transcendentals=0
        ),
    )(second, parts, w_join)


def local(features, w_first, w_second, w_lift, w_coarse, w_decode, w_joining):
    size_x = features.shape[1]
    nx, ny = lax.axis_size("gx"), lax.axis_size("gy")
    gx, gy = lax.axis_index("gx"), lax.axis_index("gy")

    def ring(count, step):
        return [(i, (i + step) % count) for i in range(count)]

    def swap(count, odd):
        return [(((i + odd) ^ 1) - odd) % count for i in range(count)]

    def shape(*dims, dtype=BF16):
        return jax.ShapeDtypeStruct(dims, dtype)

    even_x, even_y = gx % 2 == 0, gy % 2 == 0
    side = jnp.stack([even_x, ~even_x, even_y, ~even_y]).astype(jnp.int32)
    row = lax.broadcasted_iota(jnp.int32, (8, 128), 0)
    flags = [
        ~even_x, even_x & (gx > 0), even_x, ~even_x & (gx < nx - 1),
        ~even_y, even_y & (gy > 0), even_y, ~even_y & (gy < ny - 1),
    ]
    edges = [gx > 0, gx < nx - 1]
    masks = jnp.zeros((8, 128), jnp.bool_)
    for i, flag in enumerate(flags):
        masks = jnp.where(row == i, flag, masks)
    masks = masks.astype(F32)
    ends = jnp.where(row == 0, edges[0], edges[1]).astype(F32)

    planes, gy_a, gy_b, gx_a, gx_b, *corners = pack(side, features)
    across = {"x": [swap(nx, 0), swap(nx, 1)], "y": [swap(ny, 0), swap(ny, 1)]}

    def along(value, axis, to):
        return lax.ppermute(value, axis, list(enumerate(to)))

    def diagonal(value, to_x, to_y):
        pairs = [
            (i * ny + j, to_x[i] * ny + to_y[j]) for i in range(nx) for j in range(ny)
        ]
        return lax.ppermute(value, ("gx", "gy"), pairs)

    gy_a, gy_b = along(gy_a, "gy", across["y"][0]), along(gy_b, "gy", across["y"][1])
    gx_a, gx_b = along(gx_a, "gx", across["x"][0]), along(gx_b, "gx", across["x"][1])
    corners = [
        diagonal(corners[2 * i + j], across["x"][i], across["y"][j])
        for i in range(2)
        for j in range(2)
    ]

    t1, t2, t2_last = vmem_call(
        prep_kernel,
        [shape(144, 240), shape(144, 240), shape(48, 144)],
        flops=1 << 27,
        nbytes=1 << 20,
    )(w_first, w_second)
    count = w_coarse.shape[0]
    w_rows = jnp.transpose(w_coarse, (1, 0, 2)).reshape(27 * count, w_coarse.shape[2])
    w_dec = lax.dynamic_slice_in_dim(w_decode, gy * count, count, axis=1)

    second, pooled = convolve(
        (planes, gy_a, gy_b, gx_a, gx_b, *corners, masks, t1, t2, t2_last), size_x
    )

    gathered = lax.all_to_all(pooled, "gy", 0, 0)
    gl = lax.ppermute(gathered[:, 1, :], "gx", ring(nx, 1))
    gr = lax.ppermute(gathered[:, 0, :], "gx", ring(nx, -1))
    parts = vmem_call(
        coarse_kernel,
        shape(16, 2, 128, dtype=F32),
        flops=2 * 864 * 512 * 512,
        nbytes=2 << 20,
    )(gathered, gl, gr, ends, w_lift, w_rows, w_dec)
    parts = lax.all_to_all(parts, "gy", 0, 0)
    return join(second, parts, w_joining)


def solution(mesh):
    in_specs = (P(None, "gx", "gy", None), P(), P(), P(), P("gy", None, None), P(), P())
    out_specs = P(None, "gx", "gy", None)
    return jax.shard_map(local, mesh=mesh, in_specs=in_specs, out_specs=out_specs, check_vma=False)
```

```python
import jax
import jax.numpy as jnp
from jax import lax
from jax.experimental import pallas as pl
from jax.experimental.pallas import tpu as pltpu
from jax.sharding import PartitionSpec as P

POOL = 16
F32 = jnp.float32
BF16 = jnp.bfloat16
VMEM = pl.BlockSpec(memory_space=pltpu.VMEM)
LIMIT = 12 << 20


def iota(shape, dim):
    return lax.broadcasted_iota(jnp.int32, shape, dim)


def dot(a, b):
    return jnp.dot(a, b, preferred_element_type=F32)


def shape(*dims, dtype=BF16):
    return jax.ShapeDtypeStruct(dims, dtype)


def vmem_call(kernel, out_shape, args, scratch=(), flops=0, nbytes=0, aliases={}):
    single = not isinstance(out_shape, (list, tuple))
    return pl.pallas_call(
        kernel,
        out_shape=out_shape,
        in_specs=[VMEM for _ in args],
        out_specs=VMEM if single else [VMEM for _ in out_shape],
        scratch_shapes=list(scratch),
        input_output_aliases=aliases,
        compiler_params=pltpu.CompilerParams(vmem_limit_bytes=LIMIT),
        cost_estimate=pl.CostEstimate(flops=flops, bytes_accessed=nbytes, transcendentals=0),
    )(*args)


def side_flags(axis):
    at, count = lax.axis_index(axis), lax.axis_size(axis)
    even = lax.rem(at, 2) == 0

    def number(flag):
        return jnp.where(flag, 1.0, 0.0).astype(F32)

    inner_left, inner_right = at > 0, at < count - 1
    left = number(jnp.logical_not(even)), number(jnp.logical_and(even, inner_left))
    right = number(even), number(jnp.logical_and(jnp.logical_not(even), inner_right))
    return left, right


def mix(a, b, flags):
    return (a.astype(F32) * flags[0] + b.astype(F32) * flags[1]).astype(BF16)


def scaled(v, m):
    return (v.astype(F32) * m).astype(BF16)


def is_even(axis):
    return jnp.where(lax.rem(lax.axis_index(axis), 2) == 0, 1, 0)


def pack_kernel(feat, planes, gy_a, gy_b, held, sems):
    chunks, _, count = held.shape[:3]

    def copy(i):
        return pltpu.make_async_copy(
            feat.at[:, i * count : (i + 1) * count], held.at[i], sems.at[i]
        )

    for i in range(chunks):
        copy(i).start()
    row, col = iota((256, 256), 0), iota((256, 256), 1)
    match = ((row >> 4) == (col & 15)) & ((row & 15) == (col >> 4))
    swap = jnp.where(match, 1.0, 0.0).astype(BF16)
    even = is_even("gy")
    rows_a = pl.multiple_of(even * 224, 32)
    rows_b = pl.multiple_of((1 - even) * 224, 32)
    for i in range(chunks):
        copy(i).wait()
        for x in range(0, count, 2):
            both = jnp.concatenate(
                [held[i, :, x].reshape(256, 128), held[i, :, x + 1].reshape(256, 128)], axis=1
            )
            moved = dot(swap, both).astype(BF16)
            planes[i * count + x] = moved[:, :128]
            planes[i * count + x + 1] = moved[:, 128:]
    gy_a[...] = planes[:, pl.ds(rows_a, 32), :]
    gy_b[...] = planes[:, pl.ds(rows_b, 32), :]


def pack(features):
    size_x = features.shape[1]
    step = 8
    return pl.pallas_call(
        pack_kernel,
        in_specs=[pl.BlockSpec(memory_space=pltpu.HBM)],
        out_specs=[VMEM] * 3,
        out_shape=[shape(size_x, 256, 128), shape(size_x, 32, 128), shape(size_x, 32, 128)],
        scratch_shapes=[
            pltpu.VMEM((size_x // step, 16, step, 16, 128), BF16),
            pltpu.SemaphoreType.DMA((size_x // step,)),
        ],
        compiler_params=pltpu.CompilerParams(vmem_limit_bytes=LIMIT),
        cost_estimate=pl.CostEstimate(
            flops=2 * 256 * 256 * 128 * size_x, bytes_accessed=5 << 20, transcendentals=0
        ),
    )(features)


def band(wide, t_ref, block):
    cols = t_ref.shape[1]
    group = iota((16, cols), 1) >> 4
    for c in range(3):
        for y in range(block):
            total = jnp.zeros((16, cols), F32)
            for a in range(3):
                for b in range(3):
                    k = 9 * a + 3 * b + c
                    here = group == a * (block + 2) + y + b
                    total = jnp.where(here, wide[16 * k : 16 * k + 16, :cols], total)
            at = 16 * (c * block + y)
            t_ref[at : at + 16, :] = total.astype(BF16)


def spread_channels(w):
    copies = jnp.where((iota((16, 240), 1) & 15) == iota((16, 240), 0), 1.0, 0.0).astype(BF16)
    return dot(w, copies)


def shifted_sum(acc, rows, half):
    lanes = slice(half * 128, half * 128 + 128)
    lane = iota((rows, 128), 1)
    before = pltpu.roll(acc[0:rows, lanes], 1, 1)
    after = pltpu.roll(acc[2 * rows : 3 * rows, lanes], 127, 1)
    total = acc[rows : 2 * rows, lanes]
    total = total + jnp.where(lane > 0, before, 0.0)
    total = total + jnp.where(lane < 127, after, 0.0)
    return jnp.maximum(total, 0.0)


def side_by_side(parts):
    halves = [jnp.concatenate([parts(h + a) for a in range(3)], axis=0) for h in range(2)]
    return jnp.concatenate(halves, axis=1)


def conv_block(matrix, rhs):
    acc = dot(matrix, rhs)
    rows = matrix.shape[0] // 3
    return [shifted_sum(acc, rows, h) for h in range(2)]


def interior_kernel(planes, w, f1, t1, t2, t2_last):
    size_x = planes.shape[0]
    wide = spread_channels(w[0:432, :])
    band(wide, t1, 3)
    wide = spread_channels(w[432:864, :])
    band(wide, t2, 3)
    band(wide, t2_last, 1)

    def step(p, carry):
        for j in range(1, 5):
            row = 16 * (3 * j - 2)
            rhs = side_by_side(lambda x: planes[2 * p - 2 + x, row : row + 80])
            for h, value in enumerate(conv_block(t1[...], rhs)):
                f1[2 * p + h, 48 * j : 48 * j + 48] = value.astype(BF16)
        return carry

    lax.fori_loop(1, size_x // 2, step, 0)


def face_kernel(planes, gy_a, gy_b, faces, send_a, send_b):
    size_x = planes.shape[0]
    left, right = side_flags("gy")
    for side in range(2):
        for j in range(2):
            x = side * (size_x - 2) + j
            faces[side, j, 0:32] = mix(gy_a[x], gy_b[x], left)
            faces[side, j, 32:288] = planes[x]
            faces[side, j, 288:320] = mix(gy_a[x], gy_b[x], right)
    even = is_even("gx")
    send_a[...] = faces[even]
    send_b[...] = faces[1 - even]


def conv_two_pair(f1_of, t2, t2_last, store):
    summed = jnp.zeros((16, 128), F32)
    for j in range(6):
        rows = 48 if j < 5 else 16
        size = 80 if j < 5 else 48
        rhs = side_by_side(lambda x: f1_of(x, 48 * j, size))
        for h, value in enumerate(conv_block(t2[...] if j < 5 else t2_last[...], rhs)):
            value = value.astype(BF16)
            store(h, 48 * j, rows, value)
            summed = summed + jnp.sum(value.astype(F32).reshape(rows // 16, 16, 128), axis=0)
    return summed


def middle_kernel(f1_in, planes, gy_a, gy_b, t1, t2, t2_last, f1, second, psum, hl, hr):
    size_x = planes.shape[0]
    left, right = side_flags("gy")
    y_left, y_right = left[0] + left[1], right[0] + right[1]

    def fill(x, carry):
        hl[x] = mix(gy_a[x], gy_b[x], left)
        hr[x] = mix(gy_a[x], gy_b[x], right)
        return carry

    lax.fori_loop(0, size_x, fill, 0, unroll=4)

    def rim(p, carry):
        at = 2 * p - 2
        low = side_by_side(
            lambda x: jnp.concatenate([hl[at + x], planes[at + x, 0:48]], axis=0)
        )
        high = side_by_side(
            lambda x: jnp.concatenate([planes[at + x, 208:256], hr[at + x]], axis=0)
        )
        for h, value in enumerate(conv_block(t1[...], low)):
            f1[2 * p + h, 0:16] = (value[:16] * y_left).astype(BF16)
            f1[2 * p + h, 16:48] = value[16:].astype(BF16)
        for h, value in enumerate(conv_block(t1[...], high)):
            f1[2 * p + h, 240:272] = value[:32].astype(BF16)
            f1[2 * p + h, 272:288] = (value[32:] * y_right).astype(BF16)
        return carry

    lax.fori_loop(1, size_x // 2, rim, 0)
    psum[...] = jnp.zeros(psum.shape, F32)

    def step(q, carry):
        def store(h, row, rows, value):
            second[2 * q + h, row : row + rows] = value

        psum[q // (POOL // 2)] += conv_two_pair(
            lambda x, row, size: f1[2 * q + x, row : row + size], t2, t2_last, store
        )
        return carry

    lax.fori_loop(1, size_x // 2 - 1, step, 0)


def edge_kernel(
    second_in, f1, faces, got_a, got_b, psum_in, t1, t2, t2_last, second, pooled, fe, fx
):
    size_x = second.shape[0]
    x_left, x_right = side_flags("gx")
    y_left, y_right = side_flags("gy")
    y_left, y_right = y_left[0] + y_left[1], y_right[0] + y_right[1]
    for j in range(2):
        fe[0, j] = mix(got_a[j], got_b[j], x_left)
        fe[0, 2 + j] = faces[0, j]
        fe[1, j] = faces[1, j]
        fe[1, 2 + j] = mix(got_a[j], got_b[j], x_right)
    keeps = ((x_left[0] + x_left[1], 1.0), (1.0, x_right[0] + x_right[1]))

    def rim(side, keep_of):
        for j in range(6):
            rhs = side_by_side(lambda x: fe[side, x, 48 * j : 48 * j + 80])
            for h, value in enumerate(conv_block(t1[...], rhs)):
                keep = keep_of[h]
                low, mid, high = value[:16], value[16:32], value[32:]
                if j == 0:
                    low = low * y_left
                if j == 5:
                    high = high * y_right
                value = jnp.concatenate([low, mid, high], axis=0) * keep
                fx[side, h, 48 * j : 48 * j + 48] = value.astype(BF16)

    for side in range(2):
        rim(side, keeps[side])

    z, lane = iota((128, 128), 0), iota((128, 128), 1)
    gather = jnp.where((z >> 4) == (lane & 7), 1.0, 0.0).astype(F32)
    keep = (iota((16, 128), 1) >> 3) == iota((16, 128), 0)
    results = []
    for side in range(2):
        base = side * (size_x - 2)

        def f1_of(x, row, size):
            if side == 0:
                return fx[0, x, row : row + size] if x < 2 else f1[x, row : row + size]
            if x < 2:
                return f1[size_x - 2 + x, row : row + size]
            return fx[1, x - 2, row : row + size]

        def store(h, row, rows, value):
            second[base + h, row : row + rows] = value

        summed = psum_in[side] + conv_two_pair(f1_of, t2, t2_last, store)
        cells = jnp.dot(
            summed, gather, preferred_element_type=F32, precision=lax.Precision.HIGHEST
        )
        row = jnp.sum(jnp.where(keep, cells, 0.0), axis=0, keepdims=True) * (1.0 / POOL**3)
        results.append(row)
    both = jnp.concatenate(results, axis=0)
    for d in range(16):
        pooled[d] = both


def split3(v):
    a = v.astype(BF16)
    v = v - a.astype(F32)
    b = v.astype(BF16)
    c = (v - b.astype(F32)).astype(BF16)
    return a, b, c


def swap_groups(rows):
    lane = iota((256, 128), 1)
    major, minor = iota((256, 128), 0) >> 4, iota((256, 128), 0) & 15
    spread = jnp.broadcast_to(rows[:, None, :], (16, 16, 128)).reshape(256, 128)
    spread = jnp.where((lane >> 3) == minor, spread, 0.0)
    l0, l1 = iota((128, 128), 0), iota((128, 128), 1)
    fold = jnp.where((l0 & 7) == (l1 & 7), 1.0, 0.0).astype(BF16)
    out = []
    for piece in split3(spread):
        moved = jnp.where((lane >> 3) == major, dot(piece, fold), 0.0)
        out.append(jnp.sum(moved.reshape(16, 16, 128), axis=0))
    return out


def lift_slabs(slabs, w_lift):
    columns = []
    for slab in slabs:
        pieces = [v.astype(BF16) for v in swap_groups(slab)]
        columns.append(jnp.concatenate(pieces, axis=0))
    stacked = jnp.concatenate(columns, axis=1)
    lift3 = jnp.concatenate([w_lift] * 3, axis=1)
    return jnp.maximum(dot(lift3, stacked), 0.0).astype(BF16)


def taps(partial, count):
    lane = iota((count, 128), 1)
    y, z = lane >> 3, lane & 7
    total = jnp.zeros((count, 128), F32)
    for k in range(9):
        b, c = k // 3 - 1, k % 3 - 1
        piece = partial[k * count : (k + 1) * count, :]
        step = 8 * b + c
        if step:
            piece = pltpu.roll(piece, (-step) % 128, 1)
        good = None
        if b:
            good = (y < 15) if b > 0 else (y > 0)
        if c:
            inside = (z < 7) if c > 0 else (z > 0)
            good = inside if good is None else good & inside
        total = total + (piece if good is None else jnp.where(good, piece, 0.0))
    return total


def own_kernel(own, w_lift, w_coarse, out):
    count = w_coarse.shape[0] // 27
    lifted = lift_slabs([own[:, 0, :], own[:, 1, :]], w_lift[...])
    partial = dot(w_coarse[...], lifted)
    for x in range(2):
        total = jnp.zeros((count, 128), F32)
        for slab in range(2):
            a = slab - x + 1
            piece = partial[9 * a * count : 9 * (a + 1) * count, slab * 128 : slab * 128 + 128]
            total = total + taps(piece, count)
        out[x] = total


def beside_kernel(mine, gl, gr, w_lift, w_coarse, w_dec, out):
    count = w_coarse.shape[0] // 27
    at, last = lax.axis_index("gx"), lax.axis_size("gx") - 1
    m_left = jnp.where(at > 0, 1.0, 0.0).astype(F32)
    m_right = jnp.where(at < last, 1.0, 0.0).astype(F32)
    lifted = lift_slabs([gl[...] * m_left, gr[...] * m_right], w_lift[...])
    for x in range(2):
        a = 2 * x
        rows = w_coarse[9 * a * count : 9 * (a + 1) * count, :]
        total = mine[x] + taps(dot(rows, lifted[:, x * 128 : x * 128 + 128]), count)
        coarse = jnp.maximum(total, 0.0).astype(BF16)
        pieces = swap_groups(dot(w_dec[...], coarse))
        out[:, x, :] = pieces[0] + pieces[1] + pieces[2]


def skip_kernel(second, w_join, out):
    size_x = second.shape[0]
    r, c = iota((256, 16), 0), iota((256, 16), 1)
    rows = jnp.where((r >> 4) == c, 1.0, 0.0).astype(BF16)
    mixed = dot(rows, w_join[:, 0:16]).astype(BF16)
    r, c = iota((16, 256), 0), iota((16, 256), 1)
    cols = jnp.where((c & 15) == r, 1.0, 0.0).astype(BF16)
    r, c = iota((256, 256), 0), iota((256, 256), 1)
    matrix = jnp.where((r & 15) == (c >> 4), dot(mixed, cols), 0.0).astype(BF16)

    def step(q, carry):
        both = jnp.concatenate([second[2 * q], second[2 * q + 1]], axis=1)
        result = dot(matrix, both)
        out[2 * q] = result[:, :128]
        out[2 * q + 1] = result[:, 128:]
        return carry

    lax.fori_loop(0, size_x // 2, step, 0, unroll=4)


def join_kernel(skip, parts, w_join, out, held, sems):
    size_x = skip.shape[0]
    r, c = iota((256, 16), 0), iota((256, 16), 1)
    rows = jnp.where((r >> 4) == c, 1.0, 0.0).astype(BF16)
    up = dot(rows, w_join[:, 16:32]).astype(BF16)
    keep = (iota((16, 128), 1) >> 3) == iota((16, 128), 0)
    l0, l1 = iota((128, 128), 0), iota((128, 128), 1)
    widen = jnp.where((l0 & 7) == (l1 >> 4), 1.0, 0.0).astype(BF16)
    total = parts[0]
    for d in range(1, 16):
        total = total + parts[d]
    terms = []
    for block in range(2):
        decoded = jnp.broadcast_to(total[block : block + 1, :], (16, 128))
        decoded = jnp.where(keep, decoded, 0.0).astype(BF16)
        terms.append(dot(up, dot(decoded, widen).astype(BF16)))
    chunks, _, count = held.shape[:3]

    def copy(i):
        return pltpu.make_async_copy(
            held.at[i], out.at[:, i * count : (i + 1) * count], sems.at[i]
        )

    for i in range(chunks):
        for x in range(count):
            at = i * count + x
            value = (skip[at] + terms[at // POOL]).astype(BF16)
            held[i, :, x] = value.reshape(16, 16, 128)
        copy(i).start()
    for i in range(chunks):
        copy(i).wait()


def join(skip, parts, w_join):
    size_x = skip.shape[0]
    step = 4
    return pl.pallas_call(
        join_kernel,
        in_specs=[VMEM] * 3,
        out_specs=pl.BlockSpec(memory_space=pltpu.HBM),
        out_shape=shape(16, size_x, 16, 128),
        scratch_shapes=[
            pltpu.VMEM((size_x // step, 16, step, 16, 128), BF16),
            pltpu.SemaphoreType.DMA((size_x // step,)),
        ],
        compiler_params=pltpu.CompilerParams(vmem_limit_bytes=LIMIT),
        cost_estimate=pl.CostEstimate(flops=1 << 22, bytes_accessed=4 << 20, transcendentals=0),
    )(skip, parts, w_join)


def local(features, w_first, w_second, w_lift, w_coarse, w_decode, w_joining):
    size_x = features.shape[1]
    nx, ny = lax.axis_size("gx"), lax.axis_size("gy")
    gy = lax.axis_index("gy")

    def ring(count, step):
        return [(i, (i + step) % count) for i in range(count)]

    def swap(count, odd):
        return [(i, (((i + odd) ^ 1) - odd) % count) for i in range(count)]

    planes, gy_a, gy_b = pack(features)
    gy_a = lax.ppermute(gy_a, "gy", swap(ny, 0))
    gy_b = lax.ppermute(gy_b, "gy", swap(ny, 1))

    w_fine = jnp.concatenate([w_first, w_second], axis=0).reshape(864, 16)
    f1, t1, t2, t2_last = vmem_call(
        interior_kernel,
        [shape(size_x + 2, 288, 128), shape(144, 240), shape(144, 240), shape(48, 144)],
        (planes, w_fine),
        flops=2 * 1152 * 256 * 128 * size_x,
        nbytes=4 << 20,
    )
    faces, send_a, send_b = vmem_call(
        face_kernel,
        [shape(2, 2, 320, 128), shape(2, 320, 128), shape(2, 320, 128)],
        (planes, gy_a, gy_b),
        nbytes=1 << 19,
    )
    got_a = lax.ppermute(send_a, "gx", swap(nx, 0))
    got_b = lax.ppermute(send_b, "gx", swap(nx, 1))
    f1, second, psum = vmem_call(
        middle_kernel,
        [shape(size_x + 2, 288, 128), shape(size_x, 256, 128), shape(2, 16, 128, dtype=F32)],
        (f1, planes, gy_a, gy_b, t1, t2, t2_last),
        scratch=[pltpu.VMEM((size_x, 32, 128), BF16), pltpu.VMEM((size_x, 32, 128), BF16)],
        flops=2 * 2 * 1152 * 256 * 128 * size_x,
        nbytes=6 << 20,
        aliases={0: 0},
    )
    second, pooled = vmem_call(
        edge_kernel,
        [shape(size_x, 256, 128), shape(16, 2, 128, dtype=F32)],
        (second, f1, faces, got_a, got_b, psum, t1, t2, t2_last),
        scratch=[pltpu.VMEM((2, 4, 320, 128), BF16), pltpu.VMEM((2, 2, 288, 128), BF16)],
        flops=1 << 29,
        nbytes=1 << 20,
        aliases={0: 0},
    )

    count = w_coarse.shape[0]
    w_rows = jnp.transpose(w_coarse, (1, 0, 2)).reshape(27 * count, w_coarse.shape[2])
    w_dec = lax.dynamic_slice_in_dim(w_decode, gy * count, count, axis=1)
    own = lax.all_to_all(pooled, "gy", 0, 0)
    skip = vmem_call(
        skip_kernel,
        shape(size_x, 256, 128, dtype=F32),
        (second, w_joining),
        flops=2 * 256 * 256 * 128 * size_x,
        nbytes=6 << 20,
    )
    gl = lax.ppermute(own[:, 1, :], "gx", ring(nx, 1))
    gr = lax.ppermute(own[:, 0, :], "gx", ring(nx, -1))
    mine = vmem_call(
        own_kernel,
        shape(2, count, 128, dtype=F32),
        (own, w_lift, w_rows),
        flops=2 * 864 * 512 * 512,
        nbytes=2 << 20,
    )
    parts = vmem_call(
        beside_kernel,
        shape(16, 2, 128, dtype=F32),
        (mine, gl, gr, w_lift, w_rows, w_dec),
        flops=2 * 864 * 512 * 256,
        nbytes=2 << 20,
    )
    parts = lax.all_to_all(parts, "gy", 0, 0)
    return join(skip, parts, w_joining)


def solution(mesh):
    in_specs = (P(None, "gx", "gy", None), P(), P(), P(), P("gy", None, None), P(), P())
    out_specs = P(None, "gx", "gy", None)
    return jax.shard_map(local, mesh=mesh, in_specs=in_specs, out_specs=out_specs, check_vma=False)
```

```python
import jax
import jax.numpy as jnp
from jax import lax
from jax.experimental import pallas as pl
from jax.experimental.pallas import tpu as pltpu
from jax.sharding import PartitionSpec as P

POOL = 16
F32 = jnp.float32
BF16 = jnp.bfloat16
VMEM = pl.BlockSpec(memory_space=pltpu.VMEM)
LIMIT = 12 << 20


def iota(shape, dim):
    return lax.broadcasted_iota(jnp.int32, shape, dim)


def dot(a, b):
    return jnp.dot(a, b, preferred_element_type=F32)


def shape(*dims, dtype=BF16):
    return jax.ShapeDtypeStruct(dims, dtype)


def vmem_call(kernel, out_shape, args, scratch=(), flops=0, nbytes=0, far=()):
    args = [
        pltpu.with_memory_space_constraint(arg, pltpu.HBM) if i in far else arg
        for i, arg in enumerate(args)
    ]
    single = not isinstance(out_shape, (list, tuple))
    return pl.pallas_call(
        kernel,
        out_shape=out_shape,
        in_specs=[
            pl.BlockSpec(memory_space=pltpu.HBM) if i in far else VMEM for i in range(len(args))
        ],
        out_specs=VMEM if single else [VMEM for _ in out_shape],
        scratch_shapes=list(scratch),
        compiler_params=pltpu.CompilerParams(vmem_limit_bytes=LIMIT),
        cost_estimate=pl.CostEstimate(flops=flops, bytes_accessed=nbytes, transcendentals=0),
    )(*args)


def side_flags(axis):
    at, count = lax.axis_index(axis), lax.axis_size(axis)
    even = lax.rem(at, 2) == 0

    def number(flag):
        return jnp.where(flag, 1.0, 0.0).astype(F32)

    inner_left, inner_right = at > 0, at < count - 1
    left = number(jnp.logical_not(even)), number(jnp.logical_and(even, inner_left))
    right = number(even), number(jnp.logical_and(jnp.logical_not(even), inner_right))
    return left, right


def mix(a, b, flags):
    return (a.astype(F32) * flags[0] + b.astype(F32) * flags[1]).astype(BF16)


def scaled(v, m):
    return (v.astype(F32) * m).astype(BF16)


def is_even(axis):
    return jnp.where(lax.rem(lax.axis_index(axis), 2) == 0, 1, 0)


def pack_kernel(feat, planes, gy_a, gy_b, held, sems):
    chunks, _, count = held.shape[:3]

    def copy(i):
        return pltpu.make_async_copy(
            feat.at[:, i * count : (i + 1) * count], held.at[i], sems.at[i]
        )

    for i in range(chunks):
        copy(i).start()
    row, col = iota((256, 256), 0), iota((256, 256), 1)
    match = ((row >> 4) == (col & 15)) & ((row & 15) == (col >> 4))
    swap = jnp.where(match, 1.0, 0.0).astype(BF16)
    even = is_even("gy")
    rows_a = pl.multiple_of(even * 224, 32)
    rows_b = pl.multiple_of((1 - even) * 224, 32)
    for i in range(chunks):
        copy(i).wait()
        for x in range(0, count, 2):
            both = jnp.concatenate(
                [held[i, :, x].reshape(256, 128), held[i, :, x + 1].reshape(256, 128)], axis=1
            )
            moved = dot(swap, both).astype(BF16)
            planes[i * count + x] = moved[:, :128]
            planes[i * count + x + 1] = moved[:, 128:]
    gy_a[...] = planes[:, pl.ds(rows_a, 32), :]
    gy_b[...] = planes[:, pl.ds(rows_b, 32), :]


def pack(features):
    size_x = features.shape[1]
    step = 8
    return pl.pallas_call(
        pack_kernel,
        in_specs=[pl.BlockSpec(memory_space=pltpu.HBM)],
        out_specs=[VMEM] * 3,
        out_shape=[shape(size_x, 256, 128), shape(size_x, 32, 128), shape(size_x, 32, 128)],
        scratch_shapes=[
            pltpu.VMEM((size_x // step, 16, step, 16, 128), BF16),
            pltpu.SemaphoreType.DMA((size_x // step,)),
        ],
        compiler_params=pltpu.CompilerParams(vmem_limit_bytes=LIMIT),
        cost_estimate=pl.CostEstimate(
            flops=2 * 256 * 256 * 128 * size_x, bytes_accessed=5 << 20, transcendentals=0
        ),
    )(features)


def band(w, t_ref):
    copies = jnp.where((iota((16, 256), 1) & 15) == iota((16, 256), 0), 1.0, 0.0).astype(BF16)
    wide = dot(w, copies)
    group = iota((16, 256), 1) >> 4
    for c in range(3):
        for x in range(2):
            for y in range(2):
                total = jnp.zeros((16, 256), F32)
                for a in range(3):
                    for b in range(3):
                        k = 9 * a + 3 * b + c
                        here = group == 4 * (x + a) + y + b
                        total = jnp.where(here, wide[16 * k : 16 * k + 16], total)
                at = 16 * (4 * c + 2 * x + y)
                t_ref[at : at + 16, :] = total.astype(BF16)


def shifted_sum(acc, rows, half):
    lanes = slice(half * 128, half * 128 + 128)
    lane = iota((rows, 128), 1)
    before = pltpu.roll(acc[0:rows, lanes], 1, 1)
    after = pltpu.roll(acc[2 * rows : 3 * rows, lanes], 127, 1)
    total = acc[rows : 2 * rows, lanes]
    total = total + jnp.where(lane > 0, before, 0.0)
    total = total + jnp.where(lane < 127, after, 0.0)
    return jnp.maximum(total, 0.0)


def window(rows_of):
    return jnp.concatenate([rows_of(x) for x in range(4)], axis=0)


def conv_pair(t, first, second):
    acc = dot(t[...], jnp.concatenate([first, second], axis=1))
    return shifted_sum(acc, 64, 0), shifted_sum(acc, 64, 1)


def interior_kernel(planes, w, f1, rims, faces, t1, t2):
    size_x = planes.shape[0]
    rims[0] = planes[:, 0:32]
    rims[1] = planes[:, 224:256]
    faces[0] = planes[0:2]
    faces[1] = planes[size_x - 2 : size_x]
    band(w[0:432, :], t1)
    band(w[432:864, :], t2)

    def piece(at, j):
        return window(lambda x: planes[at + x, 32 * j : 32 * j + 64])

    def store(at, j, value):
        for x in range(2):
            f1[at + x, 32 * j + 32 : 32 * j + 64] = value[32 * x : 32 * x + 32].astype(BF16)

    def step(p, carry):
        at = 4 * p
        for j in range(7):
            for h, value in enumerate(conv_pair(t1, piece(at, j), piece(at + 2, j))):
                store(at + 2 * h, j, value)
        return carry

    lax.fori_loop(0, (size_x - 2) // 4, step, 0, unroll=7)
    at = size_x - 4
    for pair in ((0, 1), (2, 3), (4, 5), (5, 6)):
        for j, value in zip(pair, conv_pair(t1, piece(at, pair[0]), piece(at, pair[1]))):
            store(at, j, value)


def rim_kernel(inner, rims, faces, gy_a, gy_b, t1, f1, send_a, send_b, halo):
    size_x = rims.shape[1]
    left, right = side_flags("gy")
    y_left, y_right = left[0] + left[1], right[0] + right[1]

    def fill(x, carry):
        halo[0, x] = mix(gy_a[x], gy_b[x], left)
        halo[1, x] = mix(gy_a[x], gy_b[x], right)
        return carry

    lax.fori_loop(0, size_x, fill, 0, unroll=4)
    even = is_even("gx")
    for send, side in ((send_a, even), (send_b, 1 - even)):
        for j in range(2):
            x = side * (size_x - 2) + j
            send[j, 0:32] = halo[0, x]
            send[j, 32:288] = faces[side, j]
            send[j, 288:320] = halo[1, x]

    def step(p, carry):
        at = 2 * p
        low = window(lambda x: jnp.concatenate([halo[0, at + x], rims[0, at + x]], axis=0))
        high = window(lambda x: jnp.concatenate([rims[1, at + x], halo[1, at + x]], axis=0))
        low, high = conv_pair(t1, low, high)
        for x in range(2):
            cut = slice(32 * x, 32 * x + 16), slice(32 * x + 16, 32 * x + 32)
            f1[at + x, 0:16] = (low[cut[0]] * y_left).astype(BF16)
            f1[at + x, 16:32] = low[cut[1]].astype(BF16)
            f1[at + x, 32:256] = inner[at + x, 32:256]
            f1[at + x, 256:272] = high[cut[0]].astype(BF16)
            f1[at + x, 272:288] = (high[cut[1]] * y_right).astype(BF16)
        return carry

    lax.fori_loop(0, (size_x - 2) // 2, step, 0, unroll=15)


def fold_rows(value):
    return jnp.sum(value.astype(F32).reshape(4, 16, 128), axis=0)


def middle_kernel(f1, t2, second, f1_ends, psum):
    size_x = f1.shape[0] + 2
    f1_ends[0:2] = f1[0:2]
    f1_ends[2:4] = f1[size_x - 4 : size_x - 2]
    psum[...] = jnp.zeros(psum.shape, F32)

    def step(q, carry):
        at = 2 * q - 2
        summed = jnp.zeros((16, 128), F32)

        def piece(j):
            return window(lambda x: f1[at + x, 32 * j : 32 * j + 64])

        for j in range(0, 8, 2):
            for h, value in enumerate(conv_pair(t2, piece(j), piece(j + 1))):
                value = value.astype(BF16)
                row = 32 * (j + h)
                for x in range(2):
                    second[at + x, row : row + 32] = value[32 * x : 32 * x + 32]
                summed = summed + fold_rows(value)
        psum[q // (POOL // 2)] += summed
        return carry

    lax.fori_loop(1, size_x // 2 - 1, step, 0, unroll=14)


def edge_kernel(
    inner, f1_ends, send_a, send_b, far_a, far_b, psum_in, t1, t2, left_out, right_out,
    pooled, fe, fx, got_a, got_b, sems,
):
    fetches = [
        pltpu.make_async_copy(far_a, got_a, sems.at[0]),
        pltpu.make_async_copy(far_b, got_b, sems.at[1]),
    ]
    for fetch in fetches:
        fetch.start()
    half = left_out.shape[0]
    size_x = 2 * half
    moved = iter(range(size_x - 4))

    def put(x, rows, value):
        if x < half:
            left_out[x, rows] = value
        else:
            right_out[x - half, rows] = value

    def carry_over():
        for at in (next(moved, None), next(moved, None)):
            if at is not None:
                put(at + 2, slice(0, 256), inner[at])

    x_left, x_right = side_flags("gx")
    y_left, y_right = side_flags("gy")
    y_left, y_right = y_left[0] + y_left[1], y_right[0] + y_right[1]
    even = is_even("gx").astype(F32)
    for fetch in fetches:
        fetch.wait()
    for j in range(2):
        fe[0, j] = mix(got_a[j], got_b[j], x_left)
        fe[0, 2 + j] = mix(send_a[j], send_b[j], (1.0 - even, even))
        fe[1, j] = mix(send_a[j], send_b[j], (even, 1.0 - even))
        fe[1, 2 + j] = mix(got_a[j], got_b[j], x_right)
    keeps = ((x_left[0] + x_left[1], 1.0), (1.0, x_right[0] + x_right[1]))
    for j in range(9):
        carry_over()
        pieces = [window(lambda x: fe[s, x, 32 * j : 32 * j + 64]) for s in range(2)]
        for s, value in enumerate(conv_pair(t1, *pieces)):
            for x in range(2):
                for y in range(2):
                    part = value[32 * x + 16 * y : 32 * x + 16 * y + 16] * keeps[s][x]
                    if j == 0 and y == 0:
                        part = part * y_left
                    if j == 8 and y == 1:
                        part = part * y_right
                    row = 32 * j + 16 * y
                    fx[s, x, row : row + 16] = part.astype(BF16)

    def left(j):
        cut = slice(32 * j, 32 * j + 64)
        return window(lambda x: fx[0, x, cut] if x < 2 else f1_ends[x - 2, cut])

    def right(j):
        cut = slice(32 * j, 32 * j + 64)
        return window(lambda x: f1_ends[2 + x, cut] if x < 2 else fx[1, x - 2, cut])

    sums = [psum_in[0], psum_in[1]]
    for j in range(8):
        carry_over()
        for s, value in enumerate(conv_pair(t2, left(j), right(j))):
            value = value.astype(BF16)
            for x in range(2):
                cut = slice(32 * j, 32 * j + 32)
                put(s * (size_x - 2) + x, cut, value[32 * x : 32 * x + 32])
            sums[s] = sums[s] + fold_rows(value)

    z, lane = iota((128, 128), 0), iota((128, 128), 1)
    gather = jnp.where((z >> 4) == (lane & 7), 1.0, 0.0).astype(F32)
    keep = (iota((16, 128), 1) >> 3) == iota((16, 128), 0)
    results = []
    for s in range(2):
        cells = jnp.dot(
            sums[s], gather, preferred_element_type=F32, precision=lax.Precision.HIGHEST
        )
        row = jnp.sum(jnp.where(keep, cells, 0.0), axis=0, keepdims=True) * (1.0 / POOL**3)
        results.append(row)
    both = jnp.concatenate(results, axis=0)
    for d in range(16):
        pooled[d] = both


def split3(v):
    a = v.astype(BF16)
    v = v - a.astype(F32)
    b = v.astype(BF16)
    c = (v - b.astype(F32)).astype(BF16)
    return a, b, c


def swap_groups(rows):
    lane = iota((256, 128), 1)
    major, minor = iota((256, 128), 0) >> 4, iota((256, 128), 0) & 15
    spread = jnp.broadcast_to(rows[:, None, :], (16, 16, 128)).reshape(256, 128)
    spread = jnp.where((lane >> 3) == minor, spread, 0.0)
    l0, l1 = iota((128, 128), 0), iota((128, 128), 1)
    fold = jnp.where((l0 & 7) == (l1 & 7), 1.0, 0.0).astype(BF16)
    out = []
    for piece in split3(spread):
        moved = jnp.where((lane >> 3) == major, dot(piece, fold), 0.0)
        out.append(jnp.sum(moved.reshape(16, 16, 128), axis=0))
    return out


def lift_slabs(slabs, w_lift):
    columns = []
    for slab in slabs:
        pieces = [v.astype(BF16) for v in swap_groups(slab)]
        columns.append(jnp.concatenate(pieces, axis=0))
    stacked = jnp.concatenate(columns, axis=1)
    lift3 = jnp.concatenate([w_lift] * 3, axis=1)
    return jnp.maximum(dot(lift3, stacked), 0.0).astype(BF16)


def taps(partial, count):
    lane = iota((count, 128), 1)
    y, z = lane >> 3, lane & 7
    total = jnp.zeros((count, 128), F32)
    for k in range(9):
        b, c = k // 3 - 1, k % 3 - 1
        piece = partial[k * count : (k + 1) * count, :]
        step = 8 * b + c
        if step:
            piece = pltpu.roll(piece, (-step) % 128, 1)
        good = None
        if b:
            good = (y < 15) if b > 0 else (y > 0)
        if c:
            inside = (z < 7) if c > 0 else (z > 0)
            good = inside if good is None else good & inside
        total = total + (piece if good is None else jnp.where(good, piece, 0.0))
    return total


def own_kernel(own, w_lift, w_coarse, out):
    count = w_coarse.shape[0] // 27
    lifted = lift_slabs([own[:, 0, :], own[:, 1, :]], w_lift[...])
    partial = dot(w_coarse[...], lifted)
    for x in range(2):
        total = jnp.zeros((count, 128), F32)
        for slab in range(2):
            a = slab - x + 1
            piece = partial[9 * a * count : 9 * (a + 1) * count, slab * 128 : slab * 128 + 128]
            total = total + taps(piece, count)
        out[x] = total


def beside_kernel(mine, gl, gr, w_lift, w_coarse, w_dec, out):
    count = w_coarse.shape[0] // 27
    at, last = lax.axis_index("gx"), lax.axis_size("gx") - 1
    m_left = jnp.where(at > 0, 1.0, 0.0).astype(F32)
    m_right = jnp.where(at < last, 1.0, 0.0).astype(F32)
    lifted = lift_slabs([gl[...] * m_left, gr[...] * m_right], w_lift[...])
    for x in range(2):
        a = 2 * x
        rows = w_coarse[9 * a * count : 9 * (a + 1) * count, :]
        total = mine[x] + taps(dot(rows, lifted[:, x * 128 : x * 128 + 128]), count)
        coarse = jnp.maximum(total, 0.0).astype(BF16)
        pieces = swap_groups(dot(w_dec[...], coarse))
        out[:, x, :] = pieces[0] + pieces[1] + pieces[2]


def skip_planes(matrix, second, at):
    both = jnp.concatenate([second[at], second[at + 1]], axis=1)
    result = dot(matrix[...], both)
    return result[:, :128], result[:, 128:]


def skip_kernel(second, w_join, matrix, up, ahead):
    r, c = iota((256, 16), 0), iota((256, 16), 1)
    rows = jnp.where((r >> 4) == c, 1.0, 0.0).astype(BF16)
    mixed = dot(rows, w_join[...]).astype(BF16)
    up[...] = mixed[:, 16:32]
    r, c = iota((16, 256), 0), iota((16, 256), 1)
    cols = jnp.where((c & 15) == r, 1.0, 0.0).astype(BF16)
    r, c = iota((256, 256), 0), iota((256, 256), 1)
    match = (r & 15) == (c >> 4)
    matrix[...] = jnp.where(match, dot(mixed[:, 0:16], cols), 0.0).astype(BF16)
    for at in range(0, ahead.shape[0], 2):
        ahead[at], ahead[at + 1] = skip_planes(matrix, second, at)


def join_kernel(left, right, ahead, matrix, up, parts, out, held, sems):
    half = left.shape[0]
    keep = (iota((16, 128), 1) >> 3) == iota((16, 128), 0)
    l0, l1 = iota((128, 128), 0), iota((128, 128), 1)
    widen = jnp.where((l0 & 7) == (l1 >> 4), 1.0, 0.0).astype(BF16)
    total = parts[0]
    for d in range(1, 16):
        total = total + parts[d]
    terms = []
    for block in range(2):
        decoded = jnp.broadcast_to(total[block : block + 1, :], (16, 128))
        decoded = jnp.where(keep, decoded, 0.0).astype(BF16)
        terms.append(dot(up[...], dot(decoded, widen).astype(BF16)))
    chunks, _, count = held.shape[:3]

    def copy(i):
        return pltpu.make_async_copy(
            held.at[i], out.at[:, i * count : (i + 1) * count], sems.at[i]
        )

    for i in range(chunks):
        for x in range(0, count, 2):
            at = i * count + x
            if at < ahead.shape[0]:
                skips = ahead[at], ahead[at + 1]
            else:
                skips = skip_planes(matrix, (left, right)[at // half], at % half)
            for h in range(2):
                value = (skips[h] + terms[at // POOL]).astype(BF16)
                held[i, :, x + h] = value.reshape(16, 16, 128)
        copy(i).start()
    for i in range(chunks):
        copy(i).wait()


def join(left, right, ahead, matrix, up, parts):
    size_x = 2 * left.shape[0]
    step = 4
    return pl.pallas_call(
        join_kernel,
        in_specs=[VMEM] * 6,
        out_specs=pl.BlockSpec(memory_space=pltpu.HBM),
        out_shape=shape(16, size_x, 16, 128),
        scratch_shapes=[
            pltpu.VMEM((size_x // step, 16, step, 16, 128), BF16),
            pltpu.SemaphoreType.DMA((size_x // step,)),
        ],
        compiler_params=pltpu.CompilerParams(vmem_limit_bytes=LIMIT),
        cost_estimate=pl.CostEstimate(
            flops=2 * 256 * 256 * 128 * size_x, bytes_accessed=4 << 20, transcendentals=0
        ),
    )(left, right, ahead, matrix, up, parts)


def local(features, w_first, w_second, w_lift, w_coarse, w_decode, w_joining):
    size_x = features.shape[1]
    nx, ny = lax.axis_size("gx"), lax.axis_size("gy")
    gy = lax.axis_index("gy")

    def ring(count, step):
        return [(i, (i + step) % count) for i in range(count)]

    def swap(count, odd):
        return [(i, (((i + odd) ^ 1) - odd) % count) for i in range(count)]

    planes, gy_a, gy_b = pack(pltpu.with_memory_space_constraint(features, pltpu.HBM))
    gy_a = lax.ppermute(gy_a, "gy", swap(ny, 0))
    gy_b = lax.ppermute(gy_b, "gy", swap(ny, 1))

    w_fine = jnp.concatenate([w_first, w_second], axis=0).reshape(864, 16)
    first = shape(size_x - 2, 288, 128)
    f1, rims, faces, t1, t2 = vmem_call(
        interior_kernel,
        [
            first,
            shape(2, size_x, 32, 128),
            shape(2, 2, 256, 128),
            shape(192, 256),
            shape(192, 256),
        ],
        (planes, w_fine),
        flops=2 * 192 * 256 * 256 * 53,
        nbytes=4 << 20,
    )
    f1, send_a, send_b = vmem_call(
        rim_kernel,
        [first, shape(2, 320, 128), shape(2, 320, 128)],
        (f1, rims, faces, gy_a, gy_b, t1),
        scratch=[pltpu.VMEM((2, size_x, 32, 128), BF16)],
        flops=2 * 192 * 256 * 256 * 15,
        nbytes=1 << 20,
    )
    got_a = lax.ppermute(send_a, "gx", swap(nx, 0))
    got_b = lax.ppermute(send_b, "gx", swap(nx, 1))
    second, f1_ends, psum = vmem_call(
        middle_kernel,
        [shape(size_x - 4, 256, 128), shape(4, 288, 128), shape(2, 16, 128, dtype=F32)],
        (f1, t2),
        flops=2 * 192 * 256 * 256 * 56,
        nbytes=6 << 20,
    )
    half = shape(size_x // 2, 256, 128)
    *seconds, pooled = vmem_call(
        edge_kernel,
        [half, half, shape(16, 2, 128, dtype=F32)],
        (second, f1_ends, send_a, send_b, got_a, got_b, psum, t1, t2),
        scratch=[
            pltpu.VMEM((2, 4, 320, 128), BF16),
            pltpu.VMEM((2, 2, 288, 128), BF16),
            pltpu.VMEM((2, 320, 128), BF16),
            pltpu.VMEM((2, 320, 128), BF16),
            pltpu.SemaphoreType.DMA((2,)),
        ],
        far=(4, 5),
        flops=2 * 192 * 256 * 256 * 17,
        nbytes=1 << 20,
    )

    count = w_coarse.shape[0]
    w_rows = jnp.transpose(w_coarse, (1, 0, 2)).reshape(27 * count, w_coarse.shape[2])
    w_dec = lax.dynamic_slice_in_dim(w_decode, gy * count, count, axis=1)
    own = lax.all_to_all(pooled, "gy", 0, 0)
    gl = lax.ppermute(own[:, 1, :], "gx", ring(nx, 1))
    gr = lax.ppermute(own[:, 0, :], "gx", ring(nx, -1))
    mine = vmem_call(
        own_kernel,
        shape(2, count, 128, dtype=F32),
        (own, w_lift, w_rows),
        flops=2 * 864 * 512 * 512,
        nbytes=2 << 20,
    )
    parts = vmem_call(
        beside_kernel,
        shape(16, 2, 128, dtype=F32),
        (mine, gl, gr, w_lift, w_rows, w_dec),
        flops=2 * 864 * 512 * 256,
        nbytes=2 << 20,
    )
    parts = lax.all_to_all(parts, "gy", 0, 0)
    matrix, up, ahead = vmem_call(
        skip_kernel,
        [shape(256, 256), shape(256, 16), shape(8, 256, 128, dtype=F32)],
        (seconds[0], w_joining),
        flops=2 * 256 * 256 * 128 * 8,
        nbytes=2 << 20,
    )
    return join(*seconds, ahead, matrix, up, parts)


def solution(mesh):
    in_specs = (P(None, "gx", "gy", None), P(), P(), P(), P("gy", None, None), P(), P())
    out_specs = P(None, "gx", "gy", None)
    return jax.shard_map(local, mesh=mesh, in_specs=in_specs, out_specs=out_specs, check_vma=False)
```

```python
import jax
import jax.numpy as jnp
from jax import lax
from jax.experimental import pallas as pl
from jax.experimental.pallas import tpu as pltpu
from jax.sharding import PartitionSpec as P

POOL = 16
F32 = jnp.float32
BF16 = jnp.bfloat16
VMEM = pl.BlockSpec(memory_space=pltpu.VMEM)
LIMIT = 12 << 20


def iota(shape, dim):
    return lax.broadcasted_iota(jnp.int32, shape, dim)


def dot(a, b):
    return jnp.dot(a, b, preferred_element_type=F32)


def shape(*dims, dtype=BF16):
    return jax.ShapeDtypeStruct(dims, dtype)


def vmem_call(kernel, out_shape, args, scratch=(), flops=0, nbytes=0, far=(), far_out=()):
    args = [
        pltpu.with_memory_space_constraint(arg, pltpu.HBM) if i in far else arg
        for i, arg in enumerate(args)
    ]
    single = not isinstance(out_shape, (list, tuple))
    if far_out:
        out_shape = [
            pltpu.HBM(out.shape, out.dtype) if i in far_out else out
            for i, out in enumerate(out_shape)
        ]
    return pl.pallas_call(
        kernel,
        out_shape=out_shape,
        in_specs=[
            pl.BlockSpec(memory_space=pltpu.HBM) if i in far else VMEM for i in range(len(args))
        ],
        out_specs=(
            VMEM
            if single
            else [
                pl.BlockSpec(memory_space=pltpu.HBM) if i in far_out else VMEM
                for i in range(len(out_shape))
            ]
        ),
        scratch_shapes=list(scratch),
        compiler_params=pltpu.CompilerParams(vmem_limit_bytes=LIMIT),
        cost_estimate=pl.CostEstimate(flops=flops, bytes_accessed=nbytes, transcendentals=0),
    )(*args)


def side_flags(axis):
    at, count = lax.axis_index(axis), lax.axis_size(axis)
    even = lax.rem(at, 2) == 0

    def number(flag):
        return jnp.where(flag, 1.0, 0.0).astype(F32)

    inner_left, inner_right = at > 0, at < count - 1
    left = number(jnp.logical_not(even)), number(jnp.logical_and(even, inner_left))
    right = number(even), number(jnp.logical_and(jnp.logical_not(even), inner_right))
    return left, right


def mix(a, b, flags):
    return (a.astype(F32) * flags[0] + b.astype(F32) * flags[1]).astype(BF16)


def scaled(v, m):
    return (v.astype(F32) * m).astype(BF16)


def is_even(axis):
    return jnp.where(lax.rem(lax.axis_index(axis), 2) == 0, 1, 0)


def fetch_planes(far, feat, sems):
    parts = sems.shape[0]
    count = far.shape[1] // parts
    fetches = [
        pltpu.make_async_copy(
            far.at[:, i * count : (i + 1) * count],
            feat.at[:, i * count : (i + 1) * count],
            sems.at[i],
        )
        for i in range(parts)
    ]
    for fetch in fetches:
        fetch.start()
    return fetches, count


def rows_kernel(far, gy_a, gy_b, feat, sems):
    fetches, count = fetch_planes(far, feat, sems)
    size_x = feat.shape[1]
    even = is_even("gy")
    row, col = iota((64, 256), 0), iota((64, 256), 1)
    upper = jnp.where(row < 32, even, 1 - even)
    match = ((row & 15) == (col >> 4)) & ((col & 15) == ((row >> 4) & 1) + 14 * upper)
    select = jnp.where(match, 1.0, 0.0).astype(BF16)
    for x in range(0, size_x, 2):
        if x % count == 0:
            fetches[x // count].wait()
        both = jnp.concatenate(
            [feat[:, x].reshape(256, 128), feat[:, x + 1].reshape(256, 128)], axis=1
        )
        rows = dot(select, both).astype(BF16)
        for h in range(2):
            gy_a[x + h] = rows[0:32, 128 * h : 128 * h + 128]
            gy_b[x + h] = rows[32:64, 128 * h : 128 * h + 128]


def swap_rows(feat, planes):
    row, col = iota((256, 256), 0), iota((256, 256), 1)
    match = ((row >> 4) == (col & 15)) & ((row & 15) == (col >> 4))
    swap = jnp.where(match, 1.0, 0.0).astype(BF16)
    for x in range(0, feat.shape[1], 2):
        both = jnp.concatenate(
            [feat[:, x].reshape(256, 128), feat[:, x + 1].reshape(256, 128)], axis=1
        )
        moved = dot(swap, both).astype(BF16)
        planes[x] = moved[:, :128]
        planes[x + 1] = moved[:, 128:]


def band(w, t_ref):
    copies = jnp.where((iota((16, 256), 1) & 15) == iota((16, 256), 0), 1.0, 0.0).astype(BF16)
    wide = dot(w, copies)
    group = iota((16, 256), 1) >> 4
    for c in range(3):
        for x in range(2):
            for y in range(2):
                total = jnp.zeros((16, 256), F32)
                for a in range(3):
                    for b in range(3):
                        k = 9 * a + 3 * b + c
                        here = group == 4 * (x + a) + y + b
                        total = jnp.where(here, wide[16 * k : 16 * k + 16], total)
                at = 16 * (4 * c + 2 * x + y)
                t_ref[at : at + 16, :] = total.astype(BF16)


def shifted_sum(acc, rows, half):
    lanes = slice(half * 128, half * 128 + 128)
    lane = iota((rows, 128), 1)
    before = pltpu.roll(acc[0:rows, lanes], 1, 1)
    after = pltpu.roll(acc[2 * rows : 3 * rows, lanes], 127, 1)
    total = acc[rows : 2 * rows, lanes]
    total = total + jnp.where(lane > 0, before, 0.0)
    total = total + jnp.where(lane < 127, after, 0.0)
    return jnp.maximum(total, 0.0)


def window(rows_of):
    return jnp.concatenate([rows_of(x) for x in range(4)], axis=0)


def conv_pair(t, first, second):
    acc = dot(t[...], jnp.concatenate([first, second], axis=1))
    return shifted_sum(acc, 64, 0), shifted_sum(acc, 64, 1)


def plane_of(parts, x):
    count = parts[0].shape[0]
    return (parts[0], x) if x < count else (parts[1], x - count)


def interior_kernel(far, w, low, high_far, rims, faces, t1, t2, planes, feat, high, sems, puts):
    fetches, _ = fetch_planes(far, feat, sems)
    size_x = planes.shape[0]
    band(w[0:432, :], t1)
    band(w[432:864, :], t2)
    for fetch in fetches:
        fetch.wait()
    swap_rows(feat, planes)
    rims[0] = planes[:, 0:32]
    rims[1] = planes[:, 224:256]
    faces[0] = planes[0:2]
    faces[1] = planes[size_x - 2 : size_x]

    def piece(at, j):
        return window(lambda x: planes[at + x, 32 * j : 32 * j + 64])

    def store(at, j, value):
        for x in range(2):
            to, index = plane_of((low, high), at + x)
            to[index, 32 * j : 32 * j + 32] = value[32 * x : 32 * x + 32].astype(BF16)

    half = high.shape[0] // 2

    def put(i):
        span = pl.ds(i * half, half)
        return pltpu.make_async_copy(high.at[span], high_far.at[span], puts.at[i])

    at = size_x - 4
    for pair in ((0, 1), (2, 3), (4, 5), (5, 6)):
        for j, value in zip(pair, conv_pair(t1, piece(at, pair[0]), piece(at, pair[1]))):
            store(at, j, value)
    for at in range(size_x - 8, -1, -4):
        for j in range(7):
            for h, value in enumerate(conv_pair(t1, piece(at, j), piece(at + 2, j))):
                store(at + 2 * h, j, value)
        start = low.shape[0]
        for i in (1, 0):
            if at <= start + i * half < at + 4:
                put(i).start()
    for i in range(2):
        put(i).wait()


def rim_kernel(rims, faces, gy_a, gy_b, t1, rim_rows, send_a, send_b, halo):
    size_x = rims.shape[1]
    left, right = side_flags("gy")
    y_left, y_right = left[0] + left[1], right[0] + right[1]

    def fill(x, carry):
        halo[0, x] = mix(gy_a[x], gy_b[x], left)
        halo[1, x] = mix(gy_a[x], gy_b[x], right)
        return carry

    lax.fori_loop(0, size_x, fill, 0, unroll=4)
    even = is_even("gx")
    for send, side in ((send_a, even), (send_b, 1 - even)):
        for j in range(2):
            x = side * (size_x - 2) + j
            send[j, 0:32] = halo[0, x]
            send[j, 32:288] = faces[side, j]
            send[j, 288:320] = halo[1, x]

    for at in range(0, size_x - 2, 2):
        low = window(lambda x: jnp.concatenate([halo[0, at + x], rims[0, at + x]], axis=0))
        high = window(lambda x: jnp.concatenate([rims[1, at + x], halo[1, at + x]], axis=0))
        low, high = conv_pair(t1, low, high)
        for x in range(2):
            cut = slice(32 * x, 32 * x + 16), slice(32 * x + 16, 32 * x + 32)
            rim_rows[at + x, 0:16] = (low[cut[0]] * y_left).astype(BF16)
            rim_rows[at + x, 16:32] = low[cut[1]].astype(BF16)
            rim_rows[at + x, 32:48] = high[cut[0]].astype(BF16)
            rim_rows[at + x, 48:64] = (high[cut[1]] * y_right).astype(BF16)


def fold_rows(value):
    return jnp.sum(value.astype(F32).reshape(4, 16, 128), axis=0)


def middle_kernel(low, high_far, rim_rows, t2, second, f1_ends, psum, high, sem):
    fetch = pltpu.make_async_copy(high_far, high, sem)
    fetch.start()
    size_x = low.shape[0] + high.shape[0] + 2

    def rows(x, j):
        inner, at = plane_of((low, high), x)
        if j == 0:
            return jnp.concatenate([rim_rows[x, 0:32], inner[at, 0:32]], axis=0)
        if j == 7:
            return jnp.concatenate([inner[at, 192:224], rim_rows[x, 32:64]], axis=0)
        return inner[at, 32 * j - 32 : 32 * j + 32]

    sums = [jnp.zeros((16, 128), F32) for _ in range(2)]
    for at in range(0, size_x - 4, 2):
        if at + 2 == low.shape[0]:
            fetch.wait()

        def piece(j):
            return window(lambda x: rows(at + x, j))

        for j in range(0, 8, 2):
            for h, value in enumerate(conv_pair(t2, piece(j), piece(j + 1))):
                value = value.astype(BF16)
                row = 32 * (j + h)
                for x in range(2):
                    second[at + x, row : row + 32] = value[32 * x : 32 * x + 32]
                sums[(at + 2) // POOL] += fold_rows(value)
    psum[0], psum[1] = sums
    for i, x in enumerate((0, 1, size_x - 4, size_x - 3)):
        inner, at = plane_of((low, high), x)
        f1_ends[i, 0:32] = rim_rows[x, 0:32]
        f1_ends[i, 32:256] = inner[at]
        f1_ends[i, 256:288] = rim_rows[x, 32:64]


def edge_kernel(
    inner, f1_ends, send_a, send_b, got_a, got_b, psum_in, t1, t2, left_out, right_out,
    pooled, fe, fx,
):
    half = left_out.shape[0]
    size_x = 2 * half
    moved = iter(range(size_x - 4))

    def put(x, rows, value):
        if x < half:
            left_out[x, rows] = value
        else:
            right_out[x - half, rows] = value

    def carry_over():
        for at in (next(moved, None), next(moved, None)):
            if at is not None:
                put(at + 2, slice(0, 256), inner[at])

    x_left, x_right = side_flags("gx")
    y_left, y_right = side_flags("gy")
    y_left, y_right = y_left[0] + y_left[1], y_right[0] + y_right[1]
    even = is_even("gx").astype(F32)
    for j in range(2):
        fe[0, j] = mix(got_a[j], got_b[j], x_left)
        fe[0, 2 + j] = mix(send_a[j], send_b[j], (1.0 - even, even))
        fe[1, j] = mix(send_a[j], send_b[j], (even, 1.0 - even))
        fe[1, 2 + j] = mix(got_a[j], got_b[j], x_right)
    keeps = ((x_left[0] + x_left[1], 1.0), (1.0, x_right[0] + x_right[1]))
    for j in range(9):
        carry_over()
        pieces = [window(lambda x: fe[s, x, 32 * j : 32 * j + 64]) for s in range(2)]
        for s, value in enumerate(conv_pair(t1, *pieces)):
            for x in range(2):
                for y in range(2):
                    part = value[32 * x + 16 * y : 32 * x + 16 * y + 16] * keeps[s][x]
                    if j == 0 and y == 0:
                        part = part * y_left
                    if j == 8 and y == 1:
                        part = part * y_right
                    row = 32 * j + 16 * y
                    fx[s, x, row : row + 16] = part.astype(BF16)

    def left(j):
        cut = slice(32 * j, 32 * j + 64)
        return window(lambda x: fx[0, x, cut] if x < 2 else f1_ends[x - 2, cut])

    def right(j):
        cut = slice(32 * j, 32 * j + 64)
        return window(lambda x: f1_ends[2 + x, cut] if x < 2 else fx[1, x - 2, cut])

    sums = [psum_in[0], psum_in[1]]
    for j in range(8):
        carry_over()
        for s, value in enumerate(conv_pair(t2, left(j), right(j))):
            value = value.astype(BF16)
            for x in range(2):
                cut = slice(32 * j, 32 * j + 32)
                put(s * (size_x - 2) + x, cut, value[32 * x : 32 * x + 32])
            sums[s] = sums[s] + fold_rows(value)

    z, lane = iota((128, 128), 0), iota((128, 128), 1)
    gather = jnp.where((z >> 4) == (lane & 7), 1.0, 0.0).astype(F32)
    keep = (iota((16, 128), 1) >> 3) == iota((16, 128), 0)
    results = []
    for s in range(2):
        cells = jnp.dot(
            sums[s], gather, preferred_element_type=F32, precision=lax.Precision.HIGHEST
        )
        row = jnp.sum(jnp.where(keep, cells, 0.0), axis=0, keepdims=True) * (1.0 / POOL**3)
        results.append(row)
    both = jnp.concatenate(results, axis=0)
    for d in range(16):
        pooled[d] = both


def split3(v):
    a = v.astype(BF16)
    v = v - a.astype(F32)
    b = v.astype(BF16)
    c = (v - b.astype(F32)).astype(BF16)
    return [a, b, c]


def swap_groups(rows):
    lane = iota((16, 128), 1) >> 3
    total = jnp.zeros((16, 128), F32)
    rows = pltpu.roll(pltpu.roll(rows, 0, 1, stride=8, stride_axis=0), 8, 1)
    for s in range(16):
        spread = jnp.broadcast_to(rows[s : s + 1, :], (16, 128))
        moved = pltpu.roll(spread, 0, 1, stride=8, stride_axis=0)
        total = jnp.where(lane == s, moved, total)
    return total


def load_kernel(far, after, out, sem):
    fetch = pltpu.make_async_copy(far, out, sem)
    fetch.start()
    fetch.wait()


def lift_slabs(slabs, w_lift):
    columns = []
    for slab in slabs:
        columns.append(jnp.concatenate(split3(swap_groups(slab)), axis=0))
    stacked = jnp.concatenate(columns, axis=1)
    lift3 = jnp.concatenate([w_lift] * 3, axis=1)
    return jnp.maximum(dot(lift3, stacked), 0.0).astype(BF16)


def taps(partial, count):
    lane = iota((count, 128), 1)
    y, z = lane >> 3, lane & 7
    total = jnp.zeros((count, 128), F32)
    for k in range(9):
        b, c = k // 3 - 1, k % 3 - 1
        piece = partial[k * count : (k + 1) * count, :]
        step = 8 * b + c
        if step:
            piece = pltpu.roll(piece, (-step) % 128, 1)
        good = None
        if b:
            good = (y < 15) if b > 0 else (y > 0)
        if c:
            inside = (z < 7) if c > 0 else (z > 0)
            good = inside if good is None else good & inside
        total = total + (piece if good is None else jnp.where(good, piece, 0.0))
    return total


def own_kernel(own, w_lift, w_coarse, out):
    count = w_coarse.shape[0] // 27
    lifted = lift_slabs([own[:, 0, :], own[:, 1, :]], w_lift[...])
    partial = dot(w_coarse[...], lifted)
    for x in range(2):
        total = jnp.zeros((count, 128), F32)
        for slab in range(2):
            a = slab - x + 1
            piece = partial[9 * a * count : 9 * (a + 1) * count, slab * 128 : slab * 128 + 128]
            total = total + taps(piece, count)
        out[x] = total


def beside_kernel(mine, gl, gr, w_lift, w_coarse, w_dec, out):
    count = w_coarse.shape[0] // 27
    at, last = lax.axis_index("gx"), lax.axis_size("gx") - 1
    m_left = jnp.where(at > 0, 1.0, 0.0).astype(F32)
    m_right = jnp.where(at < last, 1.0, 0.0).astype(F32)
    lifted = lift_slabs([gl[...] * m_left, gr[...] * m_right], w_lift[...])
    for x in range(2):
        a = 2 * x
        rows = w_coarse[9 * a * count : 9 * (a + 1) * count, :]
        total = mine[x] + taps(dot(rows, lifted[:, x * 128 : x * 128 + 128]), count)
        coarse = jnp.maximum(total, 0.0).astype(BF16)
        rows = swap_groups(dot(w_dec[...], coarse))
        for y in range(16):
            out[y, x : x + 1, :] = rows[15 - y : 16 - y, :]


def skip_planes(matrix, second, at):
    both = jnp.concatenate([second[at], second[at + 1]], axis=1)
    result = dot(matrix[...], both)
    return result[:, :128], result[:, 128:]


def skip_kernel(second, w_join, matrix, up, ahead):
    r, c = iota((256, 16), 0), iota((256, 16), 1)
    rows = jnp.where((r >> 4) == c, 1.0, 0.0).astype(BF16)
    mixed = dot(rows, w_join[...]).astype(BF16)
    up[...] = mixed[:, 16:32]
    r, c = iota((16, 256), 0), iota((16, 256), 1)
    cols = jnp.where((c & 15) == r, 1.0, 0.0).astype(BF16)
    r, c = iota((256, 256), 0), iota((256, 256), 1)
    match = (r & 15) == (c >> 4)
    matrix[...] = jnp.where(match, dot(mixed[:, 0:16], cols), 0.0).astype(BF16)
    for at in range(0, ahead.shape[0], 2):
        ahead[at], ahead[at + 1] = skip_planes(matrix, second, at)


def join_kernel(left, right, ahead, matrix, up, parts, out, held, sems):
    half = left.shape[0]
    keep = (iota((16, 128), 1) >> 3) == iota((16, 128), 0)
    l0, l1 = iota((128, 128), 0), iota((128, 128), 1)
    widen = jnp.where((l0 & 7) == (l1 >> 4), 1.0, 0.0).astype(BF16)
    total = parts[0]
    for d in range(1, 16):
        total = total + parts[d]
    terms = []
    for block in range(2):
        decoded = jnp.broadcast_to(total[block : block + 1, :], (16, 128))
        decoded = jnp.where(keep, decoded, 0.0).astype(BF16)
        terms.append(dot(up[...], dot(decoded, widen).astype(BF16)))
    chunks, _, count = held.shape[:3]

    def copy(i):
        return pltpu.make_async_copy(
            held.at[i], out.at[:, i * count : (i + 1) * count], sems.at[i]
        )

    for i in range(chunks):
        for x in range(0, count, 2):
            at = i * count + x
            if at < ahead.shape[0]:
                skips = ahead[at], ahead[at + 1]
            else:
                skips = skip_planes(matrix, (left, right)[at // half], at % half)
            for h in range(2):
                value = (skips[h] + terms[at // POOL]).astype(BF16)
                held[i, :, x + h] = value.reshape(16, 16, 128)
        copy(i).start()
    for i in range(chunks):
        copy(i).wait()


def join(left, right, ahead, matrix, up, parts):
    size_x = 2 * left.shape[0]
    step = 4
    return pl.pallas_call(
        join_kernel,
        in_specs=[VMEM] * 6,
        out_specs=pl.BlockSpec(memory_space=pltpu.HBM),
        out_shape=shape(16, size_x, 16, 128),
        scratch_shapes=[
            pltpu.VMEM((size_x // step, 16, step, 16, 128), BF16),
            pltpu.SemaphoreType.DMA((size_x // step,)),
        ],
        compiler_params=pltpu.CompilerParams(vmem_limit_bytes=LIMIT),
        cost_estimate=pl.CostEstimate(
            flops=2 * 256 * 256 * 128 * size_x, bytes_accessed=4 << 20, transcendentals=0
        ),
    )(left, right, ahead, matrix, up, parts)


def local(features, w_first, w_second, w_lift, w_coarse, w_decode, w_joining):
    size_x = features.shape[1]
    nx, ny = lax.axis_size("gx"), lax.axis_size("gy")
    gy = lax.axis_index("gy")

    def ring(count, step):
        return [(i, (i + step) % count) for i in range(count)]

    def swap(count, odd):
        return [(i, (((i + odd) ^ 1) - odd) % count) for i in range(count)]

    gy_a, gy_b = vmem_call(
        rows_kernel,
        [shape(size_x, 32, 128), shape(size_x, 32, 128)],
        (features,),
        scratch=[pltpu.VMEM(features.shape, BF16), pltpu.SemaphoreType.DMA((1,))],
        far=(0,),
        flops=2 * 64 * 256 * 128 * size_x,
        nbytes=3 << 20,
    )
    gy_a = lax.ppermute(gy_a, "gy", swap(ny, 0))
    gy_b = lax.ppermute(gy_b, "gy", swap(ny, 1))

    w_fine = jnp.concatenate([w_first, w_second], axis=0).reshape(864, 16)
    near, rest = size_x // 2 - 2, size_x // 2
    low, high, rims, faces, t1, t2 = vmem_call(
        interior_kernel,
        [
            shape(near, 224, 128),
            shape(rest, 224, 128),
            shape(2, size_x, 32, 128),
            shape(2, 2, 256, 128),
            shape(192, 256),
            shape(192, 256),
        ],
        (features, w_fine),
        scratch=[
            pltpu.VMEM((size_x, 256, 128), BF16),
            pltpu.VMEM(features.shape, BF16),
            pltpu.VMEM((rest, 224, 128), BF16),
            pltpu.SemaphoreType.DMA((1,)),
            pltpu.SemaphoreType.DMA((2,)),
        ],
        far=(0,),
        far_out=(1,),
        flops=2 * 192 * 256 * 256 * 70,
        nbytes=4 << 20,
    )
    rim_rows, send_a, send_b = vmem_call(
        rim_kernel,
        [shape(size_x - 2, 64, 128), shape(2, 320, 128), shape(2, 320, 128)],
        (rims, faces, gy_a, gy_b, t1),
        scratch=[pltpu.VMEM((2, size_x, 32, 128), BF16)],
        flops=2 * 192 * 256 * 256 * 15,
        nbytes=1 << 20,
    )
    got_a = lax.ppermute(send_a, "gx", swap(nx, 0))
    got_b = lax.ppermute(send_b, "gx", swap(nx, 1))
    second, f1_ends, psum = vmem_call(
        middle_kernel,
        [shape(size_x - 4, 256, 128), shape(4, 288, 128), shape(2, 16, 128, dtype=F32)],
        (low, high, rim_rows, t2),
        scratch=[pltpu.VMEM((rest, 224, 128), BF16), pltpu.SemaphoreType.DMA],
        far=(1,),
        flops=2 * 192 * 256 * 256 * 56,
        nbytes=6 << 20,
    )
    half = shape(size_x // 2, 256, 128)
    *seconds, pooled = vmem_call(
        edge_kernel,
        [half, half, shape(16, 2, 128, dtype=F32)],
        (second, f1_ends, send_a, send_b, got_a, got_b, psum, t1, t2),
        scratch=[
            pltpu.VMEM((2, 4, 320, 128), BF16),
            pltpu.VMEM((2, 2, 288, 128), BF16),
        ],
        flops=2 * 192 * 256 * 256 * 17,
        nbytes=1 << 20,
    )

    count = w_coarse.shape[0]
    w_rows = jnp.transpose(w_coarse, (1, 0, 2)).reshape(27 * count, w_coarse.shape[2])
    w_dec = lax.dynamic_slice_in_dim(w_decode, gy * count, count, axis=1)
    w_lift = jnp.flip(w_lift, axis=1)
    own = lax.all_to_all(pooled, "gy", 0, 0)
    w_rows = vmem_call(
        load_kernel,
        shape(*w_rows.shape),
        (w_rows, pooled),
        scratch=[pltpu.SemaphoreType.DMA],
        far=(0,),
        flops=1 << 28,
        nbytes=4 << 20,
    )
    gl = lax.ppermute(own[:, 1, :], "gx", ring(nx, 1))
    gr = lax.ppermute(own[:, 0, :], "gx", ring(nx, -1))
    mine = vmem_call(
        own_kernel,
        shape(2, count, 128, dtype=F32),
        (own, w_lift, w_rows),
        flops=2 * 864 * 512 * 512,
        nbytes=2 << 20,
    )
    parts = vmem_call(
        beside_kernel,
        shape(16, 2, 128, dtype=F32),
        (mine, gl, gr, w_lift, w_rows, w_dec),
        flops=2 * 864 * 512 * 256,
        nbytes=2 << 20,
    )
    parts = lax.all_to_all(parts, "gy", 0, 0)
    matrix, up, ahead = vmem_call(
        skip_kernel,
        [shape(256, 256), shape(256, 16), shape(4, 256, 128, dtype=F32)],
        (seconds[0], w_joining),
        flops=2 * 256 * 256 * 128 * 8,
        nbytes=2 << 20,
    )
    return join(*seconds, ahead, matrix, up, parts)


def solution(mesh):
    in_specs = (P(None, "gx", "gy", None), P(), P(), P(), P("gy", None, None), P(), P())
    out_specs = P(None, "gx", "gy", None)
    return jax.shard_map(local, mesh=mesh, in_specs=in_specs, out_specs=out_specs, check_vma=False)
```

```python
import jax
import jax.numpy as jnp
from jax import lax
from jax.experimental import pallas as pl
from jax.experimental.pallas import tpu as pltpu
from jax.sharding import PartitionSpec as P

POOL = 16
F32 = jnp.float32
BF16 = jnp.bfloat16
VMEM = pl.BlockSpec(memory_space=pltpu.VMEM)
LIMIT = 12 << 20


def iota(shape, dim):
    return lax.broadcasted_iota(jnp.int32, shape, dim)


def dot(a, b):
    return jnp.dot(a, b, preferred_element_type=F32)


def shape(*dims, dtype=BF16):
    return jax.ShapeDtypeStruct(dims, dtype)


def vmem_call(kernel, out_shape, args, scratch=(), flops=0, nbytes=0, far=(), far_out=()):
    args = [
        pltpu.with_memory_space_constraint(arg, pltpu.HBM) if i in far else arg
        for i, arg in enumerate(args)
    ]
    single = not isinstance(out_shape, (list, tuple))
    if far_out:
        out_shape = [
            pltpu.HBM(out.shape, out.dtype) if i in far_out else out
            for i, out in enumerate(out_shape)
        ]
    return pl.pallas_call(
        kernel,
        out_shape=out_shape,
        in_specs=[
            pl.BlockSpec(memory_space=pltpu.HBM) if i in far else VMEM for i in range(len(args))
        ],
        out_specs=(
            VMEM
            if single
            else [
                pl.BlockSpec(memory_space=pltpu.HBM) if i in far_out else VMEM
                for i in range(len(out_shape))
            ]
        ),
        scratch_shapes=list(scratch),
        compiler_params=pltpu.CompilerParams(vmem_limit_bytes=LIMIT),
        cost_estimate=pl.CostEstimate(flops=flops, bytes_accessed=nbytes, transcendentals=0),
    )(*args)


def side_flags(axis):
    at, count = lax.axis_index(axis), lax.axis_size(axis)
    even = lax.rem(at, 2) == 0

    def number(flag):
        return jnp.where(flag, 1.0, 0.0).astype(F32)

    inner_left, inner_right = at > 0, at < count - 1
    left = number(jnp.logical_not(even)), number(jnp.logical_and(even, inner_left))
    right = number(even), number(jnp.logical_and(jnp.logical_not(even), inner_right))
    return left, right


def mix(a, b, flags):
    return (a.astype(F32) * flags[0] + b.astype(F32) * flags[1]).astype(BF16)


def scaled(v, m):
    return (v.astype(F32) * m).astype(BF16)


def is_even(axis):
    return jnp.where(lax.rem(lax.axis_index(axis), 2) == 0, 1, 0)


def fetch_planes(far, feat, sems):
    parts = sems.shape[0]
    count = far.shape[1] // parts
    fetches = [
        pltpu.make_async_copy(
            far.at[:, i * count : (i + 1) * count],
            feat.at[:, i * count : (i + 1) * count],
            sems.at[i],
        )
        for i in range(parts)
    ]
    for fetch in fetches:
        fetch.start()
    return fetches, count


def rows_kernel(far, gy_a, gy_b, feat, sems):
    fetches, count = fetch_planes(far, feat, sems)
    size_x = feat.shape[1]
    even = is_even("gy")
    row, col = iota((64, 256), 0), iota((64, 256), 1)
    upper = jnp.where(row < 32, even, 1 - even)
    match = ((row & 15) == (col >> 4)) & ((col & 15) == ((row >> 4) & 1) + 14 * upper)
    select = jnp.where(match, 1.0, 0.0).astype(BF16)
    for x in range(0, size_x, 2):
        if x % count == 0:
            fetches[x // count].wait()
        both = jnp.concatenate(
            [feat[:, x].reshape(256, 128), feat[:, x + 1].reshape(256, 128)], axis=1
        )
        rows = dot(select, both).astype(BF16)
        for h in range(2):
            gy_a[x + h] = rows[0:32, 128 * h : 128 * h + 128]
            gy_b[x + h] = rows[32:64, 128 * h : 128 * h + 128]


def swap_rows(feat, planes):
    row, col = iota((256, 256), 0), iota((256, 256), 1)
    match = ((row >> 4) == (col & 15)) & ((row & 15) == (col >> 4))
    swap = jnp.where(match, 1.0, 0.0).astype(BF16)
    for x in range(0, feat.shape[1], 2):
        both = jnp.concatenate(
            [feat[:, x].reshape(256, 128), feat[:, x + 1].reshape(256, 128)], axis=1
        )
        moved = dot(swap, both).astype(BF16)
        planes[x] = moved[:, :128]
        planes[x + 1] = moved[:, 128:]


def band(w, t_ref):
    copies = jnp.where((iota((16, 256), 1) & 15) == iota((16, 256), 0), 1.0, 0.0).astype(BF16)
    wide = dot(w, copies)
    group = iota((16, 256), 1) >> 4
    for c in range(3):
        for x in range(2):
            for y in range(2):
                total = jnp.zeros((16, 256), F32)
                for a in range(3):
                    for b in range(3):
                        k = 9 * a + 3 * b + c
                        here = group == 4 * (x + a) + y + b
                        total = jnp.where(here, wide[16 * k : 16 * k + 16], total)
                at = 16 * (4 * c + 2 * x + y)
                t_ref[at : at + 16, :] = total.astype(BF16)


def shifted_sum(acc, rows, half):
    lanes = slice(half * 128, half * 128 + 128)
    lane = iota((rows, 128), 1)
    before = pltpu.roll(acc[0:rows, lanes], 1, 1)
    after = pltpu.roll(acc[2 * rows : 3 * rows, lanes], 127, 1)
    total = acc[rows : 2 * rows, lanes]
    total = total + jnp.where(lane > 0, before, 0.0)
    total = total + jnp.where(lane < 127, after, 0.0)
    return jnp.maximum(total, 0.0)


def window(rows_of):
    return jnp.concatenate([rows_of(x) for x in range(4)], axis=0)


def conv_pair(t, first, second):
    acc = dot(t[...], jnp.concatenate([first, second], axis=1))
    return shifted_sum(acc, 64, 0), shifted_sum(acc, 64, 1)


def plane_of(parts, x):
    count = parts[0].shape[0]
    return (parts[0], x) if x < count else (parts[1], x - count)


def interior_kernel(far, w, low, high_far, rims, faces, t1, t2, planes, feat, high, sems, puts):
    fetches, _ = fetch_planes(far, feat, sems)
    size_x = planes.shape[0]
    band(w[0:432, :], t1)
    band(w[432:864, :], t2)
    for fetch in fetches:
        fetch.wait()
    swap_rows(feat, planes)
    rims[0] = planes[:, 0:32]
    rims[1] = planes[:, 224:256]
    faces[0] = planes[0:2]
    faces[1] = planes[size_x - 2 : size_x]

    def piece(at, j):
        return window(lambda x: planes[at + x, 32 * j : 32 * j + 64])

    def store(at, j, value):
        for x in range(2):
            to, index = plane_of((low, high), at + x)
            to[index, 32 * j : 32 * j + 32] = value[32 * x : 32 * x + 32].astype(BF16)

    half = high.shape[0] // 2

    def put(i):
        span = pl.ds(i * half, half)
        return pltpu.make_async_copy(high.at[span], high_far.at[span], puts.at[i])

    at = size_x - 4
    for pair in ((0, 1), (2, 3), (4, 5), (5, 6)):
        for j, value in zip(pair, conv_pair(t1, piece(at, pair[0]), piece(at, pair[1]))):
            store(at, j, value)
    for at in range(size_x - 8, -1, -4):
        for j in range(7):
            for h, value in enumerate(conv_pair(t1, piece(at, j), piece(at + 2, j))):
                store(at + 2 * h, j, value)
        start = low.shape[0]
        for i in (1, 0):
            if at <= start + i * half < at + 4:
                put(i).start()
    for i in range(2):
        put(i).wait()


def face_kernel(faces, gy_a, gy_b, send_a, send_b):
    last = gy_a.shape[0] - 2
    left, right = side_flags("gy")
    even = is_even("gx")
    for send, side in ((send_a, even), (send_b, 1 - even)):
        for j in range(2):
            x = side * last + j
            send[j, 0:32] = mix(gy_a[x], gy_b[x], left)
            send[j, 32:288] = faces[side, j]
            send[j, 288:320] = mix(gy_a[x], gy_b[x], right)


def rim_rows_of(rims, gy_a, gy_b, t1, rim_rows, halo):
    size_x = rims.shape[1]
    left, right = side_flags("gy")
    y_left, y_right = left[0] + left[1], right[0] + right[1]
    for x in range(size_x):
        halo[0, x] = mix(gy_a[x], gy_b[x], left)
        halo[1, x] = mix(gy_a[x], gy_b[x], right)
    for at in range(0, size_x - 2, 2):
        low = window(lambda x: jnp.concatenate([halo[0, at + x], rims[0, at + x]], axis=0))
        high = window(lambda x: jnp.concatenate([rims[1, at + x], halo[1, at + x]], axis=0))
        low, high = conv_pair(t1, low, high)
        for x in range(2):
            cut = slice(32 * x, 32 * x + 16), slice(32 * x + 16, 32 * x + 32)
            rim_rows[at + x, 0:16] = (low[cut[0]] * y_left).astype(BF16)
            rim_rows[at + x, 16:32] = low[cut[1]].astype(BF16)
            rim_rows[at + x, 32:48] = high[cut[0]].astype(BF16)
            rim_rows[at + x, 48:64] = (high[cut[1]] * y_right).astype(BF16)


def fold_rows(value):
    return jnp.sum(value.astype(F32).reshape(4, 16, 128), axis=0)


def middle_kernel(
    low, high_far, rims, gy_a, gy_b, t1, t2, second, f1_ends, psum, high, rim_rows, halo, sem
):
    fetch = pltpu.make_async_copy(high_far, high, sem)
    fetch.start()
    rim_rows_of(rims, gy_a, gy_b, t1, rim_rows, halo)
    size_x = low.shape[0] + high.shape[0] + 2

    def rows(x, j):
        inner, at = plane_of((low, high), x)
        if j == 0:
            return jnp.concatenate([rim_rows[x, 0:32], inner[at, 0:32]], axis=0)
        if j == 7:
            return jnp.concatenate([inner[at, 192:224], rim_rows[x, 32:64]], axis=0)
        return inner[at, 32 * j - 32 : 32 * j + 32]

    sums = [jnp.zeros((16, 128), F32) for _ in range(2)]
    for at in range(0, size_x - 4, 2):
        if at + 2 == low.shape[0]:
            fetch.wait()

        def piece(j):
            return window(lambda x: rows(at + x, j))

        for j in range(0, 8, 2):
            for h, value in enumerate(conv_pair(t2, piece(j), piece(j + 1))):
                value = value.astype(BF16)
                row = 32 * (j + h)
                for x in range(2):
                    second[at + x, row : row + 32] = value[32 * x : 32 * x + 32]
                sums[(at + 2) // POOL] += fold_rows(value)
    psum[0], psum[1] = sums
    for i, x in enumerate((0, 1, size_x - 4, size_x - 3)):
        inner, at = plane_of((low, high), x)
        f1_ends[i, 0:32] = rim_rows[x, 0:32]
        f1_ends[i, 32:256] = inner[at]
        f1_ends[i, 256:288] = rim_rows[x, 32:64]


def edge_kernel(
    inner, f1_ends, send_a, send_b, got_a, got_b, psum_in, t1, t2, left_out, right_out,
    pooled, fe, fx,
):
    half = left_out.shape[0]
    size_x = 2 * half
    moved = iter(range(size_x - 4))

    def put(x, rows, value):
        if x < half:
            left_out[x, rows] = value
        else:
            right_out[x - half, rows] = value

    def carry_over():
        for at in (next(moved, None), next(moved, None)):
            if at is not None:
                put(at + 2, slice(0, 256), inner[at])

    x_left, x_right = side_flags("gx")
    y_left, y_right = side_flags("gy")
    y_left, y_right = y_left[0] + y_left[1], y_right[0] + y_right[1]
    even = is_even("gx").astype(F32)
    for j in range(2):
        fe[0, j] = mix(got_a[j], got_b[j], x_left)
        fe[0, 2 + j] = mix(send_a[j], send_b[j], (1.0 - even, even))
        fe[1, j] = mix(send_a[j], send_b[j], (even, 1.0 - even))
        fe[1, 2 + j] = mix(got_a[j], got_b[j], x_right)
    keeps = ((x_left[0] + x_left[1], 1.0), (1.0, x_right[0] + x_right[1]))
    for j in range(9):
        carry_over()
        pieces = [window(lambda x: fe[s, x, 32 * j : 32 * j + 64]) for s in range(2)]
        for s, value in enumerate(conv_pair(t1, *pieces)):
            for x in range(2):
                for y in range(2):
                    part = value[32 * x + 16 * y : 32 * x + 16 * y + 16] * keeps[s][x]
                    if j == 0 and y == 0:
                        part = part * y_left
                    if j == 8 and y == 1:
                        part = part * y_right
                    row = 32 * j + 16 * y
                    fx[s, x, row : row + 16] = part.astype(BF16)

    def left(j):
        cut = slice(32 * j, 32 * j + 64)
        return window(lambda x: fx[0, x, cut] if x < 2 else f1_ends[x - 2, cut])

    def right(j):
        cut = slice(32 * j, 32 * j + 64)
        return window(lambda x: f1_ends[2 + x, cut] if x < 2 else fx[1, x - 2, cut])

    sums = [psum_in[0], psum_in[1]]
    for j in range(8):
        carry_over()
        for s, value in enumerate(conv_pair(t2, left(j), right(j))):
            value = value.astype(BF16)
            for x in range(2):
                cut = slice(32 * j, 32 * j + 32)
                put(s * (size_x - 2) + x, cut, value[32 * x : 32 * x + 32])
            sums[s] = sums[s] + fold_rows(value)

    z, lane = iota((128, 128), 0), iota((128, 128), 1)
    gather = jnp.where((z >> 4) == (lane & 7), 1.0, 0.0).astype(F32)
    keep = (iota((16, 128), 1) >> 3) == iota((16, 128), 0)
    results = []
    for s in range(2):
        cells = jnp.dot(
            sums[s], gather, preferred_element_type=F32, precision=lax.Precision.HIGHEST
        )
        row = jnp.sum(jnp.where(keep, cells, 0.0), axis=0, keepdims=True) * (1.0 / POOL**3)
        results.append(row)
    both = jnp.concatenate(results, axis=0)
    for d in range(16):
        pooled[d] = both


def split3(v):
    a = v.astype(BF16)
    v = v - a.astype(F32)
    b = v.astype(BF16)
    c = (v - b.astype(F32)).astype(BF16)
    return [a, b, c]


def swap_groups(rows):
    lane = iota((16, 128), 1) >> 3
    total = jnp.zeros((16, 128), F32)
    rows = pltpu.roll(pltpu.roll(rows, 0, 1, stride=8, stride_axis=0), 8, 1)
    for s in range(16):
        spread = jnp.broadcast_to(rows[s : s + 1, :], (16, 128))
        moved = pltpu.roll(spread, 0, 1, stride=8, stride_axis=0)
        total = jnp.where(lane == s, moved, total)
    return total


def load_kernel(far, after, out, sem):
    fetch = pltpu.make_async_copy(far, out, sem)
    fetch.start()
    fetch.wait()


def lift_slabs(slabs, w_lift):
    columns = []
    for slab in slabs:
        columns.append(jnp.concatenate(split3(swap_groups(slab)), axis=0))
    stacked = jnp.concatenate(columns, axis=1)
    lift3 = jnp.concatenate([w_lift] * 3, axis=1)
    return jnp.maximum(dot(lift3, stacked), 0.0).astype(BF16)


def taps(partial, count):
    lane = iota((count, 128), 1)
    y, z = lane >> 3, lane & 7
    total = jnp.zeros((count, 128), F32)
    for k in range(9):
        b, c = k // 3 - 1, k % 3 - 1
        piece = partial[k * count : (k + 1) * count, :]
        step = 8 * b + c
        if step:
            piece = pltpu.roll(piece, (-step) % 128, 1)
        good = None
        if b:
            good = (y < 15) if b > 0 else (y > 0)
        if c:
            inside = (z < 7) if c > 0 else (z > 0)
            good = inside if good is None else good & inside
        total = total + (piece if good is None else jnp.where(good, piece, 0.0))
    return total


def own_kernel(own, w_lift, w_coarse, out):
    count = w_coarse.shape[0] // 27
    lifted = lift_slabs([own[:, 0, :], own[:, 1, :]], w_lift[...])
    partial = dot(w_coarse[...], lifted)
    for x in range(2):
        total = jnp.zeros((count, 128), F32)
        for slab in range(2):
            a = slab - x + 1
            piece = partial[9 * a * count : 9 * (a + 1) * count, slab * 128 : slab * 128 + 128]
            total = total + taps(piece, count)
        out[x] = total


def beside_kernel(mine, gl, gr, w_lift, w_coarse, w_dec, out):
    count = w_coarse.shape[0] // 27
    at, last = lax.axis_index("gx"), lax.axis_size("gx") - 1
    m_left = jnp.where(at > 0, 1.0, 0.0).astype(F32)
    m_right = jnp.where(at < last, 1.0, 0.0).astype(F32)
    lifted = lift_slabs([gl[...] * m_left, gr[...] * m_right], w_lift[...])
    for x in range(2):
        a = 2 * x
        rows = w_coarse[9 * a * count : 9 * (a + 1) * count, :]
        total = mine[x] + taps(dot(rows, lifted[:, x * 128 : x * 128 + 128]), count)
        coarse = jnp.maximum(total, 0.0).astype(BF16)
        rows = swap_groups(dot(w_dec[...], coarse))
        for y in range(16):
            out[y, x : x + 1, :] = rows[15 - y : 16 - y, :]


def skip_planes(matrix, second, at):
    both = jnp.concatenate([second[at], second[at + 1]], axis=1)
    result = dot(matrix[...], both)
    return result[:, :128], result[:, 128:]


def skip_kernel(second, w_join, matrix, up, ahead):
    r, c = iota((256, 16), 0), iota((256, 16), 1)
    rows = jnp.where((r >> 4) == c, 1.0, 0.0).astype(BF16)
    mixed = dot(rows, w_join[...]).astype(BF16)
    up[...] = mixed[:, 16:32]
    r, c = iota((16, 256), 0), iota((16, 256), 1)
    cols = jnp.where((c & 15) == r, 1.0, 0.0).astype(BF16)
    r, c = iota((256, 256), 0), iota((256, 256), 1)
    match = (r & 15) == (c >> 4)
    matrix[...] = jnp.where(match, dot(mixed[:, 0:16], cols), 0.0).astype(BF16)
    for at in range(0, ahead.shape[0], 2):
        ahead[at], ahead[at + 1] = skip_planes(matrix, second, at)


def join_kernel(left, right, ahead, matrix, up, parts, out, held, sems):
    half = left.shape[0]
    keep = (iota((16, 128), 1) >> 3) == iota((16, 128), 0)
    l0, l1 = iota((128, 128), 0), iota((128, 128), 1)
    widen = jnp.where((l0 & 7) == (l1 >> 4), 1.0, 0.0).astype(BF16)
    total = parts[0]
    for d in range(1, 16):
        total = total + parts[d]
    terms = []
    for block in range(2):
        decoded = jnp.broadcast_to(total[block : block + 1, :], (16, 128))
        decoded = jnp.where(keep, decoded, 0.0).astype(BF16)
        terms.append(dot(up[...], dot(decoded, widen).astype(BF16)))
    chunks, _, count = held.shape[:3]

    def copy(i):
        return pltpu.make_async_copy(
            held.at[i], out.at[:, i * count : (i + 1) * count], sems.at[i]
        )

    for i in range(chunks):
        for x in range(0, count, 2):
            at = i * count + x
            if at < ahead.shape[0]:
                skips = ahead[at], ahead[at + 1]
            else:
                skips = skip_planes(matrix, (left, right)[at // half], at % half)
            for h in range(2):
                value = (skips[h] + terms[at // POOL]).astype(BF16)
                held[i, :, x + h] = value.reshape(16, 16, 128)
        copy(i).start()
    for i in range(chunks):
        copy(i).wait()


def join(left, right, ahead, matrix, up, parts):
    size_x = 2 * left.shape[0]
    step = 4
    return pl.pallas_call(
        join_kernel,
        in_specs=[VMEM] * 6,
        out_specs=pl.BlockSpec(memory_space=pltpu.HBM),
        out_shape=shape(16, size_x, 16, 128),
        scratch_shapes=[
            pltpu.VMEM((size_x // step, 16, step, 16, 128), BF16),
            pltpu.SemaphoreType.DMA((size_x // step,)),
        ],
        compiler_params=pltpu.CompilerParams(vmem_limit_bytes=LIMIT),
        cost_estimate=pl.CostEstimate(
            flops=2 * 256 * 256 * 128 * size_x, bytes_accessed=4 << 20, transcendentals=0
        ),
    )(left, right, ahead, matrix, up, parts)


def local(features, w_first, w_second, w_lift, w_coarse, w_decode, w_joining):
    size_x = features.shape[1]
    nx, ny = lax.axis_size("gx"), lax.axis_size("gy")
    gy = lax.axis_index("gy")

    def ring(count, step):
        return [(i, (i + step) % count) for i in range(count)]

    def swap(count, odd):
        return [(i, (((i + odd) ^ 1) - odd) % count) for i in range(count)]

    gy_a, gy_b = vmem_call(
        rows_kernel,
        [shape(size_x, 32, 128), shape(size_x, 32, 128)],
        (features,),
        scratch=[pltpu.VMEM(features.shape, BF16), pltpu.SemaphoreType.DMA((1,))],
        far=(0,),
        flops=2 * 64 * 256 * 128 * size_x,
        nbytes=3 << 20,
    )
    gy_a = lax.ppermute(gy_a, "gy", swap(ny, 0))
    gy_b = lax.ppermute(gy_b, "gy", swap(ny, 1))

    w_fine = jnp.concatenate([w_first, w_second], axis=0).reshape(864, 16)
    near, rest = size_x // 2 - 2, size_x // 2
    low, high, rims, faces, t1, t2 = vmem_call(
        interior_kernel,
        [
            shape(near, 224, 128),
            shape(rest, 224, 128),
            shape(2, size_x, 32, 128),
            shape(2, 2, 256, 128),
            shape(192, 256),
            shape(192, 256),
        ],
        (features, w_fine),
        scratch=[
            pltpu.VMEM((size_x, 256, 128), BF16),
            pltpu.VMEM(features.shape, BF16),
            pltpu.VMEM((rest, 224, 128), BF16),
            pltpu.SemaphoreType.DMA((1,)),
            pltpu.SemaphoreType.DMA((2,)),
        ],
        far=(0,),
        far_out=(1,),
        flops=2 * 192 * 256 * 256 * 70,
        nbytes=4 << 20,
    )
    send_a, send_b = vmem_call(
        face_kernel,
        [shape(2, 320, 128), shape(2, 320, 128)],
        (faces, gy_a, gy_b),
        nbytes=1 << 19,
    )
    got_a = lax.ppermute(send_a, "gx", swap(nx, 0))
    got_b = lax.ppermute(send_b, "gx", swap(nx, 1))
    second, f1_ends, psum = vmem_call(
        middle_kernel,
        [shape(size_x - 4, 256, 128), shape(4, 288, 128), shape(2, 16, 128, dtype=F32)],
        (low, high, rims, gy_a, gy_b, t1, t2),
        scratch=[
            pltpu.VMEM((rest, 224, 128), BF16),
            pltpu.VMEM((size_x - 2, 64, 128), BF16),
            pltpu.VMEM((2, size_x, 32, 128), BF16),
            pltpu.SemaphoreType.DMA,
        ],
        far=(1,),
        flops=2 * 192 * 256 * 256 * 71,
        nbytes=6 << 20,
    )
    half = shape(size_x // 2, 256, 128)
    *seconds, pooled = vmem_call(
        edge_kernel,
        [half, half, shape(16, 2, 128, dtype=F32)],
        (second, f1_ends, send_a, send_b, got_a, got_b, psum, t1, t2),
        scratch=[
            pltpu.VMEM((2, 4, 320, 128), BF16),
            pltpu.VMEM((2, 2, 288, 128), BF16),
        ],
        flops=2 * 192 * 256 * 256 * 17,
        nbytes=1 << 20,
    )

    count = w_coarse.shape[0]
    w_rows = jnp.transpose(w_coarse, (1, 0, 2)).reshape(27 * count, w_coarse.shape[2])
    w_dec = lax.dynamic_slice_in_dim(w_decode, gy * count, count, axis=1)
    w_lift = jnp.flip(w_lift, axis=1)
    own = lax.all_to_all(pooled, "gy", 0, 0)
    w_rows = vmem_call(
        load_kernel,
        shape(*w_rows.shape),
        (w_rows, pooled),
        scratch=[pltpu.SemaphoreType.DMA],
        far=(0,),
        flops=1 << 28,
        nbytes=4 << 20,
    )
    gl = lax.ppermute(own[:, 1, :], "gx", ring(nx, 1))
    gr = lax.ppermute(own[:, 0, :], "gx", ring(nx, -1))
    mine = vmem_call(
        own_kernel,
        shape(2, count, 128, dtype=F32),
        (own, w_lift, w_rows),
        flops=2 * 864 * 512 * 512,
        nbytes=2 << 20,
    )
    parts = vmem_call(
        beside_kernel,
        shape(16, 2, 128, dtype=F32),
        (mine, gl, gr, w_lift, w_rows, w_dec),
        flops=2 * 864 * 512 * 256,
        nbytes=2 << 20,
    )
    parts = lax.all_to_all(parts, "gy", 0, 0)
    matrix, up, ahead = vmem_call(
        skip_kernel,
        [shape(256, 256), shape(256, 16), shape(4, 256, 128, dtype=F32)],
        (seconds[0], w_joining),
        flops=2 * 256 * 256 * 128 * 8,
        nbytes=2 << 20,
    )
    return join(*seconds, ahead, matrix, up, parts)


def solution(mesh):
    in_specs = (P(None, "gx", "gy", None), P(), P(), P(), P("gy", None, None), P(), P())
    out_specs = P(None, "gx", "gy", None)
    return jax.shard_map(local, mesh=mesh, in_specs=in_specs, out_specs=out_specs, check_vma=False)
```

```python
import jax
import jax.numpy as jnp
from jax import lax
from jax.experimental import pallas as pl
from jax.experimental.pallas import tpu as pltpu
from jax.sharding import PartitionSpec as P

POOL = 16
F32 = jnp.float32
BF16 = jnp.bfloat16
VMEM = pl.BlockSpec(memory_space=pltpu.VMEM)
LIMIT = 12 << 20


def iota(shape, dim):
    return lax.broadcasted_iota(jnp.int32, shape, dim)


def dot(a, b):
    return jnp.dot(a, b, preferred_element_type=F32)


def shape(*dims, dtype=BF16):
    return jax.ShapeDtypeStruct(dims, dtype)


def vmem_call(kernel, out_shape, args, scratch=(), flops=0, nbytes=0, far=(), far_out=()):
    args = [
        pltpu.with_memory_space_constraint(arg, pltpu.HBM) if i in far else arg
        for i, arg in enumerate(args)
    ]
    single = not isinstance(out_shape, (list, tuple))
    if far_out:
        out_shape = [
            pltpu.HBM(out.shape, out.dtype) if i in far_out else out
            for i, out in enumerate(out_shape)
        ]
    return pl.pallas_call(
        kernel,
        out_shape=out_shape,
        in_specs=[
            pl.BlockSpec(memory_space=pltpu.HBM) if i in far else VMEM for i in range(len(args))
        ],
        out_specs=(
            VMEM
            if single
            else [
                pl.BlockSpec(memory_space=pltpu.HBM) if i in far_out else VMEM
                for i in range(len(out_shape))
            ]
        ),
        scratch_shapes=list(scratch),
        compiler_params=pltpu.CompilerParams(vmem_limit_bytes=LIMIT),
        cost_estimate=pl.CostEstimate(flops=flops, bytes_accessed=nbytes, transcendentals=0),
    )(*args)


def side_flags(axis):
    at, count = lax.axis_index(axis), lax.axis_size(axis)
    even = lax.rem(at, 2) == 0

    def number(flag):
        return jnp.where(flag, 1.0, 0.0).astype(F32)

    inner_left, inner_right = at > 0, at < count - 1
    left = number(jnp.logical_not(even)), number(jnp.logical_and(even, inner_left))
    right = number(even), number(jnp.logical_and(jnp.logical_not(even), inner_right))
    return left, right


def mix(a, b, flags):
    return (a.astype(F32) * flags[0] + b.astype(F32) * flags[1]).astype(BF16)


def scaled(v, m):
    return (v.astype(F32) * m).astype(BF16)


def is_even(axis):
    return jnp.where(lax.rem(lax.axis_index(axis), 2) == 0, 1, 0)


def fetch_planes(far, feat, sems):
    parts = sems.shape[0]
    count = far.shape[1] // parts
    fetches = [
        pltpu.make_async_copy(
            far.at[:, i * count : (i + 1) * count],
            feat.at[:, i * count : (i + 1) * count],
            sems.at[i],
        )
        for i in range(parts)
    ]
    for fetch in fetches:
        fetch.start()
    return fetches, count


def rows_kernel(far, gy_a, gy_b, feat, sems):
    fetches, count = fetch_planes(far, feat, sems)
    size_x = feat.shape[1]
    even = is_even("gy")
    row, col = iota((64, 256), 0), iota((64, 256), 1)
    upper = jnp.where(row < 32, even, 1 - even)
    match = ((row & 15) == (col >> 4)) & ((col & 15) == ((row >> 4) & 1) + 14 * upper)
    select = jnp.where(match, 1.0, 0.0).astype(BF16)
    for x in range(0, size_x, 2):
        if x % count == 0:
            fetches[x // count].wait()
        both = jnp.concatenate(
            [feat[:, x].reshape(256, 128), feat[:, x + 1].reshape(256, 128)], axis=1
        )
        rows = dot(select, both).astype(BF16)
        for h in range(2):
            gy_a[x + h] = rows[0:32, 128 * h : 128 * h + 128]
            gy_b[x + h] = rows[32:64, 128 * h : 128 * h + 128]


def swap_rows(feat, planes):
    row, col = iota((256, 256), 0), iota((256, 256), 1)
    match = ((row >> 4) == (col & 15)) & ((row & 15) == (col >> 4))
    swap = jnp.where(match, 1.0, 0.0).astype(BF16)
    for x in range(0, feat.shape[1], 2):
        both = jnp.concatenate(
            [feat[:, x].reshape(256, 128), feat[:, x + 1].reshape(256, 128)], axis=1
        )
        moved = dot(swap, both).astype(BF16)
        planes[x] = moved[:, :128]
        planes[x + 1] = moved[:, 128:]


def band(w, t_ref):
    copies = jnp.where((iota((16, 256), 1) & 15) == iota((16, 256), 0), 1.0, 0.0).astype(BF16)
    wide = dot(w, copies)
    group = iota((16, 256), 1) >> 4
    for c in range(3):
        for x in range(2):
            for y in range(2):
                total = jnp.zeros((16, 256), F32)
                for a in range(3):
                    for b in range(3):
                        k = 9 * a + 3 * b + c
                        here = group == 4 * (x + a) + y + b
                        total = jnp.where(here, wide[16 * k : 16 * k + 16], total)
                at = 16 * (4 * c + 2 * x + y)
                t_ref[at : at + 16, :] = total.astype(BF16)


def shifted_sum(acc, rows, half):
    lanes = slice(half * 128, half * 128 + 128)
    lane = iota((rows, 128), 1)
    before = pltpu.roll(acc[0:rows, lanes], 1, 1)
    after = pltpu.roll(acc[2 * rows : 3 * rows, lanes], 127, 1)
    total = acc[rows : 2 * rows, lanes]
    total = total + jnp.where(lane > 0, before, 0.0)
    total = total + jnp.where(lane < 127, after, 0.0)
    return jnp.maximum(total, 0.0)


def window(rows_of):
    return jnp.concatenate([rows_of(x) for x in range(4)], axis=0)


def conv_pair(t, first, second):
    acc = dot(t[...], jnp.concatenate([first, second], axis=1))
    return shifted_sum(acc, 64, 0), shifted_sum(acc, 64, 1)


def plane_of(parts, x):
    count = parts[0].shape[0]
    return (parts[0], x) if x < count else (parts[1], x - count)


def interior_kernel(far, w, low, high_far, rims, faces, t1, t2, planes, feat, high, sems, puts):
    fetches, _ = fetch_planes(far, feat, sems)
    size_x = planes.shape[0]
    band(w[0:432, :], t1)
    band(w[432:864, :], t2)
    for fetch in fetches:
        fetch.wait()
    swap_rows(feat, planes)
    rims[0] = planes[:, 0:32]
    rims[1] = planes[:, 224:256]
    faces[0] = planes[0:2]
    faces[1] = planes[size_x - 2 : size_x]

    def piece(at, j):
        return window(lambda x: planes[at + x, 32 * j : 32 * j + 64])

    def store(at, j, value):
        for x in range(2):
            to, index = plane_of((low, high), at + x)
            to[index, 32 * j : 32 * j + 32] = value[32 * x : 32 * x + 32].astype(BF16)

    half = high.shape[0] // 2

    def put(i):
        span = pl.ds(i * half, half)
        return pltpu.make_async_copy(high.at[span], high_far.at[span], puts.at[i])

    at = size_x - 4
    for pair in ((0, 1), (2, 3), (4, 5), (5, 6)):
        for j, value in zip(pair, conv_pair(t1, piece(at, pair[0]), piece(at, pair[1]))):
            store(at, j, value)
    for at in range(size_x - 8, -1, -4):
        for j in range(7):
            for h, value in enumerate(conv_pair(t1, piece(at, j), piece(at + 2, j))):
                store(at + 2 * h, j, value)
        start = low.shape[0]
        for i in (1, 0):
            if at <= start + i * half < at + 4:
                put(i).start()
    for i in range(2):
        put(i).wait()


def face_kernel(faces, gy_a, gy_b, send_a, send_b):
    last = gy_a.shape[0] - 2
    left, right = side_flags("gy")
    even = is_even("gx")
    for send, side in ((send_a, even), (send_b, 1 - even)):
        for j in range(2):
            x = side * last + j
            send[j, 0:32] = mix(gy_a[x], gy_b[x], left)
            send[j, 32:288] = faces[side, j]
            send[j, 288:320] = mix(gy_a[x], gy_b[x], right)


def rim_rows_of(rims, gy_a, gy_b, t1, rim_rows, halo):
    size_x = rims.shape[1]
    left, right = side_flags("gy")
    y_left, y_right = left[0] + left[1], right[0] + right[1]
    for x in range(size_x):
        halo[0, x] = mix(gy_a[x], gy_b[x], left)
        halo[1, x] = mix(gy_a[x], gy_b[x], right)
    for at in range(0, size_x - 2, 2):
        low = window(lambda x: jnp.concatenate([halo[0, at + x], rims[0, at + x]], axis=0))
        high = window(lambda x: jnp.concatenate([rims[1, at + x], halo[1, at + x]], axis=0))
        low, high = conv_pair(t1, low, high)
        for x in range(2):
            cut = slice(32 * x, 32 * x + 16), slice(32 * x + 16, 32 * x + 32)
            rim_rows[at + x, 0:16] = (low[cut[0]] * y_left).astype(BF16)
            rim_rows[at + x, 16:32] = low[cut[1]].astype(BF16)
            rim_rows[at + x, 32:48] = high[cut[0]].astype(BF16)
            rim_rows[at + x, 48:64] = (high[cut[1]] * y_right).astype(BF16)


def fold_rows(value):
    return jnp.sum(value.astype(F32).reshape(4, 16, 128), axis=0)


def middle_kernel(
    low, high_far, rims, gy_a, gy_b, t1, t2, second, f1_ends, psum, high, rim_rows, halo, sem
):
    fetch = pltpu.make_async_copy(high_far, high, sem)
    fetch.start()
    rim_rows_of(rims, gy_a, gy_b, t1, rim_rows, halo)
    size_x = low.shape[0] + high.shape[0] + 2

    def rows(x, j):
        inner, at = plane_of((low, high), x)
        if j == 0:
            return jnp.concatenate([rim_rows[x, 0:32], inner[at, 0:32]], axis=0)
        if j == 7:
            return jnp.concatenate([inner[at, 192:224], rim_rows[x, 32:64]], axis=0)
        return inner[at, 32 * j - 32 : 32 * j + 32]

    sums = [jnp.zeros((16, 128), F32) for _ in range(2)]
    for at in range(0, size_x - 4, 2):
        if at + 2 == low.shape[0]:
            fetch.wait()

        def piece(j):
            return window(lambda x: rows(at + x, j))

        for j in range(0, 8, 2):
            for h, value in enumerate(conv_pair(t2, piece(j), piece(j + 1))):
                value = value.astype(BF16)
                row = 32 * (j + h)
                for x in range(2):
                    second[at + x, row : row + 32] = value[32 * x : 32 * x + 32]
                sums[(at + 2) // POOL] += fold_rows(value)
    psum[0], psum[1] = sums
    for i, x in enumerate((0, 1, size_x - 4, size_x - 3)):
        inner, at = plane_of((low, high), x)
        f1_ends[i, 0:32] = rim_rows[x, 0:32]
        f1_ends[i, 32:256] = inner[at]
        f1_ends[i, 256:288] = rim_rows[x, 32:64]


def edge_kernel(
    inner, f1_ends, send_a, send_b, got_a, got_b, psum_in, t1, t2, left_out, right_out,
    pooled, fe, fx,
):
    half = left_out.shape[0]
    size_x = 2 * half
    moved = iter(range(size_x - 4))

    def put(x, rows, value):
        if x < half:
            left_out[x, rows] = value
        else:
            right_out[x - half, rows] = value

    def carry_over():
        for at in (next(moved, None), next(moved, None)):
            if at is not None:
                put(at + 2, slice(0, 256), inner[at])

    x_left, x_right = side_flags("gx")
    y_left, y_right = side_flags("gy")
    y_left, y_right = y_left[0] + y_left[1], y_right[0] + y_right[1]
    even = is_even("gx").astype(F32)
    for j in range(2):
        fe[0, j] = mix(got_a[j], got_b[j], x_left)
        fe[0, 2 + j] = mix(send_a[j], send_b[j], (1.0 - even, even))
        fe[1, j] = mix(send_a[j], send_b[j], (even, 1.0 - even))
        fe[1, 2 + j] = mix(got_a[j], got_b[j], x_right)
    keeps = ((x_left[0] + x_left[1], 1.0), (1.0, x_right[0] + x_right[1]))
    for j in range(9):
        carry_over()
        pieces = [window(lambda x: fe[s, x, 32 * j : 32 * j + 64]) for s in range(2)]
        for s, value in enumerate(conv_pair(t1, *pieces)):
            for x in range(2):
                for y in range(2):
                    part = value[32 * x + 16 * y : 32 * x + 16 * y + 16] * keeps[s][x]
                    if j == 0 and y == 0:
                        part = part * y_left
                    if j == 8 and y == 1:
                        part = part * y_right
                    row = 32 * j + 16 * y
                    fx[s, x, row : row + 16] = part.astype(BF16)

    def left(j):
        cut = slice(32 * j, 32 * j + 64)
        return window(lambda x: fx[0, x, cut] if x < 2 else f1_ends[x - 2, cut])

    def right(j):
        cut = slice(32 * j, 32 * j + 64)
        return window(lambda x: f1_ends[2 + x, cut] if x < 2 else fx[1, x - 2, cut])

    sums = [psum_in[0], psum_in[1]]
    for j in range(8):
        carry_over()
        for s, value in enumerate(conv_pair(t2, left(j), right(j))):
            value = value.astype(BF16)
            for x in range(2):
                cut = slice(32 * j, 32 * j + 32)
                put(s * (size_x - 2) + x, cut, value[32 * x : 32 * x + 32])
            sums[s] = sums[s] + fold_rows(value)

    z, lane = iota((128, 128), 0), iota((128, 128), 1)
    gather = jnp.where((z >> 4) == (lane & 7), 1.0, 0.0).astype(BF16)
    keep = (iota((16, 128), 1) >> 3) == iota((16, 128), 0)
    results = []
    folded = dot(jnp.concatenate(split3(sums[0]) + split3(sums[1]), axis=0), gather)
    for s in range(2):
        first, second, third = (folded[16 * (3 * s + i) : 16 * (3 * s + i) + 16] for i in range(3))
        cells = first + second + third
        row = jnp.sum(jnp.where(keep, cells, 0.0), axis=0, keepdims=True) * (1.0 / POOL**3)
        results.append(row)
    both = jnp.concatenate(results, axis=0)
    for d in range(16):
        pooled[d] = both


def split3(v):
    a = v.astype(BF16)
    v = v - a.astype(F32)
    b = v.astype(BF16)
    c = (v - b.astype(F32)).astype(BF16)
    return [a, b, c]


def swap_groups(rows):
    lane = iota((16, 128), 1) >> 3
    total = jnp.zeros((16, 128), F32)
    rows = pltpu.roll(pltpu.roll(rows, 0, 1, stride=8, stride_axis=0), 8, 1)
    for s in range(16):
        spread = jnp.broadcast_to(rows[s : s + 1, :], (16, 128))
        moved = pltpu.roll(spread, 0, 1, stride=8, stride_axis=0)
        total = jnp.where(lane == s, moved, total)
    return total


def load_kernel(far, w_lift, after, out, lift, sem):
    fetch = pltpu.make_async_copy(far, out, sem)
    fetch.start()
    back = (iota((16, 48), 1) & 15) == 15 - iota((16, 48), 0)
    lift[...] = dot(w_lift[...], jnp.where(back, 1.0, 0.0).astype(BF16)).astype(BF16)
    fetch.wait()


def lift_slabs(slabs, w_lift):
    columns = []
    for slab in slabs:
        columns.append(jnp.concatenate(split3(swap_groups(slab)), axis=0))
    stacked = jnp.concatenate(columns, axis=1)
    return jnp.maximum(dot(w_lift, stacked), 0.0).astype(BF16)


def taps(partial, count):
    lane = iota((count, 128), 1)
    y, z = lane >> 3, lane & 7
    total = jnp.zeros((count, 128), F32)
    for k in range(9):
        b, c = k // 3 - 1, k % 3 - 1
        piece = partial[k * count : (k + 1) * count, :]
        step = 8 * b + c
        if step:
            piece = pltpu.roll(piece, (-step) % 128, 1)
        good = None
        if b:
            good = (y < 15) if b > 0 else (y > 0)
        if c:
            inside = (z < 7) if c > 0 else (z > 0)
            good = inside if good is None else good & inside
        total = total + (piece if good is None else jnp.where(good, piece, 0.0))
    return total


def own_kernel(own, w_lift, w_coarse, out):
    count = w_coarse.shape[0] // 27
    lifted = lift_slabs([own[:, 0, :], own[:, 1, :]], w_lift[...])
    partial = dot(w_coarse[...], lifted)
    for x in range(2):
        total = jnp.zeros((count, 128), F32)
        for slab in range(2):
            a = slab - x + 1
            piece = partial[9 * a * count : 9 * (a + 1) * count, slab * 128 : slab * 128 + 128]
            total = total + taps(piece, count)
        out[x] = total


def beside_kernel(mine, gl, gr, w_lift, w_coarse, w_dec, out):
    count = w_coarse.shape[0] // 27
    at, last = lax.axis_index("gx"), lax.axis_size("gx") - 1
    m_left = jnp.where(at > 0, 1.0, 0.0).astype(F32)
    m_right = jnp.where(at < last, 1.0, 0.0).astype(F32)
    lifted = lift_slabs([gl[...] * m_left, gr[...] * m_right], w_lift[...])
    sums = []
    for x in range(2):
        a = 2 * x
        rows = w_coarse[9 * a * count : 9 * (a + 1) * count, :]
        sums.append(mine[x] + taps(dot(rows, lifted[:, x * 128 : x * 128 + 128]), count))
    coarse = jnp.maximum(jnp.concatenate(sums, axis=1), 0.0).astype(BF16)
    decoded = dot(w_dec[...], coarse)
    for x in range(2):
        rows = swap_groups(decoded[:, x * 128 : x * 128 + 128])
        for y in range(16):
            out[y, x : x + 1, :] = rows[15 - y : 16 - y, :]


def skip_planes(matrix, second, at):
    both = jnp.concatenate([second[at], second[at + 1]], axis=1)
    result = dot(matrix[...], both)
    return result[:, :128], result[:, 128:]


def skip_kernel(second, w_join, matrix, up, ahead):
    r, c = iota((256, 16), 0), iota((256, 16), 1)
    rows = jnp.where((r >> 4) == c, 1.0, 0.0).astype(BF16)
    mixed = dot(rows, w_join[...]).astype(BF16)
    up[...] = mixed[:, 16:32]
    r, c = iota((16, 256), 0), iota((16, 256), 1)
    cols = jnp.where((c & 15) == r, 1.0, 0.0).astype(BF16)
    r, c = iota((256, 256), 0), iota((256, 256), 1)
    match = (r & 15) == (c >> 4)
    matrix[...] = jnp.where(match, dot(mixed[:, 0:16], cols), 0.0).astype(BF16)
    for at in range(0, ahead.shape[0], 2):
        ahead[at], ahead[at + 1] = skip_planes(matrix, second, at)


def join_kernel(left, right, ahead, matrix, up, parts, out, held, sems):
    half = left.shape[0]
    keep = (iota((16, 128), 1) >> 3) == iota((16, 128), 0)
    l0, l1 = iota((128, 128), 0), iota((128, 128), 1)
    widen = jnp.where((l0 & 7) == (l1 >> 4), 1.0, 0.0).astype(BF16)
    total = parts[0]
    for d in range(1, 16):
        total = total + parts[d]
    terms = []
    for block in range(2):
        decoded = jnp.broadcast_to(total[block : block + 1, :], (16, 128))
        decoded = jnp.where(keep, decoded, 0.0).astype(BF16)
        terms.append(dot(up[...], dot(decoded, widen).astype(BF16)))
    chunks, _, count = held.shape[:3]

    def copy(i):
        return pltpu.make_async_copy(
            held.at[i], out.at[:, i * count : (i + 1) * count], sems.at[i]
        )

    for i in range(chunks):
        for x in range(0, count, 2):
            at = i * count + x
            if at < ahead.shape[0]:
                skips = ahead[at], ahead[at + 1]
            else:
                skips = skip_planes(matrix, (left, right)[at // half], at % half)
            for h in range(2):
                value = (skips[h] + terms[at // POOL]).astype(BF16)
                held[i, :, x + h] = value.reshape(16, 16, 128)
        copy(i).start()
    for i in range(chunks):
        copy(i).wait()


def join(left, right, ahead, matrix, up, parts):
    size_x = 2 * left.shape[0]
    step = 4
    return pl.pallas_call(
        join_kernel,
        in_specs=[VMEM] * 6,
        out_specs=pl.BlockSpec(memory_space=pltpu.HBM),
        out_shape=shape(16, size_x, 16, 128),
        scratch_shapes=[
            pltpu.VMEM((size_x // step, 16, step, 16, 128), BF16),
            pltpu.SemaphoreType.DMA((size_x // step,)),
        ],
        compiler_params=pltpu.CompilerParams(vmem_limit_bytes=LIMIT),
        cost_estimate=pl.CostEstimate(
            flops=2 * 256 * 256 * 128 * size_x, bytes_accessed=4 << 20, transcendentals=0
        ),
    )(left, right, ahead, matrix, up, parts)


def local(features, w_first, w_second, w_lift, w_coarse, w_decode, w_joining):
    size_x = features.shape[1]
    nx, ny = lax.axis_size("gx"), lax.axis_size("gy")
    gy = lax.axis_index("gy")

    def ring(count, step):
        return [(i, (i + step) % count) for i in range(count)]

    def swap(count, odd):
        return [(i, (((i + odd) ^ 1) - odd) % count) for i in range(count)]

    gy_a, gy_b = vmem_call(
        rows_kernel,
        [shape(size_x, 32, 128), shape(size_x, 32, 128)],
        (features,),
        scratch=[pltpu.VMEM(features.shape, BF16), pltpu.SemaphoreType.DMA((1,))],
        far=(0,),
        flops=2 * 64 * 256 * 128 * size_x,
        nbytes=3 << 20,
    )
    gy_a = lax.ppermute(gy_a, "gy", swap(ny, 0))
    gy_b = lax.ppermute(gy_b, "gy", swap(ny, 1))

    w_fine = jnp.concatenate([w_first, w_second], axis=0).reshape(864, 16)
    near, rest = size_x // 2 - 2, size_x // 2
    low, high, rims, faces, t1, t2 = vmem_call(
        interior_kernel,
        [
            shape(near, 224, 128),
            shape(rest, 224, 128),
            shape(2, size_x, 32, 128),
            shape(2, 2, 256, 128),
            shape(192, 256),
            shape(192, 256),
        ],
        (features, w_fine),
        scratch=[
            pltpu.VMEM((size_x, 256, 128), BF16),
            pltpu.VMEM(features.shape, BF16),
            pltpu.VMEM((rest, 224, 128), BF16),
            pltpu.SemaphoreType.DMA((1,)),
            pltpu.SemaphoreType.DMA((2,)),
        ],
        far=(0,),
        far_out=(1,),
        flops=2 * 192 * 256 * 256 * 70,
        nbytes=4 << 20,
    )
    send_a, send_b = vmem_call(
        face_kernel,
        [shape(2, 320, 128), shape(2, 320, 128)],
        (faces, gy_a, gy_b),
        nbytes=1 << 19,
    )
    got_a = lax.ppermute(send_a, "gx", swap(nx, 0))
    got_b = lax.ppermute(send_b, "gx", swap(nx, 1))
    second, f1_ends, psum = vmem_call(
        middle_kernel,
        [shape(size_x - 4, 256, 128), shape(4, 288, 128), shape(2, 16, 128, dtype=F32)],
        (low, high, rims, gy_a, gy_b, t1, t2),
        scratch=[
            pltpu.VMEM((rest, 224, 128), BF16),
            pltpu.VMEM((size_x - 2, 64, 128), BF16),
            pltpu.VMEM((2, size_x, 32, 128), BF16),
            pltpu.SemaphoreType.DMA,
        ],
        far=(1,),
        flops=2 * 192 * 256 * 256 * 71,
        nbytes=6 << 20,
    )
    half = shape(size_x // 2, 256, 128)
    *seconds, pooled = vmem_call(
        edge_kernel,
        [half, half, shape(16, 2, 128, dtype=F32)],
        (second, f1_ends, send_a, send_b, got_a, got_b, psum, t1, t2),
        scratch=[
            pltpu.VMEM((2, 4, 320, 128), BF16),
            pltpu.VMEM((2, 2, 288, 128), BF16),
        ],
        flops=2 * 192 * 256 * 256 * 17,
        nbytes=1 << 20,
    )

    count = w_coarse.shape[0]
    w_rows = jnp.transpose(w_coarse, (1, 0, 2)).reshape(27 * count, w_coarse.shape[2])
    w_dec = lax.dynamic_slice_in_dim(w_decode, gy * count, count, axis=1)
    own = lax.all_to_all(pooled, "gy", 0, 0)
    w_rows, w_lift = vmem_call(
        load_kernel,
        [shape(*w_rows.shape), shape(w_lift.shape[0], 48)],
        (w_rows, w_lift, pooled),
        scratch=[pltpu.SemaphoreType.DMA],
        far=(0,),
        flops=1 << 28,
        nbytes=4 << 20,
    )
    gl = lax.ppermute(own[:, 1, :], "gx", ring(nx, 1))
    gr = lax.ppermute(own[:, 0, :], "gx", ring(nx, -1))
    mine = vmem_call(
        own_kernel,
        shape(2, count, 128, dtype=F32),
        (own, w_lift, w_rows),
        flops=2 * 864 * 512 * 512,
        nbytes=2 << 20,
    )
    parts = vmem_call(
        beside_kernel,
        shape(16, 2, 128, dtype=F32),
        (mine, gl, gr, w_lift, w_rows, w_dec),
        flops=2 * 864 * 512 * 256,
        nbytes=2 << 20,
    )
    parts = lax.all_to_all(parts, "gy", 0, 0)
    matrix, up, ahead = vmem_call(
        skip_kernel,
        [shape(256, 256), shape(256, 16), shape(4, 256, 128, dtype=F32)],
        (seconds[0], w_joining),
        flops=2 * 256 * 256 * 128 * 8,
        nbytes=2 << 20,
    )
    return join(*seconds, ahead, matrix, up, parts)


def solution(mesh):
    in_specs = (P(None, "gx", "gy", None), P(), P(), P(), P("gy", None, None), P(), P())
    out_specs = P(None, "gx", "gy", None)
    return jax.shard_map(local, mesh=mesh, in_specs=in_specs, out_specs=out_specs, check_vma=False)
```

```python
import jax
import jax.numpy as jnp
from jax import lax
from jax.experimental import pallas as pl
from jax.experimental.pallas import tpu as pltpu
from jax.sharding import PartitionSpec as P

POOL = 16
F32 = jnp.float32
BF16 = jnp.bfloat16
VMEM = pl.BlockSpec(memory_space=pltpu.VMEM)
LIMIT = 12 << 20


def iota(shape, dim):
    return lax.broadcasted_iota(jnp.int32, shape, dim)


def dot(a, b):
    return jnp.dot(a, b, preferred_element_type=F32)


def shape(*dims, dtype=BF16):
    return jax.ShapeDtypeStruct(dims, dtype)


def vmem_call(kernel, out_shape, args, scratch=(), flops=0, nbytes=0, far=(), far_out=()):
    args = [
        pltpu.with_memory_space_constraint(arg, pltpu.HBM) if i in far else arg
        for i, arg in enumerate(args)
    ]
    single = not isinstance(out_shape, (list, tuple))
    if far_out:
        out_shape = [
            pltpu.HBM(out.shape, out.dtype) if i in far_out else out
            for i, out in enumerate(out_shape)
        ]
    return pl.pallas_call(
        kernel,
        out_shape=out_shape,
        in_specs=[
            pl.BlockSpec(memory_space=pltpu.HBM) if i in far else VMEM for i in range(len(args))
        ],
        out_specs=(
            VMEM
            if single
            else [
                pl.BlockSpec(memory_space=pltpu.HBM) if i in far_out else VMEM
                for i in range(len(out_shape))
            ]
        ),
        scratch_shapes=list(scratch),
        compiler_params=pltpu.CompilerParams(vmem_limit_bytes=LIMIT),
        cost_estimate=pl.CostEstimate(flops=flops, bytes_accessed=nbytes, transcendentals=0),
    )(*args)


RINGS = ('gy',)


def side_flags(axis):
    at, count = lax.axis_index(axis), lax.axis_size(axis)
    even = lax.rem(at, 2) == 0

    def number(flag):
        return jnp.where(flag, 1.0, 0.0).astype(F32)

    inner_left, inner_right = at > 0, at < count - 1
    if axis in RINGS:
        return (number(inner_left), 0.0), (0.0, number(inner_right))
    left = number(jnp.logical_not(even)), number(jnp.logical_and(even, inner_left))
    right = number(even), number(jnp.logical_and(jnp.logical_not(even), inner_right))
    return left, right


def mix(a, b, flags):
    return (a.astype(F32) * flags[0] + b.astype(F32) * flags[1]).astype(BF16)


def scaled(v, m):
    return (v.astype(F32) * m).astype(BF16)


def is_even(axis):
    if axis in RINGS:
        return jnp.int32(1)
    return jnp.where(lax.rem(lax.axis_index(axis), 2) == 0, 1, 0)


def fetch_planes(far, feat, sems):
    parts = sems.shape[0]
    count = far.shape[1] // parts
    fetches = [
        pltpu.make_async_copy(
            far.at[:, i * count : (i + 1) * count],
            feat.at[:, i * count : (i + 1) * count],
            sems.at[i],
        )
        for i in range(parts)
    ]
    for fetch in fetches:
        fetch.start()
    return fetches, count


def rows_kernel(far, gy_a, gy_b, feat, sems):
    fetches, count = fetch_planes(far, feat, sems)
    size_x = feat.shape[1]
    even = is_even("gy")
    row, col = iota((64, 256), 0), iota((64, 256), 1)
    upper = jnp.where(row < 32, even, 1 - even)
    match = ((row & 15) == (col >> 4)) & ((col & 15) == ((row >> 4) & 1) + 14 * upper)
    select = jnp.where(match, 1.0, 0.0).astype(BF16)
    for x in range(0, size_x, 2):
        if x % count == 0:
            fetches[x // count].wait()
        both = jnp.concatenate(
            [feat[:, x].reshape(256, 128), feat[:, x + 1].reshape(256, 128)], axis=1
        )
        rows = dot(select, both).astype(BF16)
        for h in range(2):
            gy_a[x + h] = rows[0:32, 128 * h : 128 * h + 128]
            gy_b[x + h] = rows[32:64, 128 * h : 128 * h + 128]


def swap_rows(feat, planes):
    row, col = iota((256, 256), 0), iota((256, 256), 1)
    match = ((row >> 4) == (col & 15)) & ((row & 15) == (col >> 4))
    swap = jnp.where(match, 1.0, 0.0).astype(BF16)
    for x in range(0, feat.shape[1], 2):
        both = jnp.concatenate(
            [feat[:, x].reshape(256, 128), feat[:, x + 1].reshape(256, 128)], axis=1
        )
        moved = dot(swap, both).astype(BF16)
        planes[x] = moved[:, :128]
        planes[x + 1] = moved[:, 128:]


def band(w, t_ref):
    copies = jnp.where((iota((16, 256), 1) & 15) == iota((16, 256), 0), 1.0, 0.0).astype(BF16)
    wide = dot(w, copies)
    group = iota((16, 256), 1) >> 4
    for c in range(3):
        for x in range(2):
            for y in range(2):
                total = jnp.zeros((16, 256), F32)
                for a in range(3):
                    for b in range(3):
                        k = 9 * a + 3 * b + c
                        here = group == 4 * (x + a) + y + b
                        total = jnp.where(here, wide[16 * k : 16 * k + 16], total)
                at = 16 * (4 * c + 2 * x + y)
                t_ref[at : at + 16, :] = total.astype(BF16)


def shifted_sum(acc, rows, half):
    lanes = slice(half * 128, half * 128 + 128)
    lane = iota((rows, 128), 1)
    before = pltpu.roll(acc[0:rows, lanes], 1, 1)
    after = pltpu.roll(acc[2 * rows : 3 * rows, lanes], 127, 1)
    total = acc[rows : 2 * rows, lanes]
    total = total + jnp.where(lane > 0, before, 0.0)
    total = total + jnp.where(lane < 127, after, 0.0)
    return jnp.maximum(total, 0.0)


def window(rows_of):
    return jnp.concatenate([rows_of(x) for x in range(4)], axis=0)


def conv_pair(t, first, second):
    acc = dot(t[...], jnp.concatenate([first, second], axis=1))
    return shifted_sum(acc, 64, 0), shifted_sum(acc, 64, 1)


def plane_of(parts, x):
    count = parts[0].shape[0]
    return (parts[0], x) if x < count else (parts[1], x - count)


def interior_kernel(far, w, low, high_far, rims, faces, t1, t2, planes, feat, high, sems, puts):
    fetches, _ = fetch_planes(far, feat, sems)
    size_x = planes.shape[0]
    band(w[0:432, :], t1)
    band(w[432:864, :], t2)
    for fetch in fetches:
        fetch.wait()
    swap_rows(feat, planes)
    rims[0] = planes[:, 0:32]
    rims[1] = planes[:, 224:256]
    faces[0] = planes[0:2]
    faces[1] = planes[size_x - 2 : size_x]

    def piece(at, j):
        return window(lambda x: planes[at + x, 32 * j : 32 * j + 64])

    def store(at, j, value):
        for x in range(2):
            to, index = plane_of((low, high), at + x)
            to[index, 32 * j : 32 * j + 32] = value[32 * x : 32 * x + 32].astype(BF16)

    half = high.shape[0] // 2

    def put(i):
        span = pl.ds(i * half, half)
        return pltpu.make_async_copy(high.at[span], high_far.at[span], puts.at[i])

    at = size_x - 4
    for pair in ((0, 1), (2, 3), (4, 5), (5, 6)):
        for j, value in zip(pair, conv_pair(t1, piece(at, pair[0]), piece(at, pair[1]))):
            store(at, j, value)
    for at in range(size_x - 8, -1, -4):
        for j in range(7):
            for h, value in enumerate(conv_pair(t1, piece(at, j), piece(at + 2, j))):
                store(at + 2 * h, j, value)
        start = low.shape[0]
        for i in (1, 0):
            if at <= start + i * half < at + 4:
                put(i).start()
    for i in range(2):
        put(i).wait()


def face_kernel(faces, gy_a, gy_b, send_a, send_b):
    last = gy_a.shape[0] - 2
    left, right = side_flags("gy")
    even = is_even("gx")
    for send, side in ((send_a, even), (send_b, 1 - even)):
        for j in range(2):
            x = side * last + j
            send[j, 0:32] = mix(gy_a[x], gy_b[x], left)
            send[j, 32:288] = faces[side, j]
            send[j, 288:320] = mix(gy_a[x], gy_b[x], right)


def rim_rows_of(rims, gy_a, gy_b, t1, rim_rows, halo):
    size_x = rims.shape[1]
    left, right = side_flags("gy")
    y_left, y_right = left[0] + left[1], right[0] + right[1]
    for x in range(size_x):
        halo[0, x] = mix(gy_a[x], gy_b[x], left)
        halo[1, x] = mix(gy_a[x], gy_b[x], right)
    for at in range(0, size_x - 2, 2):
        low = window(lambda x: jnp.concatenate([halo[0, at + x], rims[0, at + x]], axis=0))
        high = window(lambda x: jnp.concatenate([rims[1, at + x], halo[1, at + x]], axis=0))
        low, high = conv_pair(t1, low, high)
        for x in range(2):
            cut = slice(32 * x, 32 * x + 16), slice(32 * x + 16, 32 * x + 32)
            rim_rows[at + x, 0:16] = (low[cut[0]] * y_left).astype(BF16)
            rim_rows[at + x, 16:32] = low[cut[1]].astype(BF16)
            rim_rows[at + x, 32:48] = high[cut[0]].astype(BF16)
            rim_rows[at + x, 48:64] = (high[cut[1]] * y_right).astype(BF16)


def fold_rows(value):
    return jnp.sum(value.astype(F32).reshape(4, 16, 128), axis=0)


def middle_kernel(
    low, high_far, rims, gy_a, gy_b, t1, t2, second, f1_ends, psum, high, rim_rows, halo, sem
):
    fetch = pltpu.make_async_copy(high_far, high, sem)
    fetch.start()
    rim_rows_of(rims, gy_a, gy_b, t1, rim_rows, halo)
    size_x = low.shape[0] + high.shape[0] + 2

    def rows(x, j):
        inner, at = plane_of((low, high), x)
        if j == 0:
            return jnp.concatenate([rim_rows[x, 0:32], inner[at, 0:32]], axis=0)
        if j == 7:
            return jnp.concatenate([inner[at, 192:224], rim_rows[x, 32:64]], axis=0)
        return inner[at, 32 * j - 32 : 32 * j + 32]

    sums = [jnp.zeros((16, 128), F32) for _ in range(2)]
    for at in range(0, size_x - 4, 2):
        if at + 2 == low.shape[0]:
            fetch.wait()

        def piece(j):
            return window(lambda x: rows(at + x, j))

        for j in range(0, 8, 2):
            for h, value in enumerate(conv_pair(t2, piece(j), piece(j + 1))):
                value = value.astype(BF16)
                row = 32 * (j + h)
                for x in range(2):
                    second[at + x, row : row + 32] = value[32 * x : 32 * x + 32]
                sums[(at + 2) // POOL] += fold_rows(value)
    psum[0], psum[1] = sums
    for i, x in enumerate((0, 1, size_x - 4, size_x - 3)):
        inner, at = plane_of((low, high), x)
        f1_ends[i, 0:32] = rim_rows[x, 0:32]
        f1_ends[i, 32:256] = inner[at]
        f1_ends[i, 256:288] = rim_rows[x, 32:64]


def edge_kernel(
    inner, f1_ends, send_a, send_b, got_a, got_b, psum_in, t1, t2, left_out, right_out,
    pooled, fe, fx,
):
    half = left_out.shape[0]
    size_x = 2 * half
    moved = iter(range(size_x - 4))

    def put(x, rows, value):
        if x < half:
            left_out[x, rows] = value
        else:
            right_out[x - half, rows] = value

    def carry_over():
        for at in (next(moved, None), next(moved, None)):
            if at is not None:
                put(at + 2, slice(0, 256), inner[at])

    x_left, x_right = side_flags("gx")
    y_left, y_right = side_flags("gy")
    y_left, y_right = y_left[0] + y_left[1], y_right[0] + y_right[1]
    even = is_even("gx").astype(F32)
    for j in range(2):
        fe[0, j] = mix(got_a[j], got_b[j], x_left)
        fe[0, 2 + j] = mix(send_a[j], send_b[j], (1.0 - even, even))
        fe[1, j] = mix(send_a[j], send_b[j], (even, 1.0 - even))
        fe[1, 2 + j] = mix(got_a[j], got_b[j], x_right)
    keeps = ((x_left[0] + x_left[1], 1.0), (1.0, x_right[0] + x_right[1]))
    for j in range(9):
        carry_over()
        pieces = [window(lambda x: fe[s, x, 32 * j : 32 * j + 64]) for s in range(2)]
        for s, value in enumerate(conv_pair(t1, *pieces)):
            for x in range(2):
                for y in range(2):
                    part = value[32 * x + 16 * y : 32 * x + 16 * y + 16] * keeps[s][x]
                    if j == 0 and y == 0:
                        part = part * y_left
                    if j == 8 and y == 1:
                        part = part * y_right
                    row = 32 * j + 16 * y
                    fx[s, x, row : row + 16] = part.astype(BF16)

    def left(j):
        cut = slice(32 * j, 32 * j + 64)
        return window(lambda x: fx[0, x, cut] if x < 2 else f1_ends[x - 2, cut])

    def right(j):
        cut = slice(32 * j, 32 * j + 64)
        return window(lambda x: f1_ends[2 + x, cut] if x < 2 else fx[1, x - 2, cut])

    sums = [psum_in[0], psum_in[1]]
    for j in range(8):
        carry_over()
        for s, value in enumerate(conv_pair(t2, left(j), right(j))):
            value = value.astype(BF16)
            for x in range(2):
                cut = slice(32 * j, 32 * j + 32)
                put(s * (size_x - 2) + x, cut, value[32 * x : 32 * x + 32])
            sums[s] = sums[s] + fold_rows(value)

    z, lane = iota((128, 128), 0), iota((128, 128), 1)
    gather = jnp.where((z >> 4) == (lane & 7), 1.0, 0.0).astype(BF16)
    keep = (iota((16, 128), 1) >> 3) == iota((16, 128), 0)
    results = []
    folded = dot(jnp.concatenate(split3(sums[0]) + split3(sums[1]), axis=0), gather)
    for s in range(2):
        first, second, third = (folded[16 * (3 * s + i) : 16 * (3 * s + i) + 16] for i in range(3))
        cells = first + second + third
        row = jnp.sum(jnp.where(keep, cells, 0.0), axis=0, keepdims=True) * (1.0 / POOL**3)
        results.append(row)
    both = jnp.concatenate(results, axis=0)
    for d in range(16):
        pooled[d] = both


def split3(v):
    a = v.astype(BF16)
    v = v - a.astype(F32)
    b = v.astype(BF16)
    c = (v - b.astype(F32)).astype(BF16)
    return [a, b, c]


def swap_groups(rows):
    lane = iota((16, 128), 1) >> 3
    total = jnp.zeros((16, 128), F32)
    rows = pltpu.roll(pltpu.roll(rows, 0, 1, stride=8, stride_axis=0), 8, 1)
    for s in range(16):
        spread = jnp.broadcast_to(rows[s : s + 1, :], (16, 128))
        moved = pltpu.roll(spread, 0, 1, stride=8, stride_axis=0)
        total = jnp.where(lane == s, moved, total)
    return total


def load_kernel(far, w_lift, after, out, lift, sem):
    fetch = pltpu.make_async_copy(far, out, sem)
    fetch.start()
    back = (iota((16, 48), 1) & 15) == 15 - iota((16, 48), 0)
    lift[...] = dot(w_lift[...], jnp.where(back, 1.0, 0.0).astype(BF16)).astype(BF16)
    fetch.wait()


def lift_slabs(slabs, w_lift):
    columns = []
    for slab in slabs:
        columns.append(jnp.concatenate(split3(swap_groups(slab)), axis=0))
    stacked = jnp.concatenate(columns, axis=1)
    return jnp.maximum(dot(w_lift, stacked), 0.0).astype(BF16)


def taps(partial, count):
    lane = iota((count, 128), 1)
    y, z = lane >> 3, lane & 7
    total = jnp.zeros((count, 128), F32)
    for k in range(9):
        b, c = k // 3 - 1, k % 3 - 1
        piece = partial[k * count : (k + 1) * count, :]
        step = 8 * b + c
        if step:
            piece = pltpu.roll(piece, (-step) % 128, 1)
        good = None
        if b:
            good = (y < 15) if b > 0 else (y > 0)
        if c:
            inside = (z < 7) if c > 0 else (z > 0)
            good = inside if good is None else good & inside
        total = total + (piece if good is None else jnp.where(good, piece, 0.0))
    return total


def own_kernel(own, w_lift, w_coarse, out):
    count = w_coarse.shape[0] // 27
    lifted = lift_slabs([own[:, 0, :], own[:, 1, :]], w_lift[...])
    partial = dot(w_coarse[...], lifted)
    for x in range(2):
        total = jnp.zeros((count, 128), F32)
        for slab in range(2):
            a = slab - x + 1
            piece = partial[9 * a * count : 9 * (a + 1) * count, slab * 128 : slab * 128 + 128]
            total = total + taps(piece, count)
        out[x] = total


def beside_kernel(mine, gl, gr, w_lift, w_coarse, w_dec, out):
    count = w_coarse.shape[0] // 27
    at, last = lax.axis_index("gx"), lax.axis_size("gx") - 1
    m_left = jnp.where(at > 0, 1.0, 0.0).astype(F32)
    m_right = jnp.where(at < last, 1.0, 0.0).astype(F32)
    lifted = lift_slabs([gl[...] * m_left, gr[...] * m_right], w_lift[...])
    sums = []
    for x in range(2):
        a = 2 * x
        rows = w_coarse[9 * a * count : 9 * (a + 1) * count, :]
        sums.append(mine[x] + taps(dot(rows, lifted[:, x * 128 : x * 128 + 128]), count))
    coarse = jnp.maximum(jnp.concatenate(sums, axis=1), 0.0).astype(BF16)
    decoded = dot(w_dec[...], coarse)
    for x in range(2):
        rows = swap_groups(decoded[:, x * 128 : x * 128 + 128])
        for y in range(16):
            out[y, x : x + 1, :] = rows[15 - y : 16 - y, :]


def skip_planes(matrix, second, at):
    both = jnp.concatenate([second[at], second[at + 1]], axis=1)
    result = dot(matrix[...], both)
    return result[:, :128], result[:, 128:]


def skip_kernel(second, w_join, matrix, up, ahead):
    r, c = iota((256, 16), 0), iota((256, 16), 1)
    rows = jnp.where((r >> 4) == c, 1.0, 0.0).astype(BF16)
    mixed = dot(rows, w_join[...]).astype(BF16)
    up[...] = mixed[:, 16:32]
    r, c = iota((16, 256), 0), iota((16, 256), 1)
    cols = jnp.where((c & 15) == r, 1.0, 0.0).astype(BF16)
    r, c = iota((256, 256), 0), iota((256, 256), 1)
    match = (r & 15) == (c >> 4)
    matrix[...] = jnp.where(match, dot(mixed[:, 0:16], cols), 0.0).astype(BF16)
    for at in range(0, ahead.shape[0], 2):
        ahead[at], ahead[at + 1] = skip_planes(matrix, second, at)


def join_kernel(left, right, ahead, matrix, up, parts, out, held, sems):
    half = left.shape[0]
    keep = (iota((16, 128), 1) >> 3) == iota((16, 128), 0)
    l0, l1 = iota((128, 128), 0), iota((128, 128), 1)
    widen = jnp.where((l0 & 7) == (l1 >> 4), 1.0, 0.0).astype(BF16)
    total = parts[0]
    for d in range(1, 16):
        total = total + parts[d]
    terms = []
    for block in range(2):
        decoded = jnp.broadcast_to(total[block : block + 1, :], (16, 128))
        decoded = jnp.where(keep, decoded, 0.0).astype(BF16)
        terms.append(dot(up[...], dot(decoded, widen).astype(BF16)))
    chunks, _, count = held.shape[:3]

    def copy(i):
        return pltpu.make_async_copy(
            held.at[i], out.at[:, i * count : (i + 1) * count], sems.at[i]
        )

    for i in range(chunks):
        for x in range(0, count, 2):
            at = i * count + x
            if at < ahead.shape[0]:
                skips = ahead[at], ahead[at + 1]
            else:
                skips = skip_planes(matrix, (left, right)[at // half], at % half)
            for h in range(2):
                value = (skips[h] + terms[at // POOL]).astype(BF16)
                held[i, :, x + h] = value.reshape(16, 16, 128)
        copy(i).start()
    for i in range(chunks):
        copy(i).wait()


def join(left, right, ahead, matrix, up, parts):
    size_x = 2 * left.shape[0]
    step = 4
    return pl.pallas_call(
        join_kernel,
        in_specs=[VMEM] * 6,
        out_specs=pl.BlockSpec(memory_space=pltpu.HBM),
        out_shape=shape(16, size_x, 16, 128),
        scratch_shapes=[
            pltpu.VMEM((size_x // step, 16, step, 16, 128), BF16),
            pltpu.SemaphoreType.DMA((size_x // step,)),
        ],
        compiler_params=pltpu.CompilerParams(vmem_limit_bytes=LIMIT),
        cost_estimate=pl.CostEstimate(
            flops=2 * 256 * 256 * 128 * size_x, bytes_accessed=4 << 20, transcendentals=0
        ),
    )(left, right, ahead, matrix, up, parts)


def local(features, w_first, w_second, w_lift, w_coarse, w_decode, w_joining):
    size_x = features.shape[1]
    nx, ny = lax.axis_size("gx"), lax.axis_size("gy")
    gy = lax.axis_index("gy")

    def ring(count, step):
        return [(i, (i + step) % count) for i in range(count)]

    def swap(count, odd):
        return [(i, (((i + odd) ^ 1) - odd) % count) for i in range(count)]

    gy_a, gy_b = vmem_call(
        rows_kernel,
        [shape(size_x, 32, 128), shape(size_x, 32, 128)],
        (features,),
        scratch=[pltpu.VMEM(features.shape, BF16), pltpu.SemaphoreType.DMA((1,))],
        far=(0,),
        flops=2 * 64 * 256 * 128 * size_x,
        nbytes=3 << 20,
    )
    gy_a = lax.ppermute(gy_a, "gy", ring(ny, 1))
    gy_b = lax.ppermute(gy_b, "gy", ring(ny, -1))

    w_fine = jnp.concatenate([w_first, w_second], axis=0).reshape(864, 16)
    near, rest = size_x // 2 - 2, size_x // 2
    low, high, rims, faces, t1, t2 = vmem_call(
        interior_kernel,
        [
            shape(near, 224, 128),
            shape(rest, 224, 128),
            shape(2, size_x, 32, 128),
            shape(2, 2, 256, 128),
            shape(192, 256),
            shape(192, 256),
        ],
        (features, w_fine),
        scratch=[
            pltpu.VMEM((size_x, 256, 128), BF16),
            pltpu.VMEM(features.shape, BF16),
            pltpu.VMEM((rest, 224, 128), BF16),
            pltpu.SemaphoreType.DMA((1,)),
            pltpu.SemaphoreType.DMA((2,)),
        ],
        far=(0,),
        far_out=(1,),
        flops=2 * 192 * 256 * 256 * 70,
        nbytes=4 << 20,
    )
    send_a, send_b = vmem_call(
        face_kernel,
        [shape(2, 320, 128), shape(2, 320, 128)],
        (faces, gy_a, gy_b),
        nbytes=1 << 19,
    )
    got_a = lax.ppermute(send_a, "gx", swap(nx, 0))
    got_b = lax.ppermute(send_b, "gx", swap(nx, 1))
    second, f1_ends, psum = vmem_call(
        middle_kernel,
        [shape(size_x - 4, 256, 128), shape(4, 288, 128), shape(2, 16, 128, dtype=F32)],
        (low, high, rims, gy_a, gy_b, t1, t2),
        scratch=[
            pltpu.VMEM((rest, 224, 128), BF16),
            pltpu.VMEM((size_x - 2, 64, 128), BF16),
            pltpu.VMEM((2, size_x, 32, 128), BF16),
            pltpu.SemaphoreType.DMA,
        ],
        far=(1,),
        flops=2 * 192 * 256 * 256 * 71,
        nbytes=6 << 20,
    )
    half = shape(size_x // 2, 256, 128)
    *seconds, pooled = vmem_call(
        edge_kernel,
        [half, half, shape(16, 2, 128, dtype=F32)],
        (second, f1_ends, send_a, send_b, got_a, got_b, psum, t1, t2),
        scratch=[
            pltpu.VMEM((2, 4, 320, 128), BF16),
            pltpu.VMEM((2, 2, 288, 128), BF16),
        ],
        flops=2 * 192 * 256 * 256 * 17,
        nbytes=1 << 20,
    )

    count = w_coarse.shape[0]
    w_rows = jnp.transpose(w_coarse, (1, 0, 2)).reshape(27 * count, w_coarse.shape[2])
    w_dec = lax.dynamic_slice_in_dim(w_decode, gy * count, count, axis=1)
    own = lax.all_to_all(pooled, "gy", 0, 0)
    w_rows, w_lift = vmem_call(
        load_kernel,
        [shape(*w_rows.shape), shape(w_lift.shape[0], 48)],
        (w_rows, w_lift, pooled),
        scratch=[pltpu.SemaphoreType.DMA],
        far=(0,),
        flops=1 << 28,
        nbytes=4 << 20,
    )
    gl = lax.ppermute(own[:, 1, :], "gx", ring(nx, 1))
    gr = lax.ppermute(own[:, 0, :], "gx", ring(nx, -1))
    mine = vmem_call(
        own_kernel,
        shape(2, count, 128, dtype=F32),
        (own, w_lift, w_rows),
        flops=2 * 864 * 512 * 512,
        nbytes=2 << 20,
    )
    parts = vmem_call(
        beside_kernel,
        shape(16, 2, 128, dtype=F32),
        (mine, gl, gr, w_lift, w_rows, w_dec),
        flops=2 * 864 * 512 * 256,
        nbytes=2 << 20,
    )
    parts = lax.all_to_all(parts, "gy", 0, 0)
    matrix, up, ahead = vmem_call(
        skip_kernel,
        [shape(256, 256), shape(256, 16), shape(4, 256, 128, dtype=F32)],
        (seconds[0], w_joining),
        flops=2 * 256 * 256 * 128 * 8,
        nbytes=2 << 20,
    )
    return join(*seconds, ahead, matrix, up, parts)


def solution(mesh):
    in_specs = (P(None, "gx", "gy", None), P(), P(), P(), P("gy", None, None), P(), P())
    out_specs = P(None, "gx", "gy", None)
    return jax.shard_map(local, mesh=mesh, in_specs=in_specs, out_specs=out_specs, check_vma=False)
```

```python
import jax
import jax.numpy as jnp
from jax import lax
from jax.experimental import pallas as pl
from jax.experimental.pallas import tpu as pltpu
from jax.sharding import PartitionSpec as P

POOL = 16
F32 = jnp.float32
BF16 = jnp.bfloat16
VMEM = pl.BlockSpec(memory_space=pltpu.VMEM)
LIMIT = 12 << 20


def iota(shape, dim):
    return lax.broadcasted_iota(jnp.int32, shape, dim)


def dot(a, b):
    return jnp.dot(a, b, preferred_element_type=F32)


def shape(*dims, dtype=BF16):
    return jax.ShapeDtypeStruct(dims, dtype)


def vmem_call(kernel, out_shape, args, scratch=(), flops=0, nbytes=0, far=(), far_out=()):
    args = [
        pltpu.with_memory_space_constraint(arg, pltpu.HBM) if i in far else arg
        for i, arg in enumerate(args)
    ]
    single = not isinstance(out_shape, (list, tuple))
    if far_out:
        out_shape = [
            pltpu.HBM(out.shape, out.dtype) if i in far_out else out
            for i, out in enumerate(out_shape)
        ]
    return pl.pallas_call(
        kernel,
        out_shape=out_shape,
        in_specs=[
            pl.BlockSpec(memory_space=pltpu.HBM) if i in far else VMEM for i in range(len(args))
        ],
        out_specs=(
            VMEM
            if single
            else [
                pl.BlockSpec(memory_space=pltpu.HBM) if i in far_out else VMEM
                for i in range(len(out_shape))
            ]
        ),
        scratch_shapes=list(scratch),
        compiler_params=pltpu.CompilerParams(vmem_limit_bytes=LIMIT),
        cost_estimate=pl.CostEstimate(flops=flops, bytes_accessed=nbytes, transcendentals=0),
    )(*args)


RINGS = ('gy',)


def side_flags(axis):
    at, count = lax.axis_index(axis), lax.axis_size(axis)
    even = lax.rem(at, 2) == 0

    def number(flag):
        return jnp.where(flag, 1.0, 0.0).astype(F32)

    inner_left, inner_right = at > 0, at < count - 1
    if axis in RINGS:
        return (number(inner_left), 0.0), (0.0, number(inner_right))
    left = number(jnp.logical_not(even)), number(jnp.logical_and(even, inner_left))
    right = number(even), number(jnp.logical_and(jnp.logical_not(even), inner_right))
    return left, right


def mix(a, b, flags):
    for value, flag, other in ((a, *flags), (b, *flags[::-1])):
        if isinstance(other, float) and other == 0.0:
            return scaled(value, flag)
    return (a.astype(F32) * flags[0] + b.astype(F32) * flags[1]).astype(BF16)


def scaled(v, m):
    return (v.astype(F32) * m).astype(BF16)


def is_even(axis):
    if axis in RINGS:
        return jnp.int32(1)
    return jnp.where(lax.rem(lax.axis_index(axis), 2) == 0, 1, 0)


def fetch_planes(far, feat, sems):
    parts = sems.shape[0]
    count = far.shape[1] // parts
    fetches = [
        pltpu.make_async_copy(
            far.at[:, i * count : (i + 1) * count],
            feat.at[:, i * count : (i + 1) * count],
            sems.at[i],
        )
        for i in range(parts)
    ]
    for fetch in fetches:
        fetch.start()
    return fetches, count


def rows_kernel(far, gy_a, gy_b, feat, sems):
    fetches, count = fetch_planes(far, feat, sems)
    size_x = feat.shape[1]
    even = is_even("gy")
    row, col = iota((64, 256), 0), iota((64, 256), 1)
    upper = jnp.where(row < 32, even, 1 - even)
    match = ((row & 15) == (col >> 4)) & ((col & 15) == ((row >> 4) & 1) + 14 * upper)
    select = jnp.where(match, 1.0, 0.0).astype(BF16)
    for x in range(0, size_x, 2):
        if x % count == 0:
            fetches[x // count].wait()
        both = jnp.concatenate(
            [feat[:, x].reshape(256, 128), feat[:, x + 1].reshape(256, 128)], axis=1
        )
        rows = dot(select, both).astype(BF16)
        for h in range(2):
            gy_a[x + h] = rows[0:32, 128 * h : 128 * h + 128]
            gy_b[x + h] = rows[32:64, 128 * h : 128 * h + 128]


def swap_rows(feat, planes):
    row, col = iota((256, 256), 0), iota((256, 256), 1)
    match = ((row >> 4) == (col & 15)) & ((row & 15) == (col >> 4))
    swap = jnp.where(match, 1.0, 0.0).astype(BF16)
    for x in range(0, feat.shape[1], 2):
        both = jnp.concatenate(
            [feat[:, x].reshape(256, 128), feat[:, x + 1].reshape(256, 128)], axis=1
        )
        moved = dot(swap, both).astype(BF16)
        planes[x] = moved[:, :128]
        planes[x + 1] = moved[:, 128:]


def band(w, t_ref):
    copies = jnp.where((iota((16, 256), 1) & 15) == iota((16, 256), 0), 1.0, 0.0).astype(BF16)
    wide = dot(w, copies)
    group = iota((16, 256), 1) >> 4
    for c in range(3):
        for x in range(2):
            for y in range(2):
                total = jnp.zeros((16, 256), F32)
                for a in range(3):
                    for b in range(3):
                        k = 9 * a + 3 * b + c
                        here = group == 4 * (x + a) + y + b
                        total = jnp.where(here, wide[16 * k : 16 * k + 16], total)
                at = 16 * (4 * c + 2 * x + y)
                t_ref[at : at + 16, :] = total.astype(BF16)


def shifted_sum(acc, rows, half):
    lanes = slice(half * 128, half * 128 + 128)
    lane = iota((rows, 128), 1)
    before = pltpu.roll(acc[0:rows, lanes], 1, 1)
    after = pltpu.roll(acc[2 * rows : 3 * rows, lanes], 127, 1)
    total = acc[rows : 2 * rows, lanes]
    total = total + jnp.where(lane > 0, before, 0.0)
    total = total + jnp.where(lane < 127, after, 0.0)
    return jnp.maximum(total, 0.0)


def window(rows_of):
    return jnp.concatenate([rows_of(x) for x in range(4)], axis=0)


def conv_pair(t, first, second):
    acc = dot(t[...], jnp.concatenate([first, second], axis=1))
    return shifted_sum(acc, 64, 0), shifted_sum(acc, 64, 1)


def plane_of(parts, x):
    count = parts[0].shape[0]
    return (parts[0], x) if x < count else (parts[1], x - count)


def interior_kernel(far, w, low, high_far, rims, faces, t1, t2, planes, feat, high, sems, puts):
    fetches, _ = fetch_planes(far, feat, sems)
    size_x = planes.shape[0]
    band(w[0:432, :], t1)
    band(w[432:864, :], t2)
    for fetch in fetches:
        fetch.wait()
    swap_rows(feat, planes)
    rims[0] = planes[:, 0:32]
    rims[1] = planes[:, 224:256]
    faces[0] = planes[0:2]
    faces[1] = planes[size_x - 2 : size_x]

    def piece(at, j):
        return window(lambda x: planes[at + x, 32 * j : 32 * j + 64])

    def store(at, j, value):
        for x in range(2):
            to, index = plane_of((low, high), at + x)
            to[index, 32 * j : 32 * j + 32] = value[32 * x : 32 * x + 32].astype(BF16)

    half = high.shape[0] // 2

    def put(i):
        span = pl.ds(i * half, half)
        return pltpu.make_async_copy(high.at[span], high_far.at[span], puts.at[i])

    at = size_x - 4
    for pair in ((0, 1), (2, 3), (4, 5), (5, 6)):
        for j, value in zip(pair, conv_pair(t1, piece(at, pair[0]), piece(at, pair[1]))):
            store(at, j, value)
    for at in range(size_x - 8, -1, -4):
        for j in range(7):
            for h, value in enumerate(conv_pair(t1, piece(at, j), piece(at + 2, j))):
                store(at + 2 * h, j, value)
        start = low.shape[0]
        for i in (1, 0):
            if at <= start + i * half < at + 4:
                put(i).start()
    for i in range(2):
        put(i).wait()


def face_kernel(faces, gy_a, gy_b, send_a, send_b):
    last = gy_a.shape[0] - 2
    left, right = side_flags("gy")
    even = is_even("gx")
    for send, side in ((send_a, even), (send_b, 1 - even)):
        for j in range(2):
            x = side * last + j
            send[j, 0:32] = mix(gy_a[x], gy_b[x], left)
            send[j, 32:288] = faces[side, j]
            send[j, 288:320] = mix(gy_a[x], gy_b[x], right)


def rim_rows_of(rims, gy_a, gy_b, t1, rim_rows, halo):
    size_x = rims.shape[1]
    left, right = side_flags("gy")
    y_left, y_right = left[0] + left[1], right[0] + right[1]
    for x in range(size_x):
        halo[0, x] = mix(gy_a[x], gy_b[x], left)
        halo[1, x] = mix(gy_a[x], gy_b[x], right)
    for at in range(0, size_x - 2, 2):
        low = window(lambda x: jnp.concatenate([halo[0, at + x], rims[0, at + x]], axis=0))
        high = window(lambda x: jnp.concatenate([rims[1, at + x], halo[1, at + x]], axis=0))
        low, high = conv_pair(t1, low, high)
        for x in range(2):
            cut = slice(32 * x, 32 * x + 16), slice(32 * x + 16, 32 * x + 32)
            rim_rows[at + x, 0:16] = (low[cut[0]] * y_left).astype(BF16)
            rim_rows[at + x, 16:32] = low[cut[1]].astype(BF16)
            rim_rows[at + x, 32:48] = high[cut[0]].astype(BF16)
            rim_rows[at + x, 48:64] = (high[cut[1]] * y_right).astype(BF16)


def fold_rows(value):
    return jnp.sum(value.astype(F32).reshape(4, 16, 128), axis=0)


def middle_kernel(
    low, high_far, rims, gy_a, gy_b, t1, t2, second, f1_ends, psum, high, rim_rows, halo, sem
):
    fetch = pltpu.make_async_copy(high_far, high, sem)
    fetch.start()
    rim_rows_of(rims, gy_a, gy_b, t1, rim_rows, halo)
    size_x = low.shape[0] + high.shape[0] + 2

    def rows(x, j):
        inner, at = plane_of((low, high), x)
        if j == 0:
            return jnp.concatenate([rim_rows[x, 0:32], inner[at, 0:32]], axis=0)
        if j == 7:
            return jnp.concatenate([inner[at, 192:224], rim_rows[x, 32:64]], axis=0)
        return inner[at, 32 * j - 32 : 32 * j + 32]

    sums = [jnp.zeros((16, 128), F32) for _ in range(2)]
    for at in range(0, size_x - 4, 2):
        if at + 2 == low.shape[0]:
            fetch.wait()

        def piece(j):
            return window(lambda x: rows(at + x, j))

        for j in range(0, 8, 2):
            for h, value in enumerate(conv_pair(t2, piece(j), piece(j + 1))):
                value = value.astype(BF16)
                row = 32 * (j + h)
                for x in range(2):
                    second[at + x, row : row + 32] = value[32 * x : 32 * x + 32]
                sums[(at + 2) // POOL] += fold_rows(value)
    psum[0], psum[1] = sums
    for i, x in enumerate((0, 1, size_x - 4, size_x - 3)):
        inner, at = plane_of((low, high), x)
        f1_ends[i, 0:32] = rim_rows[x, 0:32]
        f1_ends[i, 32:256] = inner[at]
        f1_ends[i, 256:288] = rim_rows[x, 32:64]


def edge_kernel(
    inner, f1_ends, send_a, send_b, got_a, got_b, psum_in, t1, t2, left_out, right_out,
    pooled, fe, fx,
):
    half = left_out.shape[0]
    size_x = 2 * half
    moved = iter(range(size_x - 4))

    def put(x, rows, value):
        if x < half:
            left_out[x, rows] = value
        else:
            right_out[x - half, rows] = value

    def carry_over():
        for at in (next(moved, None), next(moved, None)):
            if at is not None:
                put(at + 2, slice(0, 256), inner[at])

    x_left, x_right = side_flags("gx")
    y_left, y_right = side_flags("gy")
    y_left, y_right = y_left[0] + y_left[1], y_right[0] + y_right[1]
    even = is_even("gx").astype(F32)
    for j in range(2):
        fe[0, j] = mix(got_a[j], got_b[j], x_left)
        fe[0, 2 + j] = mix(send_a[j], send_b[j], (1.0 - even, even))
        fe[1, j] = mix(send_a[j], send_b[j], (even, 1.0 - even))
        fe[1, 2 + j] = mix(got_a[j], got_b[j], x_right)
    keeps = ((x_left[0] + x_left[1], 1.0), (1.0, x_right[0] + x_right[1]))
    for j in range(9):
        carry_over()
        pieces = [window(lambda x: fe[s, x, 32 * j : 32 * j + 64]) for s in range(2)]
        for s, value in enumerate(conv_pair(t1, *pieces)):
            for x in range(2):
                for y in range(2):
                    part = value[32 * x + 16 * y : 32 * x + 16 * y + 16] * keeps[s][x]
                    if j == 0 and y == 0:
                        part = part * y_left
                    if j == 8 and y == 1:
                        part = part * y_right
                    row = 32 * j + 16 * y
                    fx[s, x, row : row + 16] = part.astype(BF16)

    def left(j):
        cut = slice(32 * j, 32 * j + 64)
        return window(lambda x: fx[0, x, cut] if x < 2 else f1_ends[x - 2, cut])

    def right(j):
        cut = slice(32 * j, 32 * j + 64)
        return window(lambda x: f1_ends[2 + x, cut] if x < 2 else fx[1, x - 2, cut])

    sums = [psum_in[0], psum_in[1]]
    for j in range(8):
        carry_over()
        for s, value in enumerate(conv_pair(t2, left(j), right(j))):
            value = value.astype(BF16)
            for x in range(2):
                cut = slice(32 * j, 32 * j + 32)
                put(s * (size_x - 2) + x, cut, value[32 * x : 32 * x + 32])
            sums[s] = sums[s] + fold_rows(value)

    z, lane = iota((128, 128), 0), iota((128, 128), 1)
    gather = jnp.where((z >> 4) == (lane & 7), 1.0, 0.0).astype(BF16)
    keep = (iota((16, 128), 1) >> 3) == iota((16, 128), 0)
    results = []
    folded = dot(jnp.concatenate(split3(sums[0]) + split3(sums[1]), axis=0), gather)
    for s in range(2):
        first, second, third = (folded[16 * (3 * s + i) : 16 * (3 * s + i) + 16] for i in range(3))
        cells = first + second + third
        row = jnp.sum(jnp.where(keep, cells, 0.0), axis=0, keepdims=True) * (1.0 / POOL**3)
        results.append(row)
    both = jnp.concatenate(results, axis=0)
    for d in range(16):
        pooled[d] = both


def split3(v):
    a = v.astype(BF16)
    v = v - a.astype(F32)
    b = v.astype(BF16)
    c = (v - b.astype(F32)).astype(BF16)
    return [a, b, c]


def swap_groups(rows):
    lane = iota((16, 128), 1) >> 3
    total = jnp.zeros((16, 128), F32)
    rows = pltpu.roll(pltpu.roll(rows, 0, 1, stride=8, stride_axis=0), 8, 1)
    for s in range(16):
        spread = jnp.broadcast_to(rows[s : s + 1, :], (16, 128))
        moved = pltpu.roll(spread, 0, 1, stride=8, stride_axis=0)
        total = jnp.where(lane == s, moved, total)
    return total


def load_kernel(far, w_lift, after, out, lift, sem):
    fetch = pltpu.make_async_copy(far, out, sem)
    fetch.start()
    back = (iota((16, 48), 1) & 15) == 15 - iota((16, 48), 0)
    lift[...] = dot(w_lift[...], jnp.where(back, 1.0, 0.0).astype(BF16)).astype(BF16)
    fetch.wait()


def lift_slabs(slabs, w_lift):
    columns = []
    for slab in slabs:
        columns.append(jnp.concatenate(split3(swap_groups(slab)), axis=0))
    stacked = jnp.concatenate(columns, axis=1)
    return jnp.maximum(dot(w_lift, stacked), 0.0).astype(BF16)


def taps(partial, count):
    lane = iota((count, 128), 1)
    y, z = lane >> 3, lane & 7
    total = jnp.zeros((count, 128), F32)
    for k in range(9):
        b, c = k // 3 - 1, k % 3 - 1
        piece = partial[k * count : (k + 1) * count, :]
        step = 8 * b + c
        if step:
            piece = pltpu.roll(piece, (-step) % 128, 1)
        good = None
        if b:
            good = (y < 15) if b > 0 else (y > 0)
        if c:
            inside = (z < 7) if c > 0 else (z > 0)
            good = inside if good is None else good & inside
        total = total + (piece if good is None else jnp.where(good, piece, 0.0))
    return total


def own_kernel(own, w_lift, w_coarse, out):
    count = w_coarse.shape[0] // 27
    lifted = lift_slabs([own[:, 0, :], own[:, 1, :]], w_lift[...])
    partial = dot(w_coarse[...], lifted)
    for x in range(2):
        total = jnp.zeros((count, 128), F32)
        for slab in range(2):
            a = slab - x + 1
            piece = partial[9 * a * count : 9 * (a + 1) * count, slab * 128 : slab * 128 + 128]
            total = total + taps(piece, count)
        out[x] = total


def beside_kernel(mine, gl, gr, w_lift, w_coarse, w_dec, out):
    count = w_coarse.shape[0] // 27
    at, last = lax.axis_index("gx"), lax.axis_size("gx") - 1
    m_left = jnp.where(at > 0, 1.0, 0.0).astype(F32)
    m_right = jnp.where(at < last, 1.0, 0.0).astype(F32)
    lifted = lift_slabs([gl[...] * m_left, gr[...] * m_right], w_lift[...])
    sums = []
    for x in range(2):
        a = 2 * x
        rows = w_coarse[9 * a * count : 9 * (a + 1) * count, :]
        sums.append(mine[x] + taps(dot(rows, lifted[:, x * 128 : x * 128 + 128]), count))
    coarse = jnp.maximum(jnp.concatenate(sums, axis=1), 0.0).astype(BF16)
    decoded = dot(w_dec[...], coarse)
    for x in range(2):
        rows = swap_groups(decoded[:, x * 128 : x * 128 + 128])
        for y in range(16):
            out[y, x : x + 1, :] = rows[15 - y : 16 - y, :]


def skip_planes(matrix, second, at):
    both = jnp.concatenate([second[at], second[at + 1]], axis=1)
    result = dot(matrix[...], both)
    return result[:, :128], result[:, 128:]


def skip_kernel(second, w_join, matrix, up, ahead):
    r, c = iota((256, 16), 0), iota((256, 16), 1)
    rows = jnp.where((r >> 4) == c, 1.0, 0.0).astype(BF16)
    mixed = dot(rows, w_join[...]).astype(BF16)
    up[...] = mixed[:, 16:32]
    r, c = iota((16, 256), 0), iota((16, 256), 1)
    cols = jnp.where((c & 15) == r, 1.0, 0.0).astype(BF16)
    r, c = iota((256, 256), 0), iota((256, 256), 1)
    match = (r & 15) == (c >> 4)
    matrix[...] = jnp.where(match, dot(mixed[:, 0:16], cols), 0.0).astype(BF16)
    for at in range(0, ahead.shape[0], 2):
        ahead[at], ahead[at + 1] = skip_planes(matrix, second, at)


def join_kernel(left, right, ahead, matrix, up, parts, out, held, sems):
    half = left.shape[0]
    keep = (iota((16, 128), 1) >> 3) == iota((16, 128), 0)
    l0, l1 = iota((128, 128), 0), iota((128, 128), 1)
    widen = jnp.where((l0 & 7) == (l1 >> 4), 1.0, 0.0).astype(BF16)
    total = parts[0]
    for d in range(1, 16):
        total = total + parts[d]
    terms = []
    for block in range(2):
        decoded = jnp.broadcast_to(total[block : block + 1, :], (16, 128))
        decoded = jnp.where(keep, decoded, 0.0).astype(BF16)
        terms.append(dot(up[...], dot(decoded, widen).astype(BF16)))
    chunks, _, count = held.shape[:3]

    def copy(i):
        return pltpu.make_async_copy(
            held.at[i], out.at[:, i * count : (i + 1) * count], sems.at[i]
        )

    for i in range(chunks):
        for x in range(0, count, 2):
            at = i * count + x
            if at < ahead.shape[0]:
                skips = ahead[at], ahead[at + 1]
            else:
                skips = skip_planes(matrix, (left, right)[at // half], at % half)
            for h in range(2):
                value = (skips[h] + terms[at // POOL]).astype(BF16)
                held[i, :, x + h] = value.reshape(16, 16, 128)
        copy(i).start()
    for i in range(chunks):
        copy(i).wait()


def join(left, right, ahead, matrix, up, parts):
    size_x = 2 * left.shape[0]
    step = 4
    return pl.pallas_call(
        join_kernel,
        in_specs=[VMEM] * 6,
        out_specs=pl.BlockSpec(memory_space=pltpu.HBM),
        out_shape=shape(16, size_x, 16, 128),
        scratch_shapes=[
            pltpu.VMEM((size_x // step, 16, step, 16, 128), BF16),
            pltpu.SemaphoreType.DMA((size_x // step,)),
        ],
        compiler_params=pltpu.CompilerParams(vmem_limit_bytes=LIMIT),
        cost_estimate=pl.CostEstimate(
            flops=2 * 256 * 256 * 128 * size_x, bytes_accessed=4 << 20, transcendentals=0
        ),
    )(left, right, ahead, matrix, up, parts)


def local(features, w_first, w_second, w_lift, w_coarse, w_decode, w_joining):
    size_x = features.shape[1]
    nx, ny = lax.axis_size("gx"), lax.axis_size("gy")
    gy = lax.axis_index("gy")

    def ring(count, step):
        return [(i, (i + step) % count) for i in range(count)]

    def swap(count, odd):
        return [(i, (((i + odd) ^ 1) - odd) % count) for i in range(count)]

    gy_a, gy_b = vmem_call(
        rows_kernel,
        [shape(size_x, 32, 128), shape(size_x, 32, 128)],
        (features,),
        scratch=[pltpu.VMEM(features.shape, BF16), pltpu.SemaphoreType.DMA((1,))],
        far=(0,),
        flops=2 * 64 * 256 * 128 * size_x,
        nbytes=3 << 20,
    )
    gy_a = lax.ppermute(gy_a, "gy", ring(ny, 1))
    gy_b = lax.ppermute(gy_b, "gy", ring(ny, -1))

    w_fine = jnp.concatenate([w_first, w_second], axis=0).reshape(864, 16)
    near, rest = size_x // 2 - 2, size_x // 2
    low, high, rims, faces, t1, t2 = vmem_call(
        interior_kernel,
        [
            shape(near, 224, 128),
            shape(rest, 224, 128),
            shape(2, size_x, 32, 128),
            shape(2, 2, 256, 128),
            shape(192, 256),
            shape(192, 256),
        ],
        (features, w_fine),
        scratch=[
            pltpu.VMEM((size_x, 256, 128), BF16),
            pltpu.VMEM(features.shape, BF16),
            pltpu.VMEM((rest, 224, 128), BF16),
            pltpu.SemaphoreType.DMA((1,)),
            pltpu.SemaphoreType.DMA((2,)),
        ],
        far=(0,),
        far_out=(1,),
        flops=2 * 192 * 256 * 256 * 70,
        nbytes=4 << 20,
    )
    send_a, send_b = vmem_call(
        face_kernel,
        [shape(2, 320, 128), shape(2, 320, 128)],
        (faces, gy_a, gy_b),
        nbytes=1 << 19,
    )
    got_a = lax.ppermute(send_a, "gx", swap(nx, 0))
    got_b = lax.ppermute(send_b, "gx", swap(nx, 1))
    second, f1_ends, psum = vmem_call(
        middle_kernel,
        [shape(size_x - 4, 256, 128), shape(4, 288, 128), shape(2, 16, 128, dtype=F32)],
        (low, high, rims, gy_a, gy_b, t1, t2),
        scratch=[
            pltpu.VMEM((rest, 224, 128), BF16),
            pltpu.VMEM((size_x - 2, 64, 128), BF16),
            pltpu.VMEM((2, size_x, 32, 128), BF16),
            pltpu.SemaphoreType.DMA,
        ],
        far=(1,),
        flops=2 * 192 * 256 * 256 * 71,
        nbytes=6 << 20,
    )
    half = shape(size_x // 2, 256, 128)
    *seconds, pooled = vmem_call(
        edge_kernel,
        [half, half, shape(16, 2, 128, dtype=F32)],
        (second, f1_ends, send_a, send_b, got_a, got_b, psum, t1, t2),
        scratch=[
            pltpu.VMEM((2, 4, 320, 128), BF16),
            pltpu.VMEM((2, 2, 288, 128), BF16),
        ],
        flops=2 * 192 * 256 * 256 * 17,
        nbytes=1 << 20,
    )

    count = w_coarse.shape[0]
    w_rows = jnp.transpose(w_coarse, (1, 0, 2)).reshape(27 * count, w_coarse.shape[2])
    w_dec = lax.dynamic_slice_in_dim(w_decode, gy * count, count, axis=1)
    own = lax.all_to_all(pooled, "gy", 0, 0)
    w_rows, w_lift = vmem_call(
        load_kernel,
        [shape(*w_rows.shape), shape(w_lift.shape[0], 48)],
        (w_rows, w_lift, pooled),
        scratch=[pltpu.SemaphoreType.DMA],
        far=(0,),
        flops=1 << 28,
        nbytes=4 << 20,
    )
    gl = lax.ppermute(own[:, 1, :], "gx", ring(nx, 1))
    gr = lax.ppermute(own[:, 0, :], "gx", ring(nx, -1))
    mine = vmem_call(
        own_kernel,
        shape(2, count, 128, dtype=F32),
        (own, w_lift, w_rows),
        flops=2 * 864 * 512 * 512,
        nbytes=2 << 20,
    )
    parts = vmem_call(
        beside_kernel,
        shape(16, 2, 128, dtype=F32),
        (mine, gl, gr, w_lift, w_rows, w_dec),
        flops=2 * 864 * 512 * 256,
        nbytes=2 << 20,
    )
    parts = lax.all_to_all(parts, "gy", 0, 0)
    matrix, up, ahead = vmem_call(
        skip_kernel,
        [shape(256, 256), shape(256, 16), shape(4, 256, 128, dtype=F32)],
        (seconds[0], w_joining),
        flops=2 * 256 * 256 * 128 * 8,
        nbytes=2 << 20,
    )
    return join(*seconds, ahead, matrix, up, parts)


def solution(mesh):
    in_specs = (P(None, "gx", "gy", None), P(), P(), P(), P("gy", None, None), P(), P())
    out_specs = P(None, "gx", "gy", None)
    return jax.shard_map(local, mesh=mesh, in_specs=in_specs, out_specs=out_specs, check_vma=False)
```
